32 devices in a mesh: leaf: 4 (over y, x), row: 8 (over z, core).
Axes of the slice: x: 2, y: 2, z: 4, core: 2. Of those that a mesh axis runs over, the one named last changes fastest.
Arguments:
- rhs_sub: float32 [4, 2, 1024, 512], P('leaf', None, 'row'), may hold values from -6 to 6
- rhs_anc: float32 [16384, 512], P('row'), may hold values from -6 to 6
- inv_sub: float32 [4, 2, 1024, 1024], P('leaf', None, 'row'), may hold values from -3 to 3, as said below
- panel_mid: float32 [4, 1024, 1024], P('leaf', 'row'), may hold values from -0.1875 to 0.1875
- panel_anc: float32 [4, 2, 16384, 1024], P('leaf', None, 'row'), may hold values from -0.125 to 0.125
- block_mask: int32 [4, 2, 128], P('leaf', None, 'row'), may hold values 0 or 1
- inv_anc: float32 [16384, 1024], P('row'), may hold values from -3 to 3, as said below
Outputs:
- x_sub: float32 [4, 2, 1024, 512], P('leaf', None, 'row')
- x_anc: float32 [16384, 512], P('row')
The draws below stay inside these ranges and needn't reach their ends.
Inputs may be any that keep to these rules, and one draw needn't show every extreme that they name: `inv_sub`: each [1024, 1024] block is lower triangular with its diagonal between 0.3 and 3. `inv_anc`: each block of 1024 rows has its diagonal between 0.3 and 3.
All inputs are finite; a program needn't handle non-finite values. No bound on the sum of `block_mask` on one device may be relied on, other than what follows from the above.
Results may differ from the reference program's by a relative error of at most 0.00012.
Values sent between devices are 32-bit elements; how exact they have to be, the bound alone decides.
No kernel may reach another device: no remote copies, remote signals or barrier semaphores. Data moves between devices by JAX's collectives and lax.ppermute only.
A program may use at most 128 MiB of HBM per device.

```python
import jax
import jax.numpy as jnp
from jax import lax

W = 1024
ANC = 16384
BR = 128
R = 512
GRIDS = 4


def lower_noise(key, shape):
    return jax.random.normal(key, shape, jnp.float32) * (0.5 / jnp.sqrt(W * 1.0))


def diagonal_draw(key, shape):
    return jnp.exp(jax.random.uniform(key, shape, jnp.float32, jnp.log(0.5), jnp.log(2.0)))


def draw_inv_sub(key, part):
    key_noise, key_diag = jax.random.split(jax.random.fold_in(key, 11))
    noise = jnp.tril(lower_noise(key_noise, (GRIDS, 2, W, W)), -1)
    diagonal = diagonal_draw(key_diag, (GRIDS, 2, W))
    return noise + diagonal[..., None] * jnp.eye(W, dtype=jnp.float32)


def draw_inv_anc(key, part):
    key_noise, key_diag = jax.random.split(jax.random.fold_in(key, 23))
    noise = lower_noise(key_noise, (ANC, W))
    diagonal = diagonal_draw(key_diag, (ANC, 1))
    local_row = (jnp.arange(ANC) % W)[:, None]
    column = jnp.arange(W)[None, :]
    return jnp.where(column != local_row, noise, 0.0) + jnp.where(column == local_row, diagonal, 0.0)


def touch_ends(result, rng, smallest, top_value):
    place = [jax.random.randint(jax.random.fold_in(rng, axis), (), 0, length) for axis, length in enumerate(result.shape)]
    longest = result.shape.index(max(result.shape))
    neighbour = place[:longest] + [(place[longest] + 1) % result.shape[longest]] + place[longest + 1:]
    return result.at[tuple(place)].set(smallest).at[tuple(neighbour)].set(top_value)


def levels(key, extent, shards, least, top_value):
    def one(position, parts):
        steps = jax.random.uniform(jax.random.fold_in(jax.random.fold_in(key, 6), position), (parts,), jnp.float32, least / len(shards), top_value / len(shards))
        return jnp.repeat(jnp.exp(steps), extent[position] // parts).reshape((-1,) + (1,) * (len(extent) - position - 1))

    factor_of = one(*shards[0])
    for cut in shards[1:]:
        factor_of = factor_of * one(*cut)
    return factor_of


def scatter_about(key, shape, scale, reach, cuts=(), held_as=jnp.bfloat16):
    level = levels(key, shape, cuts, -0.22, 0.18) if cuts else 1.0
    entries = jax.random.normal(key, shape, jnp.float32) * scale * level
    return jnp.minimum(jnp.maximum(entries, -reach), reach).astype(held_as)


def setup_inputs(seed: int = 0) -> dict:
    keys = jax.random.split(jax.random.key(seed), 8)
    rhs_sub = scatter_about(keys[0], (GRIDS, 2, W, R), 1.0, 6.0, ((0, 4), (2, 8)), jnp.float32)
    rhs_anc = scatter_about(keys[1], (ANC, R), 1.0, 6.0, ((0, 8),), jnp.float32)
    inv_sub = draw_inv_sub(jax.random.fold_in(keys[7], 71), 0)
    panel_mid = scatter_about(keys[3], (GRIDS, W, W), W ** -0.5, 0.1875, ((0, 4), (1, 8)), jnp.float32)
    panel_anc = scatter_about(keys[4], (GRIDS, 2, ANC, W), (2 * W) ** -0.5, 0.125, ((0, 4), (2, 8)), jnp.float32)
    block_mask = touch_ends((jax.random.randint(keys[5], (GRIDS, 2, ANC // BR), 0, 4) < 3).astype(jnp.int32), jax.random.fold_in(keys[5], 1), 0, 1)
    inv_anc = draw_inv_anc(jax.random.fold_in(keys[7], 71), 0)
    return {"rhs_sub": rhs_sub, "rhs_anc": rhs_anc, "inv_sub": inv_sub, "panel_mid": panel_mid, "panel_anc": panel_anc, "block_mask": block_mask, "inv_anc": inv_anc}


def product(left, right):
    return jnp.dot(left, right, precision=lax.Precision.HIGHEST, preferred_element_type=jnp.float32)


def reference(rhs_sub, rhs_anc, inv_sub, panel_mid, panel_anc, block_mask, inv_anc):
    mask_rows = jnp.repeat(block_mask, BR, axis=2).astype(jnp.float32)
    panels = panel_anc * mask_rows[..., None]
    update = jnp.zeros((ANC, R), jnp.float32)
    solved = []
    for grid in range(GRIDS):
        first = product(inv_sub[grid, 0], rhs_sub[grid, 0])
        second = product(inv_sub[grid, 1], rhs_sub[grid, 1] - product(panel_mid[grid], first))
        update = update + product(panels[grid, 0], first) + product(panels[grid, 1], second)
        solved.append((first, second))
    blocks = inv_anc.reshape(ANC // W, W, W)
    values = (rhs_anc - update).reshape(ANC // W, W, R)
    forward = jnp.einsum("kij,kjr->kir", blocks, values, precision=lax.Precision.HIGHEST)
    x_anc = jnp.einsum("kji,kjr->kir", blocks, forward, precision=lax.Precision.HIGHEST).reshape(ANC, R)
    outputs = []
    for grid in range(GRIDS):
        first, second = solved[grid]
        x_second = product(inv_sub[grid, 1].T, second - product(panels[grid, 1].T, x_anc))
        x_first = product(inv_sub[grid, 0].T, first - product(panel_mid[grid].T, x_second) - product(panels[grid, 0].T, x_anc))
        outputs.append(jnp.stack([x_first, x_second]))
    return jnp.stack(outputs), x_anc
```

```python
import jax
import jax.numpy as jnp
from jax import lax
from jax.sharding import PartitionSpec as P

CHUNKS = 2
PRECISION = lax.Precision.HIGH


def product(left, right):
    return jnp.dot(left, right, precision=PRECISION, preferred_element_type=jnp.float32)


def transposed(left, right):
    return lax.dot_general(
        left,
        right,
        (((0,), (0,)), ((), ())),
        precision=PRECISION,
        preferred_element_type=jnp.float32,
    )


def core_swap(value):
    count = lax.axis_size("row")
    return lax.ppermute(value, "row", [(r, r ^ 1) for r in range(count)])


def leaf_swap(value, mask):
    count = lax.axis_size("leaf")
    return lax.ppermute(value, "leaf", [(g, g ^ mask) for g in range(count)])


def chip_digits(chips):
    digits, stride = [], 1
    while chips > 1:
        size = 4 if chips % 4 == 0 else 2
        digits.append((size, stride))
        stride *= size
        chips //= size
    return digits


def digit_permute(value, size, stride, moves):
    target = dict(moves)
    pairs = []
    for r in range(lax.axis_size("row")):
        digit = (r // 2) // stride % size
        if digit in target:
            pairs.append((r, r + 2 * stride * (target[digit] - digit)))
    return lax.ppermute(value, "row", pairs)


def digit_index(size, stride):
    return lax.axis_index("row") // 2 // stride % size


def gather_digit(value, size, stride, lower):
    def moves(pairs):
        return [(a, b) for a, b in pairs if a < b] if lower else pairs

    me = digit_index(size, stride)
    near = digit_permute(value, size, stride, moves([(0, 1), (1, 0), (2, 3), (3, 2)][: 2 if size == 2 else 4]))
    if size == 2:
        first = jnp.where(me == 0, value, near)
        last = jnp.where(me == 0, near, value)
        return jnp.concatenate([first, last], 0)
    inner = digit_permute(value, size, stride, moves([(1, 2), (2, 1)]))
    relay = digit_permute(near, size, stride, moves([(1, 2), (2, 1)]))
    far = digit_permute(near, size, stride, moves([(1, 3), (2, 0)]))
    outer = digit_permute(inner, size, stride, moves([(1, 0), (2, 3)]))
    middle = (me == 1) | (me == 2)
    third = jnp.where(middle, inner, outer)
    fourth = jnp.where(middle, relay, far)
    odd = me % 2 == 1
    even_one = jnp.where(odd, near, value)
    odd_one = jnp.where(odd, value, near)
    high = me >= 2
    return jnp.concatenate(
        [
            jnp.where(high, fourth, even_one),
            jnp.where(high, third, odd_one),
            jnp.where(high, even_one, third),
            jnp.where(high, odd_one, fourth),
        ],
        0,
    )


def reduce_digit(value, size, stride, lower):
    def moves(pairs):
        return [(a, b) for a, b in pairs if a > b] if lower else pairs

    me = digit_index(size, stride)
    rows = value.shape[0] // size
    blocks = value.reshape(size, rows, value.shape[1])

    def block(*table):
        index = jnp.take(jnp.array(table, jnp.int32), me)
        return lax.dynamic_index_in_dim(blocks, index, 0, keepdims=False)

    if size == 2:
        other = digit_permute(block(1, 0), size, stride, moves([(0, 1), (1, 0)]))
        return block(0, 1) + other
    far = digit_permute(block(3, 0, 3, 0), size, stride, moves([(3, 1), (0, 2)]))
    relay = digit_permute(block(0, 3, 0, 3), size, stride, moves([(2, 1), (1, 2)]))
    outer = digit_permute(block(2, 2, 1, 1), size, stride, moves([(0, 1), (3, 2)]))
    inner = digit_permute(block(2, 2, 1, 1) + outer, size, stride, moves([(1, 2), (2, 1)]))
    near = digit_permute(block(1, 0, 3, 2) + (far + relay), size, stride, moves([(0, 1), (1, 0), (2, 3), (3, 2)]))
    return block(0, 1, 2, 3) + near + inner


def gather_rows(value, lower=False):
    digits = chip_digits(lax.axis_size("row") // 2)
    for place, (size, stride) in enumerate(digits):
        value = gather_digit(value, size, stride, lower and place == len(digits) - 1)
    return value


def reduce_rows(value, lower=False):
    digits = chip_digits(lax.axis_size("row") // 2)
    for place, (size, stride) in reversed(list(enumerate(digits))):
        value = reduce_digit(value, size, stride, lower and place == len(digits) - 1)
    return value


def by_core(core, mine, other, axis):
    return jnp.concatenate(
        [jnp.where(core == 0, mine, other), jnp.where(core == 0, other, mine)], axis
    )


def leaf_reduce(update, x_bit, y_bit):
    rows, columns = update.shape
    parts = update.reshape(2, 2, rows // 4, columns)
    half = columns // 2

    def pick_columns(value, bit):
        return lax.dynamic_slice_in_dim(value, bit * half, half, value.ndim - 1)

    def pick_block(value, bit):
        return lax.dynamic_index_in_dim(value, bit, 0, keepdims=False)

    first, second = parts[:, 0], parts[:, 1]
    from_x = leaf_swap(pick_columns(first, 1 - x_bit), 1)
    from_y = leaf_swap(pick_block(second, 1 - y_bit), 2)
    first = pick_columns(first, x_bit) + from_x
    second = pick_block(second, y_bit) + from_y
    from_y = leaf_swap(pick_block(first, 1 - y_bit), 2)
    from_x = leaf_swap(pick_columns(second, 1 - x_bit), 1)
    return jnp.concatenate(
        [pick_block(first, y_bit) + from_y, pick_columns(second, x_bit) + from_x], 0
    )


def leaf_gather(piece, x_bit, y_bit):
    rows, half = piece.shape
    first, second = piece[: rows // 2], piece[rows // 2 :]
    from_y = leaf_swap(first, 2)
    from_x = leaf_swap(second, 1)
    first = jnp.stack([jnp.where(y_bit == 0, first, from_y), jnp.where(y_bit == 0, from_y, first)])
    second = jnp.concatenate(
        [jnp.where(x_bit == 0, second, from_x), jnp.where(x_bit == 0, from_x, second)], 1
    )
    from_x = leaf_swap(first, 1)
    from_y = leaf_swap(second, 2)
    first = jnp.concatenate(
        [jnp.where(x_bit == 0, first, from_x), jnp.where(x_bit == 0, from_x, first)], 2
    )
    second = jnp.stack(
        [jnp.where(y_bit == 0, second, from_y), jnp.where(y_bit == 0, from_y, second)]
    )
    return jnp.stack([first, second], 1).reshape(2 * rows, 2 * half)


def from_partner(value, axis, bit):
    mask = 2**bit
    pairs = [(source, source ^ mask) for source in range(lax.axis_size(axis))]
    return lax.ppermute(value, axis, pairs)


def ancestor_solve(inverse_rows, values):
    rows_local, width = inverse_rows.shape
    if rows_local >= width:
        blocks = inverse_rows.reshape(rows_local // width, width, width)
        grouped = values.reshape(rows_local // width, width, values.shape[1])
        forward = jnp.einsum("kij,kjr->kir", blocks, grouped, precision=PRECISION)
        result = jnp.einsum("kji,kjr->kir", blocks, forward, precision=PRECISION)
        return result.reshape(rows_local, values.shape[1])
    row_index = lax.axis_index("row")
    levels = (width // rows_local).bit_length() - 1
    whole = values
    for bit_number in range(levels):
        other = from_partner(whole, "row", bit_number)
        upper = row_index >> bit_number & 1
        whole = jnp.where(
            upper == 1, jnp.concatenate([other, whole], 0), jnp.concatenate([whole, other], 0)
        )
    forward = product(inverse_rows, whole)
    partial_value = transposed(inverse_rows, forward)
    for bit_number in reversed(range(levels)):
        half = partial_value.shape[0] // 2
        upper = row_index >> bit_number & 1
        keep = jnp.where(upper == 1, partial_value[half:], partial_value[:half])
        outgoing = jnp.where(upper == 1, partial_value[:half], partial_value[half:])
        partial_value = keep + from_partner(outgoing, "row", bit_number)
    return partial_value


def per_device(rhs_sub, rhs_anc, inv_sub, panel_mid, panel_anc, block_mask, inv_anc):
    rhs_local = rhs_sub[0]
    rows_local = panel_anc.shape[2]
    width = panel_anc.shape[3]
    rows_own = rhs_local.shape[1]
    columns = rhs_local.shape[2]
    block_count = block_mask.shape[2]
    core = lax.axis_index("row") % 2
    leaf = lax.axis_index("leaf")
    x_bit, y_bit = leaf % 2, leaf // 2
    paired = lax.axis_size("leaf") == 4 and rows_local == 2 * width
    mask_rows = jnp.repeat(block_mask[0].astype(jnp.float32), rows_local // block_count, axis=1)[:, :, None]

    half = columns // 2
    mine = lax.dynamic_slice_in_dim(rhs_local, core * half, half, 2)
    other = core_swap(lax.dynamic_slice_in_dim(rhs_local, (1 - core) * half, half, 2))
    rhs_chip = by_core(core, mine, other, 1)
    matrices = jnp.stack([inv_sub[0, 0], inv_sub[0, 1], panel_mid[0]])
    inverse_first, inverse_second, middle = by_core(core, matrices, core_swap(matrices), 1)
    panel_first, panel_second = panel_anc[0, 0], panel_anc[0, 1]
    if paired:
        inverse_anc = lax.dynamic_slice_in_dim(inv_anc, y_bit * width, width, 0)

    part = half // CHUNKS
    pieces = []
    for chunk in range(CHUNKS):
        left = chunk * part
        rhs_part = rhs_chip[:, :, left : left + part]
        gathered = gather_rows(rhs_part[0], lower=True)
        first = product(inverse_first, gathered)
        first_all = gather_rows(first)
        residual = rhs_part[1] - product(middle, first_all)
        second = product(inverse_second, gather_rows(residual, lower=True))
        first_both = by_core(core, first_all, core_swap(first_all), 1)
        update = mask_rows[0] * product(panel_first, first_both)
        second_all = gather_rows(second)
        second_both = by_core(core, second_all, core_swap(second_all), 1)
        update = update + mask_rows[1] * product(panel_second, second_both)

        rhs_both = jnp.concatenate(
            [rhs_anc[:, left : left + part], rhs_anc[:, half + left : half + left + part]], 1
        )
        if paired:
            total = leaf_reduce(update, x_bit, y_bit)
            own = lax.dynamic_slice(rhs_both, (y_bit * width, x_bit * part), (width, part))
            forward = product(inverse_anc, own - total)
            solved = leaf_gather(transposed(inverse_anc, forward), x_bit, y_bit)
        else:
            total = lax.psum_scatter(update, "leaf", scatter_dimension=1, tiled=True)
            share = total.shape[1]
            own = lax.dynamic_slice_in_dim(rhs_both, leaf * share, share, 1)
            solved = lax.all_gather(ancestor_solve(inv_anc, own - total), "leaf", axis=1, tiled=True)

        def core_sum(value):
            keep = lax.dynamic_slice_in_dim(value, core * part, part, 1)
            return keep + core_swap(lax.dynamic_slice_in_dim(value, (1 - core) * part, part, 1))

        second_sum = reduce_rows(core_sum(transposed(panel_second, mask_rows[1] * solved)))
        x_second = reduce_rows(transposed(inverse_second, second - second_sum), lower=True)
        first_part = core_sum(transposed(panel_first, mask_rows[0] * solved))
        first_sum = reduce_rows(first_part + transposed(middle, x_second))
        x_first = reduce_rows(transposed(inverse_first, first - first_sum), lower=True)
        both = jnp.stack([x_first, x_second])
        keep = lax.dynamic_slice_in_dim(both, core * rows_own, rows_own, 1)
        other = core_swap(lax.dynamic_slice_in_dim(both, (1 - core) * rows_own, rows_own, 1))
        pieces.append((by_core(core, keep, other, 2), solved))

    def columns_in_order(values, axis):
        halves = [jnp.split(value, 2, axis) for value in values]
        return jnp.concatenate([h[0] for h in halves] + [h[1] for h in halves], axis)

    x_sub = columns_in_order([piece[0] for piece in pieces], 2)
    return x_sub[None], columns_in_order([piece[1] for piece in pieces], 1)


def solution(mesh):
    return jax.shard_map(
        per_device,
        mesh=mesh,
        in_specs=(
            P("leaf", None, "row", None),
            P("row", None),
            P("leaf", None, "row", None),
            P("leaf", "row", None),
            P("leaf", None, "row", None),
            P("leaf", None, "row"),
            P("row", None),
        ),
        out_specs=(P("leaf", None, "row", None), P("row", None)),
        check_vma=False,
    )
```

```python
import jax
import jax.numpy as jnp
from jax import lax
from jax.sharding import PartitionSpec as P

PRECISION = lax.Precision.HIGH


def product(left, right):
    return jnp.dot(left, right, precision=PRECISION, preferred_element_type=jnp.float32)


def transposed(left, right):
    return lax.dot_general(
        left,
        right,
        (((0,), (0,)), ((), ())),
        precision=PRECISION,
        preferred_element_type=jnp.float32,
    )


def core_swap(value):
    count = lax.axis_size("row")
    return lax.ppermute(value, "row", [(r, r ^ 1) for r in range(count)])


def leaf_swap(value, mask):
    count = lax.axis_size("leaf")
    return lax.ppermute(value, "leaf", [(g, g ^ mask) for g in range(count)])


def chip_digits(chips):
    digits, stride = [], 1
    while chips > 1:
        size = 4 if chips % 4 == 0 else 2
        digits.append((size, stride))
        stride *= size
        chips //= size
    return digits


def digit_permute(value, size, stride, moves):
    target = dict(moves)
    pairs = []
    for r in range(lax.axis_size("row")):
        digit = (r // 2) // stride % size
        if digit in target:
            pairs.append((r, r + 2 * stride * (target[digit] - digit)))
    return lax.ppermute(value, "row", pairs)


def digit_index(size, stride):
    return lax.axis_index("row") // 2 // stride % size


def gather_digit(value, size, stride, lower):
    def moves(pairs):
        return [(a, b) for a, b in pairs if a < b] if lower else pairs

    me = digit_index(size, stride)
    near = digit_permute(value, size, stride, moves([(0, 1), (1, 0), (2, 3), (3, 2)][: 2 if size == 2 else 4]))
    if size == 2:
        first = jnp.where(me == 0, value, near)
        last = jnp.where(me == 0, near, value)
        return jnp.concatenate([first, last], 0)
    inner = digit_permute(value, size, stride, moves([(1, 2), (2, 1)]))
    relay = digit_permute(near, size, stride, moves([(1, 2), (2, 1)]))
    far = digit_permute(near, size, stride, moves([(1, 3), (2, 0)]))
    outer = digit_permute(inner, size, stride, moves([(1, 0), (2, 3)]))
    middle = (me == 1) | (me == 2)
    third = jnp.where(middle, inner, outer)
    fourth = jnp.where(middle, relay, far)
    odd = me % 2 == 1
    even_one = jnp.where(odd, near, value)
    odd_one = jnp.where(odd, value, near)
    high = me >= 2
    return jnp.concatenate(
        [
            jnp.where(high, fourth, even_one),
            jnp.where(high, third, odd_one),
            jnp.where(high, even_one, third),
            jnp.where(high, odd_one, fourth),
        ],
        0,
    )


def reduce_digit(value, size, stride, lower):
    def moves(pairs):
        return [(a, b) for a, b in pairs if a > b] if lower else pairs

    me = digit_index(size, stride)
    rows = value.shape[0] // size
    blocks = value.reshape(size, rows, value.shape[1])

    def block(*table):
        index = jnp.take(jnp.array(table, jnp.int32), me)
        return lax.dynamic_index_in_dim(blocks, index, 0, keepdims=False)

    if size == 2:
        other = digit_permute(block(1, 0), size, stride, moves([(0, 1), (1, 0)]))
        return block(0, 1) + other
    far = digit_permute(block(3, 0, 3, 0), size, stride, moves([(3, 1), (0, 2)]))
    relay = digit_permute(block(0, 3, 0, 3), size, stride, moves([(2, 1), (1, 2)]))
    outer = digit_permute(block(2, 2, 1, 1), size, stride, moves([(0, 1), (3, 2)]))
    inner = digit_permute(block(2, 2, 1, 1) + outer, size, stride, moves([(1, 2), (2, 1)]))
    near = digit_permute(block(1, 0, 3, 2) + (far + relay), size, stride, moves([(0, 1), (1, 0), (2, 3), (3, 2)]))
    return block(0, 1, 2, 3) + near + inner


def gather_rows(value, lower=False):
    digits = chip_digits(lax.axis_size("row") // 2)
    for place, (size, stride) in enumerate(digits):
        value = gather_digit(value, size, stride, lower and place == len(digits) - 1)
    return value


def reduce_rows(value, lower=False):
    digits = chip_digits(lax.axis_size("row") // 2)
    for place, (size, stride) in reversed(list(enumerate(digits))):
        value = reduce_digit(value, size, stride, lower and place == len(digits) - 1)
    return value


def by_core(core, mine, other, axis):
    return jnp.concatenate(
        [jnp.where(core == 0, mine, other), jnp.where(core == 0, other, mine)], axis
    )


def leaf_reduce(update, x_bit, y_bit):
    rows, columns = update.shape
    half = columns // 2
    parts = update.reshape(2, 2, rows // 4, columns)

    def columns_of(value, bit):
        return jnp.where(bit == 0, value[..., :half], value[..., half:])

    def block_of(value, bit):
        return jnp.where(bit == 0, value[0], value[1])

    first, second = parts[:, 0], parts[:, 1]
    from_x = leaf_swap(columns_of(first, 1 - x_bit), 1)
    from_y = leaf_swap(block_of(second, 1 - y_bit), 2)
    first = columns_of(first, x_bit) + from_x
    second = block_of(second, y_bit) + from_y
    from_y = leaf_swap(block_of(first, 1 - y_bit), 2)
    from_x = leaf_swap(columns_of(second, 1 - x_bit), 1)
    return jnp.concatenate(
        [block_of(first, y_bit) + from_y, columns_of(second, x_bit) + from_x], 0
    )


def leaf_gather(piece, x_bit, y_bit):
    rows = piece.shape[0]
    first, second = piece[: rows // 2], piece[rows // 2 :]
    first_y = leaf_swap(first, 2)
    second_x = leaf_swap(second, 1)
    first = jnp.stack([first, first_y])
    second = jnp.stack([second, second_x])
    first_x = leaf_swap(first, 1)
    second_y = leaf_swap(second, 2)

    def at(block, column):
        own_block, own_column = y_bit == block, x_bit == column
        upper = jnp.where(
            own_column,
            jnp.where(own_block, first[0], first[1]),
            jnp.where(own_block, first_x[0], first_x[1]),
        )
        lower = jnp.where(
            own_block,
            jnp.where(own_column, second[0], second[1]),
            jnp.where(own_column, second_y[0], second_y[1]),
        )
        return [upper, lower]

    return [jnp.concatenate(at(0, column) + at(1, column), 0) for column in range(2)]


def from_partner(value, axis, bit):
    mask = 2**bit
    pairs = [(source, source ^ mask) for source in range(lax.axis_size(axis))]
    return lax.ppermute(value, axis, pairs)


def ancestor_solve(inverse_rows, values):
    rows_local, width = inverse_rows.shape
    if rows_local >= width:
        blocks = inverse_rows.reshape(rows_local // width, width, width)
        grouped = values.reshape(rows_local // width, width, values.shape[1])
        forward = jnp.einsum("kij,kjr->kir", blocks, grouped, precision=PRECISION)
        result = jnp.einsum("kji,kjr->kir", blocks, forward, precision=PRECISION)
        return result.reshape(rows_local, values.shape[1])
    row_index = lax.axis_index("row")
    levels = (width // rows_local).bit_length() - 1
    whole = values
    for bit_number in range(levels):
        other = from_partner(whole, "row", bit_number)
        upper = row_index >> bit_number & 1
        whole = jnp.where(
            upper == 1, jnp.concatenate([other, whole], 0), jnp.concatenate([whole, other], 0)
        )
    forward = product(inverse_rows, whole)
    partial_value = transposed(inverse_rows, forward)
    for bit_number in reversed(range(levels)):
        half = partial_value.shape[0] // 2
        upper = row_index >> bit_number & 1
        keep = jnp.where(upper == 1, partial_value[half:], partial_value[:half])
        outgoing = jnp.where(upper == 1, partial_value[:half], partial_value[half:])
        partial_value = keep + from_partner(outgoing, "row", bit_number)
    return partial_value


def per_device(rhs_sub, rhs_anc, inv_sub, panel_mid, panel_anc, block_mask, inv_anc):
    rhs_local = rhs_sub[0]
    rows_local = panel_anc.shape[2]
    width = panel_anc.shape[3]
    rows_own = rhs_local.shape[1]
    columns = rhs_local.shape[2]
    block_count = block_mask.shape[2]
    row_index = lax.axis_index("row")
    core = row_index % 2
    leaf = lax.axis_index("leaf")
    x_bit, y_bit = leaf % 2, leaf // 2
    paired = lax.axis_size("leaf") == 4 and rows_local == 2 * width
    mask = block_mask[0].astype(jnp.float32)
    half = columns // 2

    def masked(slot, value):
        blocks = value.reshape(block_count, rows_local // block_count, value.shape[1])
        return (blocks * mask[slot][:, None, None]).reshape(value.shape)

    def halves(value):
        return jnp.where(core == 0, value[..., :half], value[..., half:])

    def other_half(value):
        return jnp.where(core == 0, value[..., half:], value[..., :half])

    rhs_chip = by_core(core, halves(rhs_local), core_swap(other_half(rhs_local)), 1)
    matrices = jnp.stack([inv_sub[0, 0], inv_sub[0, 1], panel_mid[0]])
    inverse_first, inverse_second, middle = by_core(core, matrices, core_swap(matrices), 1)
    panel_first, panel_second = panel_anc[0, 0], panel_anc[0, 1]

    def both_halves(value):
        return by_core(core, value, core_swap(value), 1)

    first = product(inverse_first, gather_rows(rhs_chip[0], lower=True))
    first_all = gather_rows(first)
    residual = rhs_chip[1] - product(middle, first_all)
    second = product(inverse_second, gather_rows(residual, lower=True))
    update_first = masked(0, product(panel_first, both_halves(first_all)))
    second_all = gather_rows(second)
    update = update_first + masked(1, product(panel_second, both_halves(second_all)))

    local_inverses, second_all, first_all = lax.optimization_barrier(
        (inv_sub[0], second_all, first_all)
    )
    whole_second = lax.all_gather(local_inverses[1], "row", axis=0, tiled=True)
    whole_first = lax.all_gather(local_inverses[0], "row", axis=0, tiled=True)

    if paired:
        inverse_anc = jnp.where(y_bit == 0, inv_anc[:width], inv_anc[width:])
        total = leaf_reduce(update, x_bit, y_bit)
        own = jnp.where(y_bit == 0, rhs_anc[:width], rhs_anc[width:])
        own = jnp.where(x_bit == 0, own[:, :half], own[:, half:])
        forward = product(inverse_anc, own - total)
        solved = leaf_gather(transposed(inverse_anc, forward), x_bit, y_bit)
    else:
        total = lax.psum_scatter(update, "leaf", scatter_dimension=1, tiled=True)
        share = total.shape[1]
        own = lax.dynamic_slice_in_dim(rhs_anc, leaf * share, share, 1)
        whole = lax.all_gather(ancestor_solve(inv_anc, own - total), "leaf", axis=1, tiled=True)
        solved = [whole[:, :half], whole[:, half:]]

    def chip_sum(panel, slot):
        outgoing = transposed(panel, masked(slot, jnp.where(core == 0, solved[1], solved[0])))
        received = core_swap(outgoing)
        return received + transposed(panel, masked(slot, jnp.where(core == 0, solved[0], solved[1])))

    rows_chip = 2 * rows_own
    start = row_index // 2 * rows_chip

    def chip_columns(matrix):
        return lax.dynamic_slice_in_dim(matrix, start, rows_chip, 1)

    second_base = transposed(chip_columns(whole_second), second_all)
    first_base = transposed(chip_columns(whole_first), first_all)
    middle_first = product(middle, whole_first)

    x_second = second_base - reduce_rows(transposed(whole_second, chip_sum(panel_second, 1)))
    first_part = transposed(whole_first, chip_sum(panel_first, 0))
    x_first = first_base - reduce_rows(first_part + transposed(middle_first, x_second))

    both = jnp.stack([x_first, x_second])
    keep = jnp.where(core == 0, both[:, :rows_own], both[:, rows_own:])
    send = jnp.where(core == 0, both[:, rows_own:], both[:, :rows_own])
    x_sub = by_core(core, keep, core_swap(send), 2)
    return x_sub[None], jnp.concatenate(solved, 1)


def solution(mesh):
    return jax.shard_map(
        per_device,
        mesh=mesh,
        in_specs=(
            P("leaf", None, "row", None),
            P("row", None),
            P("leaf", None, "row", None),
            P("leaf", "row", None),
            P("leaf", None, "row", None),
            P("leaf", None, "row"),
            P("row", None),
        ),
        out_specs=(P("leaf", None, "row", None), P("row", None)),
        check_vma=False,
    )
```

```python
import functools

import jax
import jax.numpy as jnp
from jax import lax
from jax.experimental import pallas as pl
from jax.experimental.layout import Layout, with_layout_constraint
from jax.experimental.pallas import tpu as pltpu
from jax.sharding import PartitionSpec as P

PRECISION = lax.Precision.HIGH


def product(left, right):
    return jnp.dot(left, right, precision=PRECISION, preferred_element_type=jnp.float32)


def transposed(left, right):
    return lax.dot_general(
        left,
        right,
        (((0,), (0,)), ((), ())),
        precision=PRECISION,
        preferred_element_type=jnp.float32,
    )


def row_major(value):
    return with_layout_constraint(value, Layout(tuple(range(value.ndim))))


def core_swap(value):
    count = lax.axis_size("row")
    return lax.ppermute(value, "row", [(r, r ^ 1) for r in range(count)])


def leaf_swap(value, mask):
    count = lax.axis_size("leaf")
    return lax.ppermute(value, "leaf", [(g, g ^ mask) for g in range(count)])


def chip_digits(chips):
    digits, stride = [], 1
    while chips > 1:
        size = 4 if chips % 4 == 0 else 2
        digits.append((size, stride))
        stride *= size
        chips //= size
    return digits


def digit_permute(value, size, stride, moves):
    target = dict(moves)
    pairs = []
    for r in range(lax.axis_size("row")):
        digit = (r // 2) // stride % size
        if digit in target:
            pairs.append((r, r + 2 * stride * (target[digit] - digit)))
    return lax.ppermute(value, "row", pairs)


def digit_index(size, stride):
    return lax.axis_index("row") // 2 // stride % size


def after(values, filler):
    return lax.optimization_barrier((*values, filler))


def gather_digit(value, size, stride, lower, filler):
    def moves(pairs):
        return [(a, b) for a, b in pairs if a < b] if lower else pairs

    me = digit_index(size, stride)
    near = digit_permute(value, size, stride, moves([(0, 1), (1, 0), (2, 3), (3, 2)][: 2 if size == 2 else 4]))
    if size == 2:
        near, filler = after((near,), filler)
        first = jnp.where(me == 0, value, near)
        last = jnp.where(me == 0, near, value)
        return jnp.concatenate([first, last], 0), filler
    inner = digit_permute(value, size, stride, moves([(1, 2), (2, 1)]))
    relay = digit_permute(near, size, stride, moves([(1, 2), (2, 1)]))
    far = digit_permute(near, size, stride, moves([(1, 3), (2, 0)]))
    outer = digit_permute(inner, size, stride, moves([(1, 0), (2, 3)]))
    relay, far, outer, filler = after((relay, far, outer), filler)
    middle = (me == 1) | (me == 2)
    third = jnp.where(middle, inner, outer)
    fourth = jnp.where(middle, relay, far)
    odd = me % 2 == 1
    even_one = jnp.where(odd, near, value)
    odd_one = jnp.where(odd, value, near)
    high = me >= 2
    blocks = [
        jnp.where(high, fourth, even_one),
        jnp.where(high, third, odd_one),
        jnp.where(high, even_one, third),
        jnp.where(high, odd_one, fourth),
    ]
    return jnp.concatenate(blocks, 0), filler


def reduce_digit(value, size, stride, lower, filler):
    def moves(pairs):
        return [(a, b) for a, b in pairs if a > b] if lower else pairs

    me = digit_index(size, stride)
    rows = value.shape[0] // size
    blocks = value.reshape(size, rows, value.shape[1])

    def block(*table):
        index = jnp.take(jnp.array(table, jnp.int32), me)
        return lax.dynamic_index_in_dim(blocks, index, 0, keepdims=False)

    if size == 2:
        other = digit_permute(block(1, 0), size, stride, moves([(0, 1), (1, 0)]))
        other, filler = after((other,), filler)
        return block(0, 1) + other, filler
    far = digit_permute(block(3, 0, 3, 0), size, stride, moves([(3, 1), (0, 2)]))
    relay = digit_permute(block(0, 3, 0, 3), size, stride, moves([(2, 1), (1, 2)]))
    outer = digit_permute(block(2, 2, 1, 1), size, stride, moves([(0, 1), (3, 2)]))
    inner = digit_permute(block(2, 2, 1, 1) + outer, size, stride, moves([(1, 2), (2, 1)]))
    near = digit_permute(block(1, 0, 3, 2) + (far + relay), size, stride, moves([(0, 1), (1, 0), (2, 3), (3, 2)]))
    near, inner, filler = after((near, inner), filler)
    return block(0, 1, 2, 3) + near + inner, filler


def gather_rows(value, lower=False, filler=()):
    digits = chip_digits(lax.axis_size("row") // 2)
    for place, (size, stride) in enumerate(digits):
        outermost = place == len(digits) - 1
        value, filler = gather_digit(value, size, stride, lower and outermost, filler)
    return value, filler


def reduce_rows(value, lower=False, filler=()):
    digits = chip_digits(lax.axis_size("row") // 2)
    for place, (size, stride) in reversed(list(enumerate(digits))):
        outermost = place == len(digits) - 1
        value, filler = reduce_digit(value, size, stride, lower and outermost, filler)
    return value, filler


def by_core(core, mine, other, axis):
    return jnp.concatenate(
        [jnp.where(core == 0, mine, other), jnp.where(core == 0, other, mine)], axis
    )


def leaf_reduce(upper, lower):
    from_x = leaf_swap(upper[0], 1)
    from_y = leaf_swap(lower[0], 2)
    from_x, from_y = lax.optimization_barrier((from_x, from_y))
    first = leaf_swap(upper[1][0] + from_x[0], 2)
    second = leaf_swap(lower[1][0] + from_y[0], 1)
    first, second = lax.optimization_barrier((first, second))
    return jnp.concatenate(
        [upper[1][1] + from_x[1] + first, lower[1][1] + from_y[1] + second], 0
    )


def leaf_gather(piece):
    rows = piece.shape[0]
    first, second = piece[: rows // 2], piece[rows // 2 :]
    first_y = leaf_swap(first, 2)
    second_x = leaf_swap(second, 1)
    first_y, second_x = lax.optimization_barrier((first_y, second_x))
    upper = jnp.stack([first, first_y])
    lower = jnp.stack([second, second_x])
    upper_far = leaf_swap(upper, 1)
    lower_far = leaf_swap(lower, 2)
    upper_far, lower_far = lax.optimization_barrier((upper_far, lower_far))
    return upper, upper_far, lower, lower_far


def in_order(pieces, x_bit, y_bit):
    upper, upper_far, lower, lower_far = pieces

    def at(block, column):
        own_block, own_column = y_bit == block, x_bit == column
        return [
            jnp.where(
                own_column,
                jnp.where(own_block, upper[0], upper[1]),
                jnp.where(own_block, upper_far[0], upper_far[1]),
            ),
            jnp.where(
                own_block,
                jnp.where(own_column, lower[0], lower[1]),
                jnp.where(own_column, lower_far[0], lower_far[1]),
            ),
        ]

    return jnp.concatenate(
        [jnp.concatenate(at(0, column) + at(1, column), 0) for column in range(2)], 1
    )


def split(value):
    high = value.astype(jnp.bfloat16)
    return high, (value - high.astype(jnp.float32)).astype(jnp.bfloat16)


def scale_rows(value, mask_ref, slot, first_block, count):
    rows = value.shape[0] // count
    return jnp.concatenate(
        [
            value[k * rows : (k + 1) * rows] * mask_ref[slot, first_block + k].astype(jnp.float32)
            for k in range(count)
        ],
        0,
    )


def forward_kernel(slot, place, tiles, mask_blocks, bit_ref, mask_ref, panel_ref, near_ref, far_ref, *refs):
    prev, (out_first, out_last, high, low) = refs[:-4], refs[-4:]
    turn, step = pl.program_id(0), pl.program_id(1)
    columns = near_ref.shape[1]

    @pl.when((turn == 0) & (step == 0))
    def _():
        for k, ref in enumerate((near_ref, far_ref)):
            part = split(ref[...])
            high[:, k * columns : (k + 1) * columns] = part[0]
            low[:, k * columns : (k + 1) * columns] = part[1]

    panel_high, panel_low = split(panel_ref[...])

    def dot(left, right):
        return jnp.dot(left, right, preferred_element_type=jnp.float32)

    result = dot(panel_high, high[...]) + (dot(panel_high, low[...]) + dot(panel_low, high[...]))
    block = jnp.where(turn == 0, 1 - bit_ref[0], bit_ref[0])
    tile = (2 * block + place) * tiles + step
    result = scale_rows(result, mask_ref, slot, tile * mask_blocks, mask_blocks)
    near, far = result[:, :columns], result[:, columns:]
    if place == 0:
        out_first[...] = near + prev[0][...] if prev else near
        out_last[...] = far + prev[1][...] if prev else far
    else:

        @pl.when(turn == 0)
        def _():
            out_first[0] = near + prev[0][0] if prev else near
            out_first[1] = far + prev[0][1] if prev else far

        @pl.when(turn == 1)
        def _():
            out_last[0] = near + prev[1][0] if prev else near
            out_last[1] = far + prev[1][1] if prev else far


def panel_forward(panel_anc, mask, slot, place, y_bit, near, far, prev=(), tile_rows=256):
    rows_local, width = panel_anc.shape[2:]
    quarter = rows_local // 4
    tiles = quarter // tile_rows
    columns = near.shape[1]
    mask_blocks = mask.shape[1] // (4 * tiles)

    def panel_index(turn, step, bit_ref, mask_ref):
        block = jnp.where(turn == 0, 1 - bit_ref[0], bit_ref[0])
        return (0, slot, (2 * block + place) * tiles + step, 0)

    whole = pl.BlockSpec(near.shape, lambda *_: (0, 0))
    if place == 0:
        out_specs = [
            pl.BlockSpec((None, tile_rows, columns), lambda turn, step, *_: (turn, step, 0))
        ] * 2
    else:
        out_specs = [
            pl.BlockSpec(
                (2, tile_rows, columns),
                lambda turn, step, *_: (0, jnp.where(turn == 0, step, tiles - 1), 0),
            ),
            pl.BlockSpec(
                (2, tile_rows, columns), lambda turn, step, *_: (0, jnp.where(turn == 0, 0, step), 0)
            ),
        ]
    shape = jax.ShapeDtypeStruct((2, quarter, columns), jnp.float32)
    return pl.pallas_call(
        functools.partial(forward_kernel, slot, place, tiles, mask_blocks),
        out_shape=[shape, shape],
        grid_spec=pltpu.PrefetchScalarGridSpec(
            num_scalar_prefetch=2,
            grid=(2, tiles),
            in_specs=[
                pl.BlockSpec((None, None, tile_rows, width), panel_index),
                whole,
                whole,
                *(out_specs if prev else []),
            ],
            out_specs=out_specs,
            scratch_shapes=[pltpu.VMEM((width, 2 * columns), jnp.bfloat16)] * 2,
        ),
        cost_estimate=pl.CostEstimate(
            flops=12 * quarter * width * 2 * columns,
            bytes_accessed=4 * (2 * quarter * width + 2 * width * columns + 4 * quarter * columns),
            transcendentals=0,
        ),
        name=f"panel_forward_{slot}_{place}",
    )(y_bit.reshape(1).astype(jnp.int32), mask, panel_anc, near, far, *prev)


def backward_kernel(slot, tiles, mask_blocks, bit_ref, mask_ref, panel_ref, upper_near, upper_far, lower_near, lower_far, out_near, out_far, panel_parts, value_parts, total):
    place, turn, step = pl.program_id(0), pl.program_id(1), pl.program_id(2)
    rows = panel_ref.shape[0]
    columns = out_near.shape[1]
    block = jnp.where(turn == 0, bit_ref[0], 1 - bit_ref[0])
    tile = (2 * block + place) * tiles + step

    def put(near, far):
        for k, value in enumerate((near, far)):
            value = scale_rows(value, mask_ref, slot, tile * mask_blocks, mask_blocks)
            high, low = split(value)
            span = slice(k * columns, (k + 1) * columns)
            value_parts[0:rows, span] = high
            value_parts[rows : 2 * rows, span] = high
            value_parts[2 * rows : 3 * rows, span] = low

    @pl.when(place == 0)
    def _():
        put(upper_near[...], upper_far[...])

    @pl.when((place == 1) & (turn == 0))
    def _():
        put(lower_near[0], lower_near[1])

    @pl.when((place == 1) & (turn == 1))
    def _():
        put(lower_far[0], lower_far[1])

    high, low = split(panel_ref[...])
    panel_parts[0:rows] = high
    panel_parts[rows : 2 * rows] = low
    panel_parts[2 * rows : 3 * rows] = high
    result = lax.dot_general(
        panel_parts[...], value_parts[...], (((0,), (0,)), ((), ())), preferred_element_type=jnp.float32
    )
    start = (place == 0) & (turn == 0) & (step == 0)
    end = (place == 1) & (turn == 1) & (step == tiles - 1)

    @pl.when(start)
    def _():
        total[...] = result

    @pl.when(jnp.logical_not(start))
    def _():
        total[...] += result

    @pl.when(end)
    def _():
        out_near[...] = total[:, :columns]
        out_far[...] = total[:, columns:]


def panel_backward(panel_anc, mask, slot, y_bit, pieces, tile_rows=256):
    upper_near, upper_far, lower_near, lower_far = pieces
    rows_local, width = panel_anc.shape[2:]
    quarter = rows_local // 4
    tiles = quarter // tile_rows
    columns = upper_near.shape[2]
    mask_blocks = mask.shape[1] // (4 * tiles)

    def panel_index(place, turn, step, bit_ref, mask_ref):
        block = jnp.where(turn == 0, bit_ref[0], 1 - bit_ref[0])
        return (0, slot, (2 * block + place) * tiles + step, 0)

    def upper_index(place, turn, step, *_):
        return (jnp.where(place == 0, turn, 1), jnp.where(place == 0, step, tiles - 1), 0)

    def lower_index(mine):
        def index(place, turn, step, *_):
            before = (place == 0) | (turn < mine)
            after = (place == 1) & (turn > mine)
            return (0, jnp.where(before, 0, jnp.where(after, tiles - 1, step)), 0)

        return index

    out_spec = pl.BlockSpec((width, columns), lambda *_: (0, 0))
    shape = jax.ShapeDtypeStruct((width, columns), jnp.float32)
    return pl.pallas_call(
        functools.partial(backward_kernel, slot, tiles, mask_blocks),
        out_shape=[shape, shape],
        grid_spec=pltpu.PrefetchScalarGridSpec(
            num_scalar_prefetch=2,
            grid=(2, 2, tiles),
            in_specs=[
                pl.BlockSpec((None, None, tile_rows, width), panel_index),
                pl.BlockSpec((None, tile_rows, columns), upper_index),
                pl.BlockSpec((None, tile_rows, columns), upper_index),
                pl.BlockSpec((2, tile_rows, columns), lower_index(0)),
                pl.BlockSpec((2, tile_rows, columns), lower_index(1)),
            ],
            out_specs=[out_spec, out_spec],
            scratch_shapes=[
                pltpu.VMEM((3 * tile_rows, width), jnp.bfloat16),
                pltpu.VMEM((3 * tile_rows, 2 * columns), jnp.bfloat16),
                pltpu.VMEM((width, 2 * columns), jnp.float32),
            ],
        ),
        cost_estimate=pl.CostEstimate(
            flops=6 * rows_local * width * 2 * columns,
            bytes_accessed=4 * (rows_local * width + 2 * rows_local * columns + 2 * width * columns),
            transcendentals=0,
        ),
        name=f"panel_backward_{slot}",
    )(y_bit.reshape(1).astype(jnp.int32), mask, panel_anc, upper_near, upper_far, lower_near, lower_far)


def from_partner(value, axis, bit):
    mask = 2**bit
    pairs = [(source, source ^ mask) for source in range(lax.axis_size(axis))]
    return lax.ppermute(value, axis, pairs)


def ancestor_solve(inverse_rows, values):
    rows_local, width = inverse_rows.shape
    if rows_local >= width:
        blocks = inverse_rows.reshape(rows_local // width, width, width)
        grouped = values.reshape(rows_local // width, width, values.shape[1])
        forward = jnp.einsum("kij,kjr->kir", blocks, grouped, precision=PRECISION)
        result = jnp.einsum("kji,kjr->kir", blocks, forward, precision=PRECISION)
        return result.reshape(rows_local, values.shape[1])
    row_index = lax.axis_index("row")
    levels = (width // rows_local).bit_length() - 1
    whole = values
    for bit_number in range(levels):
        other = from_partner(whole, "row", bit_number)
        upper = row_index >> bit_number & 1
        whole = jnp.where(
            upper == 1, jnp.concatenate([other, whole], 0), jnp.concatenate([whole, other], 0)
        )
    forward = product(inverse_rows, whole)
    partial_value = transposed(inverse_rows, forward)
    for bit_number in reversed(range(levels)):
        half = partial_value.shape[0] // 2
        upper = row_index >> bit_number & 1
        keep = jnp.where(upper == 1, partial_value[half:], partial_value[:half])
        outgoing = jnp.where(upper == 1, partial_value[:half], partial_value[half:])
        partial_value = keep + from_partner(outgoing, "row", bit_number)
    return partial_value


def per_device(rhs_sub, rhs_anc, inv_sub, panel_mid, panel_anc, block_mask, inv_anc):
    rhs_local = rhs_sub[0]
    rows_local = panel_anc.shape[2]
    width = panel_anc.shape[3]
    rows_own = rhs_local.shape[1]
    columns = rhs_local.shape[2]
    block_count = block_mask.shape[2]
    row_index = lax.axis_index("row")
    core = row_index % 2
    leaf = lax.axis_index("leaf")
    x_bit, y_bit = leaf % 2, leaf // 2
    paired = lax.axis_size("leaf") == 4 and rows_local == 2 * width
    mask = block_mask[0].astype(jnp.float32)
    half = columns // 2

    def masked(slot, value):
        blocks = value.reshape(block_count, rows_local // block_count, value.shape[1])
        return (blocks * mask[slot][:, None, None]).reshape(value.shape)

    def halves(value):
        return jnp.where(core == 0, value[..., :half], value[..., half:])

    def other_half(value):
        return jnp.where(core == 0, value[..., half:], value[..., :half])

    rhs_chip = by_core(core, halves(rhs_local), core_swap(other_half(rhs_local)), 1)
    matrices = jnp.stack([inv_sub[0, 0], inv_sub[0, 1], panel_mid[0]])
    inverse_first, inverse_second, middle = by_core(core, matrices, core_swap(matrices), 1)
    panel_first, panel_second = panel_anc[0, 0], panel_anc[0, 1]

    def both_halves(value):
        return by_core(core, value, core_swap(value), 1)

    def near_and_far(value):
        swapped = core_swap(value)
        far_is_mine = core == x_bit
        return jnp.where(far_is_mine, swapped, value), jnp.where(far_is_mine, value, swapped)

    block_mask = block_mask[0]
    gathered, _ = gather_rows(rhs_chip[0], lower=True)
    first = product(inverse_first, gathered)
    first_all, _ = gather_rows(first)
    residual = rhs_chip[1] - product(middle, first_all)
    if paired:
        sides = near_and_far(first_all)
        upper = panel_forward(panel_anc, block_mask, 0, 0, y_bit, *sides)
        lower = panel_forward(panel_anc, block_mask, 0, 1, y_bit, *sides)
        gathered, upper = gather_rows(residual, lower=True, filler=upper)
        second = product(inverse_second, gathered)
        second_all, lower = gather_rows(second, filler=lower)
        sides = near_and_far(second_all)
        upper = panel_forward(panel_anc, block_mask, 1, 0, y_bit, *sides, upper)
        lower = panel_forward(panel_anc, block_mask, 1, 1, y_bit, *sides, lower)
    else:
        gathered, _ = gather_rows(residual, lower=True)
        second = product(inverse_second, gathered)
        update = masked(0, product(panel_first, both_halves(first_all)))
        second_all, _ = gather_rows(second)
        update = update + masked(1, product(panel_second, both_halves(second_all)))

    local_inverses, second_all, first_all = lax.optimization_barrier(
        (inv_sub[0], second_all, first_all)
    )
    whole_second = lax.all_gather(local_inverses[1], "row", axis=0, tiled=True)
    whole_first = lax.all_gather(local_inverses[0], "row", axis=0, tiled=True)

    if paired:
        inverse_anc = jnp.where(y_bit == 0, inv_anc[:width], inv_anc[width:])
        own = jnp.where(y_bit == 0, rhs_anc[:width], rhs_anc[width:])
        own = jnp.where(x_bit == 0, own[:, :half], own[:, half:])
        total = leaf_reduce(upper, lower)
        forward = product(inverse_anc, own - total)
        solved = row_major(transposed(inverse_anc, forward))
        pieces = leaf_gather(solved)
        x_anc = in_order(pieces, x_bit, y_bit)
    else:
        total = lax.psum_scatter(update, "leaf", scatter_dimension=1, tiled=True)
        share = total.shape[1]
        own = lax.dynamic_slice_in_dim(rhs_anc, leaf * share, share, 1)
        x_anc = lax.all_gather(ancestor_solve(inv_anc, own - total), "leaf", axis=1, tiled=True)

    def chip_sum(slot):
        if paired:
            mine, other = panel_backward(panel_anc, block_mask, slot, y_bit, pieces)
            straight = x_bit == core
            keep, send = jnp.where(straight, mine, other), jnp.where(straight, other, mine)
        else:
            keep, send = (
                transposed(panel_anc[0, slot], masked(slot, part))
                for part in (halves(x_anc), other_half(x_anc))
            )
        return keep + core_swap(send)

    rows_chip = 2 * rows_own
    start = row_index // 2 * rows_chip

    def chip_columns(matrix):
        return lax.dynamic_slice_in_dim(matrix, start, rows_chip, 1)

    second_base = transposed(chip_columns(whole_second), second_all)
    first_base = transposed(chip_columns(whole_first), first_all)
    middle_first = product(middle, whole_first)

    second_partial = transposed(whole_second, chip_sum(1))
    first_part = transposed(whole_first, chip_sum(0))
    second_total, first_part = reduce_rows(second_partial, filler=first_part)
    x_second = second_base - second_total
    first_total, x_anc = reduce_rows(first_part + transposed(middle_first, x_second), filler=x_anc)
    x_first = first_base - first_total

    both = jnp.stack([x_first, x_second])
    keep = jnp.where(core == 0, both[:, :rows_own], both[:, rows_own:])
    send = jnp.where(core == 0, both[:, rows_own:], both[:, :rows_own])
    x_sub = by_core(core, keep, core_swap(send), 2)
    return x_sub[None], x_anc


def solution(mesh):
    return jax.shard_map(
        per_device,
        mesh=mesh,
        in_specs=(
            P("leaf", None, "row", None),
            P("row", None),
            P("leaf", None, "row", None),
            P("leaf", "row", None),
            P("leaf", None, "row", None),
            P("leaf", None, "row"),
            P("row", None),
        ),
        out_specs=(P("leaf", None, "row", None), P("row", None)),
        check_vma=False,
    )
```

```python
import functools

import jax
import jax.numpy as jnp
from jax import lax
from jax.experimental import pallas as pl
from jax.experimental.layout import Layout, with_layout_constraint
from jax.experimental.pallas import tpu as pltpu
from jax.sharding import PartitionSpec as P

PRECISION = lax.Precision.HIGH


def product(left, right):
    return jnp.dot(left, right, precision=PRECISION, preferred_element_type=jnp.float32)


def transposed(left, right):
    return lax.dot_general(
        left,
        right,
        (((0,), (0,)), ((), ())),
        precision=PRECISION,
        preferred_element_type=jnp.float32,
    )


def row_major(value):
    return with_layout_constraint(value, Layout(tuple(range(value.ndim))))


def core_swap(value):
    count = lax.axis_size("row")
    return lax.ppermute(value, "row", [(r, r ^ 1) for r in range(count)])


def leaf_swap(value, mask):
    count = lax.axis_size("leaf")
    return lax.ppermute(value, "leaf", [(g, g ^ mask) for g in range(count)])


def chip_digits(chips):
    digits, stride = [], 1
    while chips > 1:
        size = 4 if chips % 4 == 0 else 2
        digits.append((size, stride))
        stride *= size
        chips //= size
    return digits


def digit_permute(value, size, stride, moves):
    target = dict(moves)
    pairs = []
    for r in range(lax.axis_size("row")):
        digit = (r // 2) // stride % size
        if digit in target:
            pairs.append((r, r + 2 * stride * (target[digit] - digit)))
    return lax.ppermute(value, "row", pairs)


def digit_index(size, stride):
    return lax.axis_index("row") // 2 // stride % size


def after(values, filler):
    return lax.optimization_barrier((*values, filler))


def gather_near(value, size, stride, lower=False):
    def moves(pairs):
        return [(a, b) for a, b in pairs if a < b] if lower else pairs

    if size == 2:
        return (digit_permute(value, size, stride, moves([(0, 1), (1, 0)])),)
    near = digit_permute(value, size, stride, moves([(0, 1), (1, 0), (2, 3), (3, 2)]))
    inner = digit_permute(value, size, stride, moves([(1, 2), (2, 1)]))
    return near, inner


def gather_far(received, size, stride, lower=False):
    def moves(pairs):
        return [(a, b) for a, b in pairs if a < b] if lower else pairs

    if size == 2:
        return ()
    near, inner = received
    relay = digit_permute(near, size, stride, moves([(1, 2), (2, 1)]))
    far = digit_permute(near, size, stride, moves([(1, 3), (2, 0)]))
    outer = digit_permute(inner, size, stride, moves([(1, 0), (2, 3)]))
    return relay, far, outer


def gather_join(value, received, passed, size, stride):
    me = digit_index(size, stride)
    if size == 2:
        (near,) = received
        return [jnp.where(me == 0, value, near), jnp.where(me == 0, near, value)]
    near, inner = received
    relay, far, outer = passed
    middle = (me == 1) | (me == 2)
    third = jnp.where(middle, inner, outer)
    fourth = jnp.where(middle, relay, far)
    odd = me % 2 == 1
    even_one = jnp.where(odd, near, value)
    odd_one = jnp.where(odd, value, near)
    high = me >= 2
    return [
        jnp.where(high, fourth, even_one),
        jnp.where(high, third, odd_one),
        jnp.where(high, even_one, third),
        jnp.where(high, odd_one, fourth),
    ]


def gather_both(value, size, stride):
    received = gather_near(value, size, stride)
    return received, gather_far(received, size, stride)


def gather_digit(value, size, stride, lower, filler):
    received = gather_near(value, size, stride, lower)
    passed = gather_far(received, size, stride, lower)
    last, filler = after((passed or received,), filler)
    received, passed = (received, last) if passed else (last, passed)
    return jnp.concatenate(gather_join(value, received, passed, size, stride), 0), filler


def reduce_digit(value, size, stride, lower, filler):
    def moves(pairs):
        return [(a, b) for a, b in pairs if a > b] if lower else pairs

    rows = value.shape[0] // size
    block = [value[k * rows : (k + 1) * rows] for k in range(size)]
    if size == 2:
        other = digit_permute(block[0], size, stride, moves([(0, 1), (1, 0)]))
        other, filler = after((other,), filler)
        return block[1] + other, filler
    far = digit_permute(block[0], size, stride, moves([(3, 1), (0, 2)]))
    relay = digit_permute(block[0], size, stride, moves([(2, 1), (1, 2)]))
    outer = digit_permute(block[1], size, stride, moves([(0, 1), (3, 2)]))
    inner = digit_permute(block[1] + outer, size, stride, moves([(1, 2), (2, 1)]))
    near = digit_permute(block[2] + (far + relay), size, stride, moves([(0, 1), (1, 0), (2, 3), (3, 2)]))
    near, inner, filler = after((near, inner), filler)
    return block[3] + near + inner, filler


def sending_order(value, size, stride, axis):
    length = value.shape[axis] // size
    me = digit_index(size, stride)
    if size == 2:
        order = (1 - me, me)
    else:
        high = me >= 2
        order = (jnp.where(high, 0, 3), jnp.where(high, 1, 2), me ^ 1, me)
    return jnp.concatenate(
        [lax.dynamic_slice_in_dim(value, k * length, length, axis) for k in order], axis
    )


def gather_rows(value, lower=False, filler=()):
    digits = chip_digits(lax.axis_size("row") // 2)
    for place, (size, stride) in enumerate(digits):
        outermost = place == len(digits) - 1
        value, filler = gather_digit(value, size, stride, lower and outermost, filler)
    return value, filler


def row_digits():
    return chip_digits(lax.axis_size("row") // 2)


def reduce_rows(value, lower=False, filler=()):
    digits = row_digits()
    for place, (size, stride) in reversed(list(enumerate(digits))):
        outermost = place == len(digits) - 1
        if not outermost:
            value = sending_order(value, size, stride, 0)
        value, filler = reduce_digit(value, size, stride, lower and outermost, filler)
    return value, filler


def by_core(core, mine, other, axis):
    return jnp.concatenate(
        [jnp.where(core == 0, mine, other), jnp.where(core == 0, other, mine)], axis
    )


def leaf_reduce(upper, lower, side):
    from_x = leaf_swap(upper[0], 1)
    from_y = leaf_swap(lower[0], 2)
    from_x, side = after((from_x,), side)
    from_x, from_y = lax.optimization_barrier((from_x, from_y))
    first = leaf_swap(upper[1][0] + from_x[0], 2)
    second = leaf_swap(lower[1][0] + from_y[0], 1)
    first, second = lax.optimization_barrier((first, second))
    return jnp.concatenate(
        [upper[1][1] + from_x[1] + first, lower[1][1] + from_y[1] + second], 0
    ), side


def leaf_gather(piece, side):
    rows = piece.shape[0]
    first, second = piece[: rows // 2], piece[rows // 2 :]
    first_y = leaf_swap(first, 2)
    second_x = leaf_swap(second, 1)
    first_y, second_x, side = after((first_y, second_x), side)
    upper = jnp.stack([first, first_y])
    lower = jnp.stack([second, second_x])
    upper_far = leaf_swap(upper, 1)
    lower_far = leaf_swap(lower, 2)
    upper_far, lower_far = lax.optimization_barrier((upper_far, lower_far))
    return (upper, upper_far, lower, lower_far), side


def in_order(pieces, x_bit, y_bit):
    upper, upper_far, lower, lower_far = pieces

    def at(block, column):
        own_block, own_column = y_bit == block, x_bit == column
        return [
            jnp.where(
                own_column,
                jnp.where(own_block, upper[0], upper[1]),
                jnp.where(own_block, upper_far[0], upper_far[1]),
            ),
            jnp.where(
                own_block,
                jnp.where(own_column, lower[0], lower[1]),
                jnp.where(own_column, lower_far[0], lower_far[1]),
            ),
        ]

    return jnp.concatenate(
        [jnp.concatenate(at(0, column) + at(1, column), 0) for column in range(2)], 1
    )


def split(value):
    high = value.astype(jnp.bfloat16)
    return high, (value - high.astype(jnp.float32)).astype(jnp.bfloat16)


def scale_rows(value, mask_ref, slot, first_block, count):
    rows = value.shape[0] // count
    return jnp.concatenate(
        [
            value[k * rows : (k + 1) * rows] * mask_ref[slot, first_block + k].astype(jnp.float32)
            for k in range(count)
        ],
        0,
    )


def forward_kernel(slot, place, tiles, mask_blocks, bit_ref, mask_ref, panel_ref, near_ref, far_ref, *refs):
    prev, (out_first, out_last, high, low) = refs[:-4], refs[-4:]
    turn, step = pl.program_id(0), pl.program_id(1)
    columns = near_ref.shape[1]

    @pl.when((turn == 0) & (step == 0))
    def _():
        for k, ref in enumerate((near_ref, far_ref)):
            part = split(ref[...])
            high[:, k * columns : (k + 1) * columns] = part[0]
            low[:, k * columns : (k + 1) * columns] = part[1]

    panel_high, panel_low = split(panel_ref[...])

    def dot(left, right):
        return jnp.dot(left, right, preferred_element_type=jnp.float32)

    result = dot(panel_high, high[...]) + (dot(panel_high, low[...]) + dot(panel_low, high[...]))
    block = jnp.where(turn == 0, 1 - bit_ref[0], bit_ref[0])
    tile = (2 * block + place) * tiles + step
    result = scale_rows(result, mask_ref, slot, tile * mask_blocks, mask_blocks)
    near, far = result[:, :columns], result[:, columns:]
    if place == 0:
        out_first[...] = near + prev[0][...] if prev else near
        out_last[...] = far + prev[1][...] if prev else far
    else:

        @pl.when(turn == 0)
        def _():
            out_first[0] = near + prev[0][0] if prev else near
            out_first[1] = far + prev[0][1] if prev else far

        @pl.when(turn == 1)
        def _():
            out_last[0] = near + prev[1][0] if prev else near
            out_last[1] = far + prev[1][1] if prev else far


def panel_forward(panel_anc, mask, slot, place, y_bit, near, far, prev=(), tile_rows=256):
    rows_local, width = panel_anc.shape[2:]
    quarter = rows_local // 4
    tiles = quarter // tile_rows
    columns = near.shape[1]
    mask_blocks = mask.shape[1] // (4 * tiles)

    def panel_index(turn, step, bit_ref, mask_ref):
        block = jnp.where(turn == 0, 1 - bit_ref[0], bit_ref[0])
        return (0, slot, (2 * block + place) * tiles + step, 0)

    whole = pl.BlockSpec(near.shape, lambda *_: (0, 0))
    if place == 0:
        out_specs = [
            pl.BlockSpec((None, tile_rows, columns), lambda turn, step, *_: (turn, step, 0))
        ] * 2
    else:
        out_specs = [
            pl.BlockSpec(
                (2, tile_rows, columns),
                lambda turn, step, *_: (0, jnp.where(turn == 0, step, tiles - 1), 0),
            ),
            pl.BlockSpec(
                (2, tile_rows, columns), lambda turn, step, *_: (0, jnp.where(turn == 0, 0, step), 0)
            ),
        ]
    shape = jax.ShapeDtypeStruct((2, quarter, columns), jnp.float32)
    return pl.pallas_call(
        functools.partial(forward_kernel, slot, place, tiles, mask_blocks),
        out_shape=[shape, shape],
        grid_spec=pltpu.PrefetchScalarGridSpec(
            num_scalar_prefetch=2,
            grid=(2, tiles),
            in_specs=[
                pl.BlockSpec((None, None, tile_rows, width), panel_index),
                whole,
                whole,
                *(out_specs if prev else []),
            ],
            out_specs=out_specs,
            scratch_shapes=[pltpu.VMEM((width, 2 * columns), jnp.bfloat16)] * 2,
        ),
        cost_estimate=pl.CostEstimate(
            flops=12 * quarter * width * 2 * columns,
            bytes_accessed=4 * (2 * quarter * width + 2 * width * columns + 4 * quarter * columns),
            transcendentals=0,
        ),
        name=f"panel_forward_{slot}_{place}",
    )(y_bit.reshape(1).astype(jnp.int32), mask, panel_anc, near, far, *prev)


def backward_kernel(slot, tiles, mask_blocks, bit_ref, mask_ref, panel_ref, upper_near, upper_far, lower_near, lower_far, out_near, out_far, panel_parts, value_parts, total):
    place, turn, step = pl.program_id(0), pl.program_id(1), pl.program_id(2)
    rows = panel_ref.shape[0]
    columns = out_near.shape[1]
    block = jnp.where(turn == 0, bit_ref[0], 1 - bit_ref[0])
    tile = (2 * block + place) * tiles + step

    def put(near, far):
        for k, value in enumerate((near, far)):
            value = scale_rows(value, mask_ref, slot, tile * mask_blocks, mask_blocks)
            high, low = split(value)
            span = slice(k * columns, (k + 1) * columns)
            value_parts[0:rows, span] = high
            value_parts[rows : 2 * rows, span] = high
            value_parts[2 * rows : 3 * rows, span] = low

    @pl.when(place == 0)
    def _():
        put(upper_near[...], upper_far[...])

    @pl.when((place == 1) & (turn == 0))
    def _():
        put(lower_near[0], lower_near[1])

    @pl.when((place == 1) & (turn == 1))
    def _():
        put(lower_far[0], lower_far[1])

    high, low = split(panel_ref[...])
    panel_parts[0:rows] = high
    panel_parts[rows : 2 * rows] = low
    panel_parts[2 * rows : 3 * rows] = high
    result = lax.dot_general(
        panel_parts[...], value_parts[...], (((0,), (0,)), ((), ())), preferred_element_type=jnp.float32
    )
    start = (place == 0) & (turn == 0) & (step == 0)
    end = (place == 1) & (turn == 1) & (step == tiles - 1)

    @pl.when(start)
    def _():
        total[...] = result

    @pl.when(jnp.logical_not(start))
    def _():
        total[...] += result

    @pl.when(end)
    def _():
        out_near[...] = total[:, :columns]
        out_far[...] = total[:, columns:]


def panel_backward(panel_anc, mask, slot, y_bit, pieces, tile_rows=256):
    upper_near, upper_far, lower_near, lower_far = pieces
    rows_local, width = panel_anc.shape[2:]
    quarter = rows_local // 4
    tiles = quarter // tile_rows
    columns = upper_near.shape[2]
    mask_blocks = mask.shape[1] // (4 * tiles)

    def panel_index(place, turn, step, bit_ref, mask_ref):
        block = jnp.where(turn == 0, bit_ref[0], 1 - bit_ref[0])
        return (0, slot, (2 * block + place) * tiles + step, 0)

    def upper_index(place, turn, step, *_):
        return (jnp.where(place == 0, turn, 1), jnp.where(place == 0, step, tiles - 1), 0)

    def lower_index(mine):
        def index(place, turn, step, *_):
            before = (place == 0) | (turn < mine)
            after = (place == 1) & (turn > mine)
            return (0, jnp.where(before, 0, jnp.where(after, tiles - 1, step)), 0)

        return index

    out_spec = pl.BlockSpec((width, columns), lambda *_: (0, 0))
    shape = jax.ShapeDtypeStruct((width, columns), jnp.float32)
    return pl.pallas_call(
        functools.partial(backward_kernel, slot, tiles, mask_blocks),
        out_shape=[shape, shape],
        grid_spec=pltpu.PrefetchScalarGridSpec(
            num_scalar_prefetch=2,
            grid=(2, 2, tiles),
            in_specs=[
                pl.BlockSpec((None, None, tile_rows, width), panel_index),
                pl.BlockSpec((None, tile_rows, columns), upper_index),
                pl.BlockSpec((None, tile_rows, columns), upper_index),
                pl.BlockSpec((2, tile_rows, columns), lower_index(0)),
                pl.BlockSpec((2, tile_rows, columns), lower_index(1)),
            ],
            out_specs=[out_spec, out_spec],
            scratch_shapes=[
                pltpu.VMEM((3 * tile_rows, width), jnp.bfloat16),
                pltpu.VMEM((3 * tile_rows, 2 * columns), jnp.bfloat16),
                pltpu.VMEM((width, 2 * columns), jnp.float32),
            ],
        ),
        cost_estimate=pl.CostEstimate(
            flops=6 * rows_local * width * 2 * columns,
            bytes_accessed=4 * (rows_local * width + 2 * rows_local * columns + 2 * width * columns),
            transcendentals=0,
        ),
        name=f"panel_backward_{slot}",
    )(y_bit.reshape(1).astype(jnp.int32), mask, panel_anc, upper_near, upper_far, lower_near, lower_far)


def from_partner(value, axis, bit):
    mask = 2**bit
    pairs = [(source, source ^ mask) for source in range(lax.axis_size(axis))]
    return lax.ppermute(value, axis, pairs)


def ancestor_solve(inverse_rows, values):
    rows_local, width = inverse_rows.shape
    if rows_local >= width:
        blocks = inverse_rows.reshape(rows_local // width, width, width)
        grouped = values.reshape(rows_local // width, width, values.shape[1])
        forward = jnp.einsum("kij,kjr->kir", blocks, grouped, precision=PRECISION)
        result = jnp.einsum("kji,kjr->kir", blocks, forward, precision=PRECISION)
        return result.reshape(rows_local, values.shape[1])
    row_index = lax.axis_index("row")
    levels = (width // rows_local).bit_length() - 1
    whole = values
    for bit_number in range(levels):
        other = from_partner(whole, "row", bit_number)
        upper = row_index >> bit_number & 1
        whole = jnp.where(
            upper == 1, jnp.concatenate([other, whole], 0), jnp.concatenate([whole, other], 0)
        )
    forward = product(inverse_rows, whole)
    partial_value = transposed(inverse_rows, forward)
    for bit_number in reversed(range(levels)):
        half = partial_value.shape[0] // 2
        upper = row_index >> bit_number & 1
        keep = jnp.where(upper == 1, partial_value[half:], partial_value[:half])
        outgoing = jnp.where(upper == 1, partial_value[:half], partial_value[half:])
        partial_value = keep + from_partner(outgoing, "row", bit_number)
    return partial_value


def per_device(rhs_sub, rhs_anc, inv_sub, panel_mid, panel_anc, block_mask, inv_anc):
    rhs_local = rhs_sub[0]
    rows_local = panel_anc.shape[2]
    width = panel_anc.shape[3]
    rows_own = rhs_local.shape[1]
    columns = rhs_local.shape[2]
    block_count = block_mask.shape[2]
    row_index = lax.axis_index("row")
    core = row_index % 2
    leaf = lax.axis_index("leaf")
    x_bit, y_bit = leaf % 2, leaf // 2
    paired = lax.axis_size("leaf") == 4 and rows_local == 2 * width
    mask = block_mask[0].astype(jnp.float32)
    half = columns // 2

    def masked(slot, value):
        blocks = value.reshape(block_count, rows_local // block_count, value.shape[1])
        return (blocks * mask[slot][:, None, None]).reshape(value.shape)

    def halves(value):
        return jnp.where(core == 0, value[..., :half], value[..., half:])

    def other_half(value):
        return jnp.where(core == 0, value[..., half:], value[..., :half])

    rhs_chip = by_core(core, halves(rhs_local), core_swap(other_half(rhs_local)), 1)
    inverses = inv_sub[0]
    inverses_other, middle_other = core_swap(inverses), core_swap(panel_mid[0])
    inverse_first = by_core(core, inverses[0], inverses_other[0], 0)
    inverse_second = by_core(core, inverses[1], inverses_other[1], 0)
    middle = by_core(core, panel_mid[0], middle_other, 0)

    def both_halves(value):
        return by_core(core, value, core_swap(value), 1)

    def near_and_far(value):
        swapped = core_swap(value)
        far_is_mine = core == x_bit
        return jnp.where(far_is_mine, swapped, value), jnp.where(far_is_mine, value, swapped)

    block_mask = block_mask[0]
    gathered, inverse_first = gather_rows(rhs_chip[0], lower=True, filler=inverse_first)
    first = product(inverse_first, gathered)
    first_all, (middle, inverse_second) = gather_rows(first, filler=(middle, inverse_second))
    residual = rhs_chip[1] - product(middle, first_all)
    if paired:
        sides = near_and_far(first_all)
        upper = panel_forward(panel_anc, block_mask, 0, 0, y_bit, *sides)
        lower = panel_forward(panel_anc, block_mask, 0, 1, y_bit, *sides)
        gathered, upper = gather_rows(residual, lower=True, filler=upper)
        second = product(inverse_second, gathered)
        second_all, lower = gather_rows(second, filler=lower)
        sides = near_and_far(second_all)
        upper = panel_forward(panel_anc, block_mask, 1, 0, y_bit, *sides, upper)
        lower = panel_forward(panel_anc, block_mask, 1, 1, y_bit, *sides, lower)
    else:
        gathered, _ = gather_rows(residual, lower=True)
        second = product(inverse_second, gathered)
        update = masked(0, product(panel_anc[0, 0], both_halves(first_all)))
        second_all, _ = gather_rows(second)
        update = update + masked(1, product(panel_anc[0, 1], both_halves(second_all)))

    *inner_digits, (size, stride) = row_digits()
    inverses, second_all, first_all = lax.optimization_barrier((inverses, second_all, first_all))
    block = inverses
    for inner_size, inner_stride in inner_digits:
        block = jnp.concatenate(gather_join(block, *gather_both(block, inner_size, inner_stride), inner_size, inner_stride), 1)
    received = gather_near(block, size, stride)

    def whole_inverses(received, passed):
        mine = jnp.stack(gather_join(block, received, passed, size, stride), 1)
        mine = mine.reshape(2, width // (2 * rows_own), 1, rows_own, width)
        other = core_swap(mine)
        both = by_core(core, mine, other, 2).reshape(2, width, width)
        return [sending_order(both[slot], size, stride, 1) for slot in range(2)]

    if paired:
        inverse_anc = jnp.where(y_bit == 0, inv_anc[:width], inv_anc[width:])
        own = jnp.where(y_bit == 0, rhs_anc[:width], rhs_anc[width:])
        own = jnp.where(x_bit == 0, own[:, :half], own[:, half:])
        total, received = leaf_reduce(upper, lower, received)
        passed = gather_far(received, size, stride)
        total, inverse_anc = lax.optimization_barrier((own - total, inverse_anc))
        forward = lax.optimization_barrier(product(inverse_anc, total))
        solved = row_major(transposed(inverse_anc, forward))
        pieces, passed = leaf_gather(solved, passed)
        whole_first, whole_second = whole_inverses(received, passed)
        x_anc = in_order(pieces, x_bit, y_bit)
    else:
        whole_first, whole_second = whole_inverses(received, gather_far(received, size, stride))
        total = lax.psum_scatter(update, "leaf", scatter_dimension=1, tiled=True)
        share = total.shape[1]
        own = lax.dynamic_slice_in_dim(rhs_anc, leaf * share, share, 1)
        x_anc = lax.all_gather(ancestor_solve(inv_anc, own - total), "leaf", axis=1, tiled=True)
        pieces = x_anc

    def chip_sum(slot, pieces):
        if paired:
            mine, other = panel_backward(panel_anc, block_mask, slot, y_bit, pieces)
            straight = x_bit == core
            keep, send = jnp.where(straight, mine, other), jnp.where(straight, other, mine)
        else:
            keep, send = (
                transposed(panel_anc[0, slot], masked(slot, part))
                for part in (halves(pieces), other_half(pieces))
            )
        return lax.optimization_barrier(keep + core_swap(send))

    rows_chip = 2 * rows_own

    def own_rows(matrix, value):
        if inner_digits:
            own = lax.dynamic_slice_in_dim(matrix, row_index // 2 % (width // rows_chip // size) * rows_chip + (size - 1) * (width // size), rows_chip, 1)
        else:
            own = matrix[:, width - rows_chip :]
        return transposed(own, value)

    second_base = own_rows(whole_second, second_all)
    first_base = own_rows(whole_first, first_all)
    middle_first = product(middle, whole_first)

    second_partial = transposed(whole_second, chip_sum(1, pieces))
    second_partial, pieces = lax.optimization_barrier((second_partial, pieces))
    first_part = transposed(whole_first, chip_sum(0, pieces))
    second_total, first_part = reduce_rows(second_partial, filler=first_part)
    x_second = second_base - second_total
    first_total, x_anc = reduce_rows(first_part + transposed(middle_first, x_second), filler=x_anc)
    x_first = first_base - first_total

    both = jnp.stack([x_first, x_second])
    keep = jnp.where(core == 0, both[:, :rows_own], both[:, rows_own:])
    send = jnp.where(core == 0, both[:, rows_own:], both[:, :rows_own])
    x_sub = by_core(core, keep, core_swap(send), 2)
    return x_sub[None], x_anc


def solution(mesh):
    return jax.shard_map(
        per_device,
        mesh=mesh,
        in_specs=(
            P("leaf", None, "row", None),
            P("row", None),
            P("leaf", None, "row", None),
            P("leaf", "row", None),
            P("leaf", None, "row", None),
            P("leaf", None, "row"),
            P("row", None),
        ),
        out_specs=(P("leaf", None, "row", None), P("row", None)),
        check_vma=False,
    )
```

```python
import functools

import jax
import jax.numpy as jnp
from jax import lax
from jax.experimental import pallas as pl
from jax.experimental.layout import Layout, with_layout_constraint
from jax.experimental.pallas import tpu as pltpu
from jax.sharding import PartitionSpec as P


PRECISION = lax.Precision.HIGH


def product(left, right):
    return jnp.dot(left, right, precision=PRECISION, preferred_element_type=jnp.float32)


def transposed(left, right):
    return lax.dot_general(
        left,
        right,
        (((0,), (0,)), ((), ())),
        precision=PRECISION,
        preferred_element_type=jnp.float32,
    )


def row_major(value):
    return with_layout_constraint(value, Layout(tuple(range(value.ndim))))


def core_swap(value):
    count = lax.axis_size("row")
    return lax.ppermute(value, "row", [(r, r ^ 1) for r in range(count)])


def leaf_swap(value, mask):
    count = lax.axis_size("leaf")
    return lax.ppermute(value, "leaf", [(g, g ^ mask) for g in range(count)])


def chip_digits(chips):
    digits, stride = [], 1
    while chips > 1:
        size = 4 if chips % 4 == 0 else 2
        digits.append((size, stride))
        stride *= size
        chips //= size
    return digits


def digit_permute(value, size, stride, moves):
    target = dict(moves)
    pairs = []
    for r in range(lax.axis_size("row")):
        digit = (r // 2) // stride % size
        if digit in target:
            pairs.append((r, r + 2 * stride * (target[digit] - digit)))
    return lax.ppermute(value, "row", pairs)


def digit_index(size, stride):
    return lax.axis_index("row") // 2 // stride % size


def after(values, filler):
    return lax.optimization_barrier((*values, filler))


def gather_near(value, size, stride, lower=False):
    def moves(pairs):
        return [(a, b) for a, b in pairs if a < b] if lower else pairs

    if size == 2:
        return (digit_permute(value, size, stride, moves([(0, 1), (1, 0)])),)
    near = digit_permute(value, size, stride, moves([(0, 1), (1, 0), (2, 3), (3, 2)]))
    inner = digit_permute(value, size, stride, moves([(1, 2), (2, 1)]))
    return near, inner


def gather_far(received, size, stride, lower=False):
    def moves(pairs):
        return [(a, b) for a, b in pairs if a < b] if lower else pairs

    if size == 2:
        return ()
    near, inner = received
    relay = digit_permute(near, size, stride, moves([(1, 2), (2, 1)]))
    far = digit_permute(near, size, stride, moves([(1, 3), (2, 0)]))
    outer = digit_permute(inner, size, stride, moves([(1, 0), (2, 3)]))
    return relay, far, outer


def gather_join(value, received, passed, size, stride):
    me = digit_index(size, stride)
    if size == 2:
        (near,) = received
        return [jnp.where(me == 0, value, near), jnp.where(me == 0, near, value)]
    near, inner = received
    relay, far, outer = passed
    middle = (me == 1) | (me == 2)
    third = jnp.where(middle, inner, outer)
    fourth = jnp.where(middle, relay, far)
    odd = me % 2 == 1
    even_one = jnp.where(odd, near, value)
    odd_one = jnp.where(odd, value, near)
    high = me >= 2
    return [
        jnp.where(high, fourth, even_one),
        jnp.where(high, third, odd_one),
        jnp.where(high, even_one, third),
        jnp.where(high, odd_one, fourth),
    ]


def gather_both(value, size, stride):
    received = gather_near(value, size, stride)
    return received, gather_far(received, size, stride)


def gather_digit(value, size, stride, lower, filler):
    received = gather_near(value, size, stride, lower)
    passed = gather_far(received, size, stride, lower)
    last, filler = after((passed or received,), filler)
    received, passed = (received, last) if passed else (last, passed)
    return jnp.concatenate(gather_join(value, received, passed, size, stride), 0), filler


def reduce_digit(value, size, stride, lower, filler):
    def moves(pairs):
        return [(a, b) for a, b in pairs if a > b] if lower else pairs

    rows = value.shape[0] // size
    block = [value[k * rows : (k + 1) * rows] for k in range(size)]
    if size == 2:
        other = digit_permute(block[0], size, stride, moves([(0, 1), (1, 0)]))
        other, filler = after((other,), filler)
        return block[1] + other, filler
    far = digit_permute(block[0], size, stride, moves([(3, 1), (0, 2)]))
    relay = digit_permute(block[0], size, stride, moves([(2, 1), (1, 2)]))
    outer = digit_permute(block[1], size, stride, moves([(0, 1), (3, 2)]))
    inner = digit_permute(block[1] + outer, size, stride, moves([(1, 2), (2, 1)]))
    near = digit_permute(block[2] + (far + relay), size, stride, moves([(0, 1), (1, 0), (2, 3), (3, 2)]))
    near, inner, filler = after((near, inner), filler)
    return block[3] + near + inner, filler


def sending_order(value, size, stride, axis):
    length = value.shape[axis] // size
    me = digit_index(size, stride)
    if size == 2:
        order = (1 - me, me)
    else:
        high = me >= 2
        order = (jnp.where(high, 0, 3), jnp.where(high, 1, 2), me ^ 1, me)
    return jnp.concatenate(
        [lax.dynamic_slice_in_dim(value, k * length, length, axis) for k in order], axis
    )


def gather_rows(value, lower=False, filler=()):
    digits = chip_digits(lax.axis_size("row") // 2)
    for place, (size, stride) in enumerate(digits):
        outermost = place == len(digits) - 1
        value, filler = gather_digit(value, size, stride, lower and outermost, filler)
    return value, filler


def row_digits():
    return chip_digits(lax.axis_size("row") // 2)


def reduce_rows(value, lower=False, filler=()):
    digits = row_digits()
    for place, (size, stride) in reversed(list(enumerate(digits))):
        outermost = place == len(digits) - 1
        if not outermost:
            value = sending_order(value, size, stride, 0)
        value, filler = reduce_digit(value, size, stride, lower and outermost, filler)
    return value, filler


def by_core(core, mine, other, axis):
    return jnp.concatenate(
        [jnp.where(core == 0, mine, other), jnp.where(core == 0, other, mine)], axis
    )


def leaf_reduce(upper, lower, side):
    from_x = leaf_swap(upper[0], 1)
    from_y = leaf_swap(lower[0], 2)
    from_x, side = after((from_x,), side)
    from_x, from_y = lax.optimization_barrier((from_x, from_y))
    first, second = upper[1][0] + from_x[0], lower[1][0] + from_y[0]
    first, second = leaf_swap(first, 2), leaf_swap(second, 1)
    first, second = lax.optimization_barrier((first, second))
    return jnp.concatenate(
        [upper[1][1] + from_x[1] + first, lower[1][1] + from_y[1] + second], 0
    ), side


def leaf_gather(piece, side, between):
    rows = piece.shape[0]
    first, second = piece[: rows // 2], piece[rows // 2 :]
    first_y = leaf_swap(first, 2)
    second_x = leaf_swap(second, 1)
    first_y, second_x = lax.optimization_barrier((first_y, second_x))
    upper = jnp.stack([first, first_y])
    lower = jnp.stack([second, second_x])
    upper_far = leaf_swap(upper, 1)
    lower_far = leaf_swap(lower, 2)
    work = between(upper, lower)
    upper_far, lower_far, work, side = lax.optimization_barrier((upper_far, lower_far, work, side))
    return (upper, upper_far, lower, lower_far), work, side


def in_order(pieces, x_bit, y_bit):
    upper, upper_far, lower, lower_far = pieces

    def at(block, column):
        own_block, own_column = y_bit == block, x_bit == column
        return [
            jnp.where(
                own_column,
                jnp.where(own_block, upper[0], upper[1]),
                jnp.where(own_block, upper_far[0], upper_far[1]),
            ),
            jnp.where(
                own_block,
                jnp.where(own_column, lower[0], lower[1]),
                jnp.where(own_column, lower_far[0], lower_far[1]),
            ),
        ]

    return jnp.concatenate(
        [jnp.concatenate(at(0, column) + at(1, column), 0) for column in range(2)], 1
    )


def split(value):
    high = value.astype(jnp.bfloat16)
    return high, (value - high.astype(jnp.float32)).astype(jnp.bfloat16)


def scale_rows(value, mask_ref, slot, first_block, count):
    rows = value.shape[0] // count
    return jnp.concatenate(
        [
            value[k * rows : (k + 1) * rows] * mask_ref[slot, first_block + k].astype(jnp.float32)
            for k in range(count)
        ],
        0,
    )


def forward_kernel(slot, place, tiles, mask_blocks, bit_ref, mask_ref, panel_ref, near_ref, far_ref, *refs):
    prev, (out_first, out_last, high, low) = refs[:-4], refs[-4:]
    turn, step = pl.program_id(0), pl.program_id(1)
    columns = near_ref.shape[1]

    @pl.when((turn == 0) & (step == 0))
    def _():
        for k, ref in enumerate((near_ref, far_ref)):
            part = split(ref[...])
            high[:, k * columns : (k + 1) * columns] = part[0]
            low[:, k * columns : (k + 1) * columns] = part[1]

    panel_high, panel_low = split(panel_ref[...])

    def dot(left, right):
        return jnp.dot(left, right, preferred_element_type=jnp.float32)

    result = dot(panel_high, high[...]) + (dot(panel_high, low[...]) + dot(panel_low, high[...]))
    block = jnp.where(turn == 0, 1 - bit_ref[0], bit_ref[0])
    tile = (2 * block + place) * tiles + step
    result = scale_rows(result, mask_ref, slot, tile * mask_blocks, mask_blocks)
    near, far = result[:, :columns], result[:, columns:]
    if place == 0:
        out_first[...] = near + prev[0][...] if prev else near
        out_last[...] = far + prev[1][...] if prev else far
    else:

        @pl.when(turn == 0)
        def _():
            out_first[0] = near + prev[0][0] if prev else near
            out_first[1] = far + prev[0][1] if prev else far

        @pl.when(turn == 1)
        def _():
            out_last[0] = near + prev[1][0] if prev else near
            out_last[1] = far + prev[1][1] if prev else far


def panel_forward(panel_anc, mask, slot, place, y_bit, near, far, prev=(), tile_rows=256):
    rows_local, width = panel_anc.shape[2:]
    quarter = rows_local // 4
    tiles = quarter // tile_rows
    columns = near.shape[1]
    mask_blocks = mask.shape[1] // (4 * tiles)

    def panel_index(turn, step, bit_ref, mask_ref):
        block = jnp.where(turn == 0, 1 - bit_ref[0], bit_ref[0])
        return (0, slot, (2 * block + place) * tiles + step, 0)

    whole = pl.BlockSpec(near.shape, lambda *_: (0, 0))
    if place == 0:
        out_specs = [
            pl.BlockSpec((None, tile_rows, columns), lambda turn, step, *_: (turn, step, 0))
        ] * 2
    else:
        out_specs = [
            pl.BlockSpec(
                (2, tile_rows, columns),
                lambda turn, step, *_: (0, jnp.where(turn == 0, step, tiles - 1), 0),
            ),
            pl.BlockSpec(
                (2, tile_rows, columns), lambda turn, step, *_: (0, jnp.where(turn == 0, 0, step), 0)
            ),
        ]
    shape = jax.ShapeDtypeStruct((2, quarter, columns), jnp.float32)
    return pl.pallas_call(
        functools.partial(forward_kernel, slot, place, tiles, mask_blocks),
        out_shape=[shape, shape],
        grid_spec=pltpu.PrefetchScalarGridSpec(
            num_scalar_prefetch=2,
            grid=(2, tiles),
            in_specs=[
                pl.BlockSpec((None, None, tile_rows, width), panel_index),
                whole,
                whole,
                *(out_specs if prev else []),
            ],
            out_specs=out_specs,
            scratch_shapes=[pltpu.VMEM((width, 2 * columns), jnp.bfloat16)] * 2,
        ),
        cost_estimate=pl.CostEstimate(
            flops=12 * quarter * width * 2 * columns,
            bytes_accessed=4 * (2 * quarter * width + 2 * width * columns + 4 * quarter * columns),
            transcendentals=0,
        ),
    )(y_bit.reshape(1).astype(jnp.int32), mask, panel_anc, near, far, *prev)


def backward_kernel(slot, side, mask_blocks, bit_ref, mask_ref, panel_ref, upper_ref, lower_ref, *refs):
    prev, (out_first, out_last, panel_parts, value_parts, total) = refs[:-5], refs[-5:]
    phase = pl.program_id(0)
    rows = panel_ref.shape[0]
    columns = upper_ref.shape[2]
    tile = backward_tile(side, phase, bit_ref)

    def put(index, value):
        value = scale_rows(value, mask_ref, slot, tile * mask_blocks, mask_blocks)
        high, low = split(value)
        span = slice(index * columns, (index + 1) * columns)
        value_parts[0:rows, span] = high
        value_parts[rows : 2 * rows, span] = high
        value_parts[2 * rows : 3 * rows, span] = low

    high, low = split(panel_ref[...])
    panel_parts[0:rows] = high
    panel_parts[rows : 2 * rows] = low
    panel_parts[2 * rows : 3 * rows] = high

    def dot(right):
        return lax.dot_general(
            panel_parts[...], right, (((0,), (0,)), ((), ())), preferred_element_type=jnp.float32
        )

    near, far = slice(0, columns), slice(columns, 2 * columns)
    here, there = (near, far) if side == 0 else (far, near)

    @pl.when(phase == 0)
    def _():
        put(0, upper_ref[0])
        result = dot(value_parts[:, near])
        if prev:
            total[:, here] = prev[side][...] + result
            total[:, there] = prev[1 - side][...]
        else:
            total[:, here] = result
            total[:, there] = jnp.zeros_like(result)

    @pl.when(phase == 1)
    def _():
        put(0, upper_ref[0])
        total[:, here] += dot(value_parts[:, near])

    @pl.when(phase == 2)
    def _():
        put(0, lower_ref[0])
        put(1, lower_ref[1])
        total[...] += dot(value_parts[...])
        if side == 0:
            out_first[...] = total[:, near]
            out_last[...] = total[:, far]
        else:

            @pl.when(bit_ref[1] == 1)
            def _():
                out_first[...] = total[:, near]
                out_last[...] = total[:, far]

            @pl.when(bit_ref[1] == 0)
            def _():
                out_first[...] = total[:, far]
                out_last[...] = total[:, near]


def backward_tile(side, phase, bit_ref):
    own, other = bit_ref[0], 1 - bit_ref[0]
    lower = 2 * (own if side == 0 else other) + 1
    return jnp.where(phase == 0, 2 * own, jnp.where(phase == 1, 2 * other, lower))


def panel_backward(panel_anc, mask, slot, side, bits, upper, lower, prev=()):
    rows_local, width = panel_anc.shape[2:]
    quarter = rows_local // 4
    columns = upper.shape[2]
    mask_blocks = mask.shape[1] // 4

    def panel_index(phase, bit_ref, mask_ref):
        return (0, slot, backward_tile(side, phase, bit_ref), 0)

    out_spec = pl.BlockSpec((width, columns), lambda *_: (0, 0))
    shape = jax.ShapeDtypeStruct((width, columns), jnp.float32)
    return pl.pallas_call(
        functools.partial(backward_kernel, slot, side, mask_blocks),
        out_shape=[shape, shape],
        grid_spec=pltpu.PrefetchScalarGridSpec(
            num_scalar_prefetch=2,
            grid=(3,),
            in_specs=[
                pl.BlockSpec((None, None, quarter, width), panel_index),
                pl.BlockSpec((1, quarter, columns), lambda phase, *_: (jnp.minimum(phase, 1), 0, 0)),
                pl.BlockSpec((2, quarter, columns), lambda *_: (0, 0, 0)),
                *[out_spec for _ in prev],
            ],
            out_specs=[out_spec, out_spec],
            scratch_shapes=[
                pltpu.VMEM((3 * quarter, width), jnp.bfloat16),
                pltpu.VMEM((3 * quarter, 2 * columns), jnp.bfloat16),
                pltpu.VMEM((width, 2 * columns), jnp.float32),
            ],
        ),
        cost_estimate=pl.CostEstimate(
            flops=6 * 4 * quarter * width * columns,
            bytes_accessed=4 * (3 * quarter * width + 4 * quarter * columns + 4 * width * columns),
            transcendentals=0,
        ),
    )(bits, mask, panel_anc, upper, lower, *prev)


def from_partner(value, axis, bit):
    mask = 2**bit
    pairs = [(source, source ^ mask) for source in range(lax.axis_size(axis))]
    return lax.ppermute(value, axis, pairs)


def ancestor_solve(inverse_rows, values):
    rows_local, width = inverse_rows.shape
    if rows_local >= width:
        blocks = inverse_rows.reshape(rows_local // width, width, width)
        grouped = values.reshape(rows_local // width, width, values.shape[1])
        forward = jnp.einsum("kij,kjr->kir", blocks, grouped, precision=PRECISION)
        result = jnp.einsum("kji,kjr->kir", blocks, forward, precision=PRECISION)
        return result.reshape(rows_local, values.shape[1])
    row_index = lax.axis_index("row")
    levels = (width // rows_local).bit_length() - 1
    whole = values
    for bit_number in range(levels):
        other = from_partner(whole, "row", bit_number)
        upper = row_index >> bit_number & 1
        whole = jnp.where(
            upper == 1, jnp.concatenate([other, whole], 0), jnp.concatenate([whole, other], 0)
        )
    forward = product(inverse_rows, whole)
    partial_value = transposed(inverse_rows, forward)
    for bit_number in reversed(range(levels)):
        half = partial_value.shape[0] // 2
        upper = row_index >> bit_number & 1
        keep = jnp.where(upper == 1, partial_value[half:], partial_value[:half])
        outgoing = jnp.where(upper == 1, partial_value[:half], partial_value[half:])
        partial_value = keep + from_partner(outgoing, "row", bit_number)
    return partial_value


def solve(rhs_sub, rhs_anc, inv_sub, panel_mid, panel_anc, block_mask, inv_anc):
    rhs_local = rhs_sub[0]
    rows_local = panel_anc.shape[2]
    width = panel_anc.shape[3]
    rows_own = rhs_local.shape[1]
    columns = rhs_local.shape[2]
    block_count = block_mask.shape[2]
    row_index = lax.axis_index("row")
    core = row_index % 2
    leaf = lax.axis_index("leaf")
    x_bit, y_bit = leaf % 2, leaf // 2
    paired = lax.axis_size("leaf") == 4 and rows_local == 2 * width
    mask = block_mask[0].astype(jnp.float32)
    half = columns // 2

    def masked(slot, value):
        blocks = value.reshape(block_count, rows_local // block_count, value.shape[1])
        return (blocks * mask[slot][:, None, None]).reshape(value.shape)

    def halves(value):
        return jnp.where(core == 0, value[..., :half], value[..., half:])

    def other_half(value):
        return jnp.where(core == 0, value[..., half:], value[..., :half])

    rhs_chip = by_core(core, halves(rhs_local), core_swap(other_half(rhs_local)), 1)
    inverses = inv_sub[0]
    inverses_other, middle_other = core_swap(inverses), core_swap(panel_mid[0])
    inverse_first = by_core(core, inverses[0], inverses_other[0], 0)
    inverse_second = by_core(core, inverses[1], inverses_other[1], 0)
    middle = by_core(core, panel_mid[0], middle_other, 0)

    def both_halves(value):
        return by_core(core, value, core_swap(value), 1)

    def near_and_far(value):
        swapped = core_swap(value)
        far_is_mine = core == x_bit
        return jnp.where(far_is_mine, swapped, value), jnp.where(far_is_mine, value, swapped)

    block_mask = block_mask[0]
    gathered, inverse_first = gather_rows(rhs_chip[0], lower=True, filler=inverse_first)
    first = product(inverse_first, gathered)
    first_all, (middle, inverse_second) = gather_rows(first, filler=(middle, inverse_second))
    residual = rhs_chip[1] - product(middle, first_all)
    if paired:
        sides = near_and_far(first_all)
        upper = panel_forward(panel_anc, block_mask, 0, 0, y_bit, *sides)
        lower = panel_forward(panel_anc, block_mask, 0, 1, y_bit, *sides)
        gathered, upper = gather_rows(residual, lower=True, filler=upper)
        second = product(inverse_second, gathered)
        second_all, lower = gather_rows(second, filler=lower)
        sides = near_and_far(second_all)
        upper = panel_forward(panel_anc, block_mask, 1, 0, y_bit, *sides, upper)
        lower = panel_forward(panel_anc, block_mask, 1, 1, y_bit, *sides, lower)
    else:
        gathered, _ = gather_rows(residual, lower=True)
        second = product(inverse_second, gathered)
        update = masked(0, product(panel_anc[0, 0], both_halves(first_all)))
        second_all, _ = gather_rows(second)
        update = update + masked(1, product(panel_anc[0, 1], both_halves(second_all)))

    *inner_digits, (size, stride) = row_digits()
    inverses, second_all, first_all = lax.optimization_barrier((inverses, second_all, first_all))
    block = inverses
    for inner_size, inner_stride in inner_digits:
        block = jnp.concatenate(gather_join(block, *gather_both(block, inner_size, inner_stride), inner_size, inner_stride), 1)
    received = gather_near(block, size, stride)

    def whole_inverses(received, passed):
        mine = jnp.stack(gather_join(block, received, passed, size, stride), 1)
        mine = mine.reshape(2, width // (2 * rows_own), 1, rows_own, width)
        other = core_swap(mine)
        both = by_core(core, mine, other, 2).reshape(2, width, width)
        return [sending_order(both[slot], size, stride, 1) for slot in range(2)]

    if paired:
        inverse_anc = jnp.where(y_bit == 0, inv_anc[:width], inv_anc[width:])
        own = jnp.where(y_bit == 0, rhs_anc[:width], rhs_anc[width:])
        own = jnp.where(x_bit == 0, own[:, :half], own[:, half:])
        total, received = leaf_reduce(upper, lower, received)
        passed = gather_far(received, size, stride)
        total, inverse_anc = lax.optimization_barrier((own - total, inverse_anc))
        forward = lax.optimization_barrier(product(inverse_anc, total))
        solved = row_major(transposed(inverse_anc, forward))
        bits = jnp.stack([y_bit, (x_bit == core).astype(jnp.int32)]).astype(jnp.int32)

        def begun(upper, lower):
            sums = []
            for slot in range(2):
                sums.append(panel_backward(panel_anc, block_mask, slot, 0, bits, upper, lower))
            return sums

        pieces, sums, passed = leaf_gather(solved, passed, begun)
        whole_first, whole_second = whole_inverses(received, passed)
        x_anc = in_order(pieces, x_bit, y_bit)
    else:
        whole_first, whole_second = whole_inverses(received, gather_far(received, size, stride))
        total = lax.psum_scatter(update, "leaf", scatter_dimension=1, tiled=True)
        share = total.shape[1]
        own = lax.dynamic_slice_in_dim(rhs_anc, leaf * share, share, 1)
        x_anc = lax.all_gather(ancestor_solve(inv_anc, own - total), "leaf", axis=1, tiled=True)
        pieces = x_anc

    def chip_sum(slot, pieces):
        if paired:
            keep, send = panel_backward(
                panel_anc, block_mask, slot, 1, bits, pieces[1], pieces[3], sums[slot]
            )
        else:
            keep, send = (
                transposed(panel_anc[0, slot], masked(slot, part))
                for part in (halves(pieces), other_half(pieces))
            )
        return lax.optimization_barrier(keep + core_swap(send))

    rows_chip = 2 * rows_own

    def own_rows(matrix, value):
        if inner_digits:
            own = lax.dynamic_slice_in_dim(matrix, row_index // 2 % (width // rows_chip // size) * rows_chip + (size - 1) * (width // size), rows_chip, 1)
        else:
            own = matrix[:, width - rows_chip :]
        return transposed(own, value)

    second_base = own_rows(whole_second, second_all)
    first_base = own_rows(whole_first, first_all)
    middle_first = product(middle, whole_first)

    second_partial = transposed(whole_second, chip_sum(1, pieces))
    second_partial, pieces = lax.optimization_barrier((second_partial, pieces))
    first_part = transposed(whole_first, chip_sum(0, pieces))
    second_total, first_part = reduce_rows(second_partial, filler=first_part)
    x_second = second_base - second_total
    first_total, x_anc = reduce_rows(first_part + transposed(middle_first, x_second), filler=x_anc)
    x_first = first_base - first_total

    both = jnp.stack([x_first, x_second])
    keep = jnp.where(core == 0, both[:, :rows_own], both[:, rows_own:])
    send = jnp.where(core == 0, both[:, rows_own:], both[:, :rows_own])
    x_sub = by_core(core, keep, core_swap(send), 2)
    return x_sub[None], x_anc


def solution(mesh):
    return jax.shard_map(
        solve,
        mesh=mesh,
        in_specs=(
            P("leaf", None, "row", None),
            P("row", None),
            P("leaf", None, "row", None),
            P("leaf", "row", None),
            P("leaf", None, "row", None),
            P("leaf", None, "row"),
            P("row", None),
        ),
        out_specs=(P("leaf", None, "row", None), P("row", None)),
        check_vma=False,
    )
```

```python
import functools

import jax
import jax.numpy as jnp
from jax import lax
from jax.experimental import pallas as pl
from jax.experimental.layout import Layout, with_layout_constraint
from jax.experimental.pallas import tpu as pltpu
from jax.sharding import PartitionSpec as P


PRECISION = lax.Precision.HIGH


def product(left, right):
    return jnp.dot(left, right, precision=PRECISION, preferred_element_type=jnp.float32)


def transposed(left, right):
    return lax.dot_general(
        left,
        right,
        (((0,), (0,)), ((), ())),
        precision=PRECISION,
        preferred_element_type=jnp.float32,
    )


def row_major(value):
    return with_layout_constraint(value, Layout(tuple(range(value.ndim))))


def core_swap(value):
    count = lax.axis_size("row")
    return lax.ppermute(value, "row", [(r, r ^ 1) for r in range(count)])


def leaf_swap(value, mask):
    count = lax.axis_size("leaf")
    return lax.ppermute(value, "leaf", [(g, g ^ mask) for g in range(count)])


def chip_digits(chips):
    digits, stride = [], 1
    while chips > 1:
        size = 4 if chips % 4 == 0 else 2
        digits.append((size, stride))
        stride *= size
        chips //= size
    return digits


def digit_permute(value, size, stride, moves):
    target = dict(moves)
    pairs = []
    for r in range(lax.axis_size("row")):
        digit = (r // 2) // stride % size
        if digit in target:
            pairs.append((r, r + 2 * stride * (target[digit] - digit)))
    return lax.ppermute(value, "row", pairs)


def digit_index(size, stride):
    return lax.axis_index("row") // 2 // stride % size


def after(values, filler):
    return lax.optimization_barrier((*values, filler))


def gather_near(value, size, stride, lower=False):
    def moves(pairs):
        return [(a, b) for a, b in pairs if a < b] if lower else pairs

    if size == 2:
        return (digit_permute(value, size, stride, moves([(0, 1), (1, 0)])),)
    near = digit_permute(value, size, stride, moves([(0, 1), (1, 0), (2, 3), (3, 2)]))
    inner = digit_permute(value, size, stride, moves([(1, 2), (2, 1)]))
    return near, inner


def gather_far(received, size, stride, lower=False):
    def moves(pairs):
        return [(a, b) for a, b in pairs if a < b] if lower else pairs

    if size == 2:
        return ()
    near, inner = received
    relay = digit_permute(near, size, stride, moves([(1, 2), (2, 1)]))
    far = digit_permute(near, size, stride, moves([(1, 3), (2, 0)]))
    outer = digit_permute(inner, size, stride, moves([(1, 0), (2, 3)]))
    return relay, far, outer


def gather_join(value, received, passed, size, stride, ordered=True):
    me = digit_index(size, stride)
    if size == 2:
        (near,) = received
        if not ordered:
            return [near, value]
        return [jnp.where(me == 0, value, near), jnp.where(me == 0, near, value)]
    near, inner = received
    relay, far, outer = passed
    middle = (me == 1) | (me == 2)
    third = jnp.where(middle, inner, outer)
    fourth = jnp.where(middle, relay, far)
    odd = me % 2 == 1
    if not ordered:
        return [fourth, third, near, value]
    even_one = jnp.where(odd, near, value)
    odd_one = jnp.where(odd, value, near)
    high = me >= 2
    return [
        jnp.where(high, fourth, even_one),
        jnp.where(high, third, odd_one),
        jnp.where(high, even_one, third),
        jnp.where(high, odd_one, fourth),
    ]


def gather_both(value, size, stride):
    received = gather_near(value, size, stride)
    return received, gather_far(received, size, stride)


def gather_digit(value, size, stride, lower, filler):
    received = gather_near(value, size, stride, lower)
    passed = gather_far(received, size, stride, lower)
    last, filler = after((passed or received,), filler)
    received, passed = (received, last) if passed else (last, passed)
    return jnp.concatenate(gather_join(value, received, passed, size, stride), 0), filler


def block_order(size, stride):
    me = digit_index(size, stride)
    if size == 2:
        return 1 - me, me
    high = me >= 2
    return jnp.where(high, 0, 3), jnp.where(high, 1, 2), me ^ 1, me


def sending_order(value, size, stride):
    rows = value.shape[0] // size
    return [
        lax.dynamic_slice_in_dim(value, k * rows, rows, 0) for k in block_order(size, stride)
    ]


def reduce_digit(value, size, stride, lower, filler):
    def moves(pairs):
        return [(a, b) for a, b in pairs if a > b] if lower else pairs

    block = sending_order(value, size, stride)
    if size == 2:
        other = digit_permute(block[0], size, stride, moves([(0, 1), (1, 0)]))
        other, filler = after((other,), filler)
        return block[1] + other, filler
    far = digit_permute(block[0], size, stride, moves([(3, 1), (0, 2)]))
    relay = digit_permute(block[0], size, stride, moves([(2, 1), (1, 2)]))
    outer = digit_permute(block[1], size, stride, moves([(0, 1), (3, 2)]))
    far, relay, outer = lax.optimization_barrier((far, relay, outer))
    inner = digit_permute(block[1] + outer, size, stride, moves([(1, 2), (2, 1)]))
    near = digit_permute(block[2] + (far + relay), size, stride, moves([(0, 1), (1, 0), (2, 3), (3, 2)]))
    near, inner, filler = after((near, inner), filler)
    return block[3] + near + inner, filler


def gather_rows(value, lower=False, filler=()):
    digits = chip_digits(lax.axis_size("row") // 2)
    for place, (size, stride) in enumerate(digits):
        outermost = place == len(digits) - 1
        value, filler = gather_digit(value, size, stride, lower and outermost, filler)
    return value, filler


def row_digits():
    return chip_digits(lax.axis_size("row") // 2)


def reduce_rows(value, lower=False, filler=()):
    digits = row_digits()
    for place, (size, stride) in reversed(list(enumerate(digits))):
        outermost = place == len(digits) - 1
        value, filler = reduce_digit(value, size, stride, lower and outermost, filler)
    return value, filler


def by_core(core, mine, other, axis):
    return jnp.concatenate(
        [jnp.where(core == 0, mine, other), jnp.where(core == 0, other, mine)], axis
    )


def leaf_reduce(upper, lower, side):
    from_x = leaf_swap(upper[0], 1)
    from_y = leaf_swap(lower[0], 2)
    lower_kept, side = after((lower[1],), side)
    lower = (lower[0], lower_kept)
    from_x, from_y = lax.optimization_barrier((from_x, from_y))
    first, second = upper[1][0] + from_x[0], lower[1][0] + from_y[0]
    first, second = leaf_swap(first, 2), leaf_swap(second, 1)
    first, second = lax.optimization_barrier((first, second))
    return jnp.concatenate(
        [upper[1][1] + from_x[1] + first, lower[1][1] + from_y[1] + second], 0
    ), side


def leaf_gather(piece, side, finish, between):
    rows = piece.shape[0]
    first, second = piece[: rows // 2], piece[rows // 2 :]
    first_y = leaf_swap(first, 2)
    second_x = leaf_swap(second, 1)
    first_y, second_x, side = lax.optimization_barrier((first_y, second_x, side))
    upper = jnp.stack([first, first_y])
    lower = jnp.stack([second, second_x])
    upper_far = leaf_swap(upper, 1)
    lower_far = leaf_swap(lower, 2)
    work = between(upper, lower), finish(side)
    upper_far, lower_far, work = lax.optimization_barrier((upper_far, lower_far, work))
    return (upper, upper_far, lower, lower_far), *work


def in_order(pieces, x_bit, y_bit):
    upper, upper_far, lower, lower_far = pieces

    def at(block, column):
        own_block, own_column = y_bit == block, x_bit == column
        return [
            jnp.where(
                own_column,
                jnp.where(own_block, upper[0], upper[1]),
                jnp.where(own_block, upper_far[0], upper_far[1]),
            ),
            jnp.where(
                own_block,
                jnp.where(own_column, lower[0], lower[1]),
                jnp.where(own_column, lower_far[0], lower_far[1]),
            ),
        ]

    return jnp.concatenate(
        [jnp.concatenate(at(0, column) + at(1, column), 0) for column in range(2)], 1
    )


def split(value):
    high = value.astype(jnp.bfloat16)
    return high, (value - high.astype(jnp.float32)).astype(jnp.bfloat16)


def scale_rows(value, mask_ref, slot, first_block, count):
    rows = value.shape[0] // count
    return jnp.concatenate(
        [
            value[k * rows : (k + 1) * rows] * mask_ref[slot, first_block + k].astype(jnp.float32)
            for k in range(count)
        ],
        0,
    )


def forward_kernel(slot, place, tiles, mask_blocks, bit_ref, mask_ref, panel_ref, near_ref, far_ref, *refs):
    prev, (out_first, out_last, high, low) = refs[:-4], refs[-4:]
    turn, step = pl.program_id(0), pl.program_id(1)
    columns = near_ref.shape[1]

    @pl.when((turn == 0) & (step == 0))
    def _():
        for k, ref in enumerate((near_ref, far_ref)):
            part = split(ref[...])
            high[:, k * columns : (k + 1) * columns] = part[0]
            low[:, k * columns : (k + 1) * columns] = part[1]

    panel_high, panel_low = split(panel_ref[...])

    def dot(left, right):
        return jnp.dot(left, right, preferred_element_type=jnp.float32)

    result = dot(panel_high, high[...]) + (dot(panel_high, low[...]) + dot(panel_low, high[...]))
    block = jnp.where(turn == 0, 1 - bit_ref[0], bit_ref[0])
    tile = (2 * block + place) * tiles + step
    result = scale_rows(result, mask_ref, slot, tile * mask_blocks, mask_blocks)
    near, far = result[:, :columns], result[:, columns:]
    if place == 0:
        out_first[...] = near + prev[0][...] if prev else near
        out_last[...] = far + prev[1][...] if prev else far
    else:

        @pl.when(turn == 0)
        def _():
            out_first[0] = near + prev[0][0] if prev else near
            out_first[1] = far + prev[0][1] if prev else far

        @pl.when(turn == 1)
        def _():
            out_last[0] = near + prev[1][0] if prev else near
            out_last[1] = far + prev[1][1] if prev else far


def panel_forward(panel_anc, mask, slot, place, y_bit, near, far, prev=(), tile_rows=256):
    rows_local, width = panel_anc.shape[2:]
    quarter = rows_local // 4
    tiles = quarter // tile_rows
    columns = near.shape[1]
    mask_blocks = mask.shape[1] // (4 * tiles)

    def panel_index(turn, step, bit_ref, mask_ref):
        block = jnp.where(turn == 0, 1 - bit_ref[0], bit_ref[0])
        return (0, slot, (2 * block + place) * tiles + step, 0)

    if place == 0:
        out_specs = [
            pl.BlockSpec((None, tile_rows, columns), lambda turn, step, *_: (turn, step, 0))
        ] * 2
    else:
        out_specs = [
            pl.BlockSpec(
                (2, tile_rows, columns),
                lambda turn, step, *_: (0, jnp.where(turn == 0, step, tiles - 1), 0),
            ),
            pl.BlockSpec(
                (2, tile_rows, columns), lambda turn, step, *_: (0, jnp.where(turn == 0, 0, step), 0)
            ),
        ]
    shape = jax.ShapeDtypeStruct((2, quarter, columns), jnp.float32)
    return pl.pallas_call(
        functools.partial(forward_kernel, slot, place, tiles, mask_blocks),
        out_shape=[shape, shape],
        grid_spec=pltpu.PrefetchScalarGridSpec(
            num_scalar_prefetch=2,
            grid=(2, tiles),
            in_specs=[
                pl.BlockSpec((None, None, tile_rows, width), panel_index),
                pl.BlockSpec(memory_space=pltpu.VMEM),
                pl.BlockSpec(memory_space=pltpu.VMEM),
                *(out_specs if prev else []),
            ],
            out_specs=out_specs,
            scratch_shapes=[pltpu.VMEM((width, 2 * columns), jnp.bfloat16)] * 2,
        ),
        cost_estimate=pl.CostEstimate(
            flops=12 * quarter * width * 2 * columns,
            bytes_accessed=4 * (2 * quarter * width + 2 * width * columns + 4 * quarter * columns),
            transcendentals=0,
        ),
    )(y_bit.reshape(1).astype(jnp.int32), mask, panel_anc, near, far, *prev)


def backward_kernel(slot, side, mask_blocks, bit_ref, mask_ref, panel_ref, upper_ref, lower_ref, *refs):
    prev, (out_first, out_last, panel_parts, value_parts, total) = refs[:-5], refs[-5:]
    if prev:
        *prev, rhs_ref = prev
    phase = pl.program_id(0)
    rows = panel_ref.shape[0]
    columns = upper_ref.shape[2]
    tile = backward_tile(side, phase, bit_ref)

    def put(index, value):
        value = scale_rows(value, mask_ref, slot, tile * mask_blocks, mask_blocks)
        high, low = split(value)
        span = slice(index * columns, (index + 1) * columns)
        value_parts[0:rows, span] = high
        value_parts[rows : 2 * rows, span] = high
        value_parts[2 * rows : 3 * rows, span] = low

    high, low = split(panel_ref[...])
    panel_parts[0:rows] = high
    panel_parts[rows : 2 * rows] = low
    panel_parts[2 * rows : 3 * rows] = high

    def dot(right):
        return lax.dot_general(
            panel_parts[...], right, (((0,), (0,)), ((), ())), preferred_element_type=jnp.float32
        )

    near, far = slice(0, columns), slice(columns, 2 * columns)
    here, there = (near, far) if side == 0 else (far, near)

    @pl.when(phase == 0)
    def _():
        put(0, upper_ref[0])
        result = dot(value_parts[:, near])
        if prev:
            total[:, here] = prev[side][...] + result
            total[:, there] = prev[1 - side][...]
        else:
            total[:, here] = result
            total[:, there] = jnp.zeros_like(result)

    @pl.when(phase == 1)
    def _():
        put(0, upper_ref[0])
        total[:, here] += dot(value_parts[:, near])

    @pl.when(phase == 2)
    def _():
        put(0, lower_ref[0])
        put(1, lower_ref[1])
        total[...] += dot(value_parts[...])
        if side == 0:
            out_first[...] = total[:, near]
            out_last[...] = total[:, far]
        else:
            length = rhs_ref.shape[0]
            count = total.shape[0] // length

            def put_out(kept, sent):
                for k in range(count):
                    source = pl.ds(pl.multiple_of(bit_ref[2 + k] * length, length), length)
                    place = slice(k * length, (k + 1) * length)
                    value = total[source, kept]
                    out_first[place] = value - rhs_ref[...] if k == count - 1 else value
                    out_last[place] = total[source, sent]

            pl.when(bit_ref[1] == 1)(functools.partial(put_out, near, far))
            pl.when(bit_ref[1] == 0)(functools.partial(put_out, far, near))


def backward_tile(side, phase, bit_ref):
    own, other = bit_ref[0], 1 - bit_ref[0]
    lower = 2 * (own if side == 0 else other) + 1
    return jnp.where(phase == 0, 2 * own, jnp.where(phase == 1, 2 * other, lower))


def panel_backward(panel_anc, mask, slot, side, bits, upper, lower, prev=()):
    rows_local, width = panel_anc.shape[2:]
    quarter = rows_local // 4
    columns = upper.shape[2]
    mask_blocks = mask.shape[1] // 4

    def panel_index(phase, bit_ref, mask_ref):
        return (0, slot, backward_tile(side, phase, bit_ref), 0)

    out_spec = pl.BlockSpec((width, columns), lambda *_: (0, 0))
    shape = jax.ShapeDtypeStruct((width, columns), jnp.float32)
    return pl.pallas_call(
        functools.partial(backward_kernel, slot, side, mask_blocks),
        out_shape=[shape, shape],
        grid_spec=pltpu.PrefetchScalarGridSpec(
            num_scalar_prefetch=2,
            grid=(3,),
            in_specs=[
                pl.BlockSpec((None, None, quarter, width), panel_index),
                pl.BlockSpec((1, quarter, columns), lambda phase, *_: (jnp.minimum(phase, 1), 0, 0)),
                pl.BlockSpec((2, quarter, columns), lambda *_: (0, 0, 0)),
                *[pl.BlockSpec(value.shape, lambda *_: (0, 0)) for value in prev],
            ],
            out_specs=[out_spec, out_spec],
            scratch_shapes=[
                pltpu.VMEM((3 * quarter, width), jnp.bfloat16),
                pltpu.VMEM((3 * quarter, 2 * columns), jnp.bfloat16),
                pltpu.VMEM((width, 2 * columns), jnp.float32),
            ],
        ),
        cost_estimate=pl.CostEstimate(
            flops=6 * 4 * quarter * width * columns,
            bytes_accessed=4 * (3 * quarter * width + 4 * quarter * columns + 4 * width * columns),
            transcendentals=0,
        ),
    )(bits, mask, panel_anc, upper, lower, *prev)


def from_partner(value, axis, bit):
    mask = 2**bit
    pairs = [(source, source ^ mask) for source in range(lax.axis_size(axis))]
    return lax.ppermute(value, axis, pairs)


def ancestor_solve(inverse_rows, values):
    rows_local, width = inverse_rows.shape
    if rows_local >= width:
        blocks = inverse_rows.reshape(rows_local // width, width, width)
        grouped = values.reshape(rows_local // width, width, values.shape[1])
        forward = jnp.einsum("kij,kjr->kir", blocks, grouped, precision=PRECISION)
        result = jnp.einsum("kji,kjr->kir", blocks, forward, precision=PRECISION)
        return result.reshape(rows_local, values.shape[1])
    row_index = lax.axis_index("row")
    levels = (width // rows_local).bit_length() - 1
    whole = values
    for bit_number in range(levels):
        other = from_partner(whole, "row", bit_number)
        upper = row_index >> bit_number & 1
        whole = jnp.where(
            upper == 1, jnp.concatenate([other, whole], 0), jnp.concatenate([whole, other], 0)
        )
    forward = product(inverse_rows, whole)
    partial_value = transposed(inverse_rows, forward)
    for bit_number in reversed(range(levels)):
        half = partial_value.shape[0] // 2
        upper = row_index >> bit_number & 1
        keep = jnp.where(upper == 1, partial_value[half:], partial_value[:half])
        outgoing = jnp.where(upper == 1, partial_value[:half], partial_value[half:])
        partial_value = keep + from_partner(outgoing, "row", bit_number)
    return partial_value


def solve(rhs_sub, rhs_anc, inv_sub, panel_mid, panel_anc, block_mask, inv_anc):
    rhs_local = rhs_sub[0]
    rows_local = panel_anc.shape[2]
    width = panel_anc.shape[3]
    rows_own = rhs_local.shape[1]
    columns = rhs_local.shape[2]
    block_count = block_mask.shape[2]
    row_index = lax.axis_index("row")
    core = row_index % 2
    leaf = lax.axis_index("leaf")
    x_bit, y_bit = leaf % 2, leaf // 2
    paired = lax.axis_size("leaf") == 4 and rows_local == 2 * width and len(row_digits()) == 1
    mask = block_mask[0].astype(jnp.float32)
    half = columns // 2

    def masked(slot, value):
        blocks = value.reshape(block_count, rows_local // block_count, value.shape[1])
        return (blocks * mask[slot][:, None, None]).reshape(value.shape)

    def halves(value):
        return jnp.where(core == 0, value[..., :half], value[..., half:])

    def other_half(value):
        return jnp.where(core == 0, value[..., half:], value[..., :half])

    rhs_chip = by_core(core, halves(rhs_local), core_swap(other_half(rhs_local)), 1)
    inverses = inv_sub[0]
    inverses_other, middle_other = core_swap(inverses), core_swap(panel_mid[0])
    inverse_first = by_core(core, inverses[0], inverses_other[0], 0)
    inverse_second = by_core(core, inverses[1], inverses_other[1], 0)
    middle = by_core(core, panel_mid[0], middle_other, 0)

    def both_halves(value):
        return by_core(core, value, core_swap(value), 1)

    def near_and_far(value):
        swapped = core_swap(value)
        far_is_mine = core == x_bit
        return jnp.where(far_is_mine, swapped, value), jnp.where(far_is_mine, value, swapped)

    block_mask = block_mask[0]
    gathered, inverse_first = gather_rows(rhs_chip[0], lower=True, filler=inverse_first)
    first = product(inverse_first, gathered)
    first_all, (middle, inverse_second) = gather_rows(first, filler=(middle, inverse_second))
    residual = rhs_chip[1] - product(middle, first_all)
    if paired:
        sides = near_and_far(first_all)
        upper = panel_forward(panel_anc, block_mask, 0, 0, y_bit, *sides)
        lower = panel_forward(panel_anc, block_mask, 0, 1, y_bit, *sides)
        gathered, upper = gather_rows(residual, lower=True, filler=upper)
        second = product(inverse_second, gathered)
        second_all, lower = gather_rows(second, filler=lower)
        sides = near_and_far(second_all)
        upper = panel_forward(panel_anc, block_mask, 1, 0, y_bit, *sides, upper)
        lower = panel_forward(panel_anc, block_mask, 1, 1, y_bit, *sides, lower)
    else:
        gathered, _ = gather_rows(residual, lower=True)
        second = product(inverse_second, gathered)
        update = masked(0, product(panel_anc[0, 0], both_halves(first_all)))
        second_all, _ = gather_rows(second)
        update = update + masked(1, product(panel_anc[0, 1], both_halves(second_all)))

    *inner_digits, (size, stride) = row_digits()
    inverses, second_all = lax.optimization_barrier((inverses, second_all))
    block = inverses
    for inner_size, inner_stride in inner_digits:
        block = jnp.concatenate(gather_join(block, *gather_both(block, inner_size, inner_stride), inner_size, inner_stride), 1)
    received = gather_near(block, size, stride)

    def whole_inverses(received, passed):
        joined = gather_join(block, received, passed, size, stride, ordered=False)
        mine = [jnp.concatenate([part[slot] for part in joined], 0) for slot in range(2)]
        return [(value, core_swap(value)) for value in mine]

    if paired:
        inverse_anc = jnp.where(y_bit == 0, inv_anc[:width], inv_anc[width:])
        own = jnp.where(y_bit == 0, rhs_anc[:width], rhs_anc[width:])
        own = jnp.where(x_bit == 0, own[:, :half], own[:, half:])
        total, received = leaf_reduce(upper, lower, received)
        passed = gather_far(received, size, stride)
        total, inverse_anc = lax.optimization_barrier((own - total, inverse_anc))
        forward = lax.optimization_barrier(product(inverse_anc, total))
        solved = row_major(transposed(inverse_anc, forward))
        bits = jnp.stack([y_bit, x_bit == core, *block_order(size, stride)], dtype=jnp.int32)

        def begun(upper, lower):
            sums = []
            for slot in range(2):
                sums.append(panel_backward(panel_anc, block_mask, slot, 0, bits, upper, lower))
            return sums

        pieces, sums, wholes = leaf_gather(
            solved, passed, lambda passed: whole_inverses(received, passed), begun
        )
        x_anc = in_order(pieces, x_bit, y_bit)
    else:
        wholes = whole_inverses(received, gather_far(received, size, stride))
        total = lax.psum_scatter(update, "leaf", scatter_dimension=1, tiled=True)
        share = total.shape[1]
        own = lax.dynamic_slice_in_dim(rhs_anc, leaf * share, share, 1)
        x_anc = lax.all_gather(ancestor_solve(inv_anc, own - total), "leaf", axis=1, tiled=True)
        pieces = x_anc

    rows_chip = 2 * rows_own

    def chip_sum(slot, rhs, pieces):
        if paired:
            keep, send = panel_backward(
                panel_anc, block_mask, slot, 1, bits, pieces[1], pieces[3], (*sums[slot], rhs)
            )
            return keep + core_swap(send)
        keep, send = (
            transposed(panel_anc[0, slot], masked(slot, part))
            for part in (halves(pieces), other_half(pieces))
        )
        value = keep + core_swap(send)
        start = row_index // 2 * rows_chip
        own = lax.dynamic_slice_in_dim(value, start, rows_chip, 0) - rhs
        value = lax.dynamic_update_slice_in_dim(value, own, start, 0)
        return jnp.concatenate(sending_order(value, size, stride), 0)

    def partial_solve(slot, value):
        cores = value.reshape(-1, 2, rows_own, half)
        first = jnp.where(core == 0, cores[:, 0], cores[:, 1]).reshape(-1, half)
        last = jnp.where(core == 0, cores[:, 1], cores[:, 0]).reshape(-1, half)
        first, last = lax.optimization_barrier((first, last))
        return transposed(wholes[slot][0], first) + transposed(wholes[slot][1], last)

    middle_columns = jnp.concatenate(
        [
            lax.dynamic_slice_in_dim(middle, k * (width // size), width // size, 1)
            for k in block_order(size, stride)
        ],
        1,
    )
    second_partial = partial_solve(1, chip_sum(1, second, pieces))
    second_partial, pieces = lax.optimization_barrier((second_partial, pieces))
    first_sum = chip_sum(0, first, pieces)
    second_total, first_sum = reduce_rows(second_partial, filler=(first_sum, middle_columns))
    first_sum, middle_columns = first_sum
    x_second = -second_total
    first_partial = partial_solve(0, first_sum + transposed(middle_columns, x_second))
    first_total, x_anc = reduce_rows(first_partial, filler=x_anc)
    x_first = -first_total

    both = jnp.stack([x_first, x_second])
    keep = jnp.where(core == 0, both[:, :rows_own], both[:, rows_own:])
    send = jnp.where(core == 0, both[:, rows_own:], both[:, :rows_own])
    x_sub = by_core(core, keep, core_swap(send), 2)
    return x_sub[None], x_anc


def solution(mesh):
    return jax.shard_map(
        solve,
        mesh=mesh,
        in_specs=(
            P("leaf", None, "row", None),
            P("row", None),
            P("leaf", None, "row", None),
            P("leaf", "row", None),
            P("leaf", None, "row", None),
            P("leaf", None, "row"),
            P("row", None),
        ),
        out_specs=(P("leaf", None, "row", None), P("row", None)),
        check_vma=False,
    )
```

```python
import functools

import jax
import jax.numpy as jnp
from jax import lax
from jax.experimental import pallas as pl
from jax.experimental.layout import Layout, with_layout_constraint
from jax.experimental.pallas import tpu as pltpu
from jax.sharding import PartitionSpec as P


PRECISION = lax.Precision.HIGH


def product(left, right):
    return jnp.dot(left, right, precision=PRECISION, preferred_element_type=jnp.float32)


def transposed(left, right):
    return lax.dot_general(
        left,
        right,
        (((0,), (0,)), ((), ())),
        precision=PRECISION,
        preferred_element_type=jnp.float32,
    )


def row_major(value):
    return with_layout_constraint(value, Layout(tuple(range(value.ndim))))


def core_swap(value):
    count = lax.axis_size("row")
    return lax.ppermute(value, "row", [(r, r ^ 1) for r in range(count)])


def leaf_swap(value, mask):
    count = lax.axis_size("leaf")
    return lax.ppermute(value, "leaf", [(g, g ^ mask) for g in range(count)])


def chip_digits(chips):
    digits, stride = [], 1
    while chips > 1:
        size = 4 if chips % 4 == 0 else 2
        digits.append((size, stride))
        stride *= size
        chips //= size
    return digits


def digit_permute(value, size, stride, moves):
    target = dict(moves)
    pairs = []
    for r in range(lax.axis_size("row")):
        digit = (r // 2) // stride % size
        if digit in target:
            pairs.append((r, r + 2 * stride * (target[digit] - digit)))
    return lax.ppermute(value, "row", pairs)


def digit_index(size, stride):
    return lax.axis_index("row") // 2 // stride % size


def after(values, filler):
    return lax.optimization_barrier((*values, filler))


def gather_near(value, size, stride, lower=False):
    def moves(pairs):
        return [(a, b) for a, b in pairs if a < b] if lower else pairs

    if size == 2:
        return (digit_permute(value, size, stride, moves([(0, 1), (1, 0)])),)
    near = digit_permute(value, size, stride, moves([(0, 1), (1, 0), (2, 3), (3, 2)]))
    inner = digit_permute(value, size, stride, moves([(1, 2), (2, 1)]))
    return near, inner


def gather_far(received, size, stride, lower=False):
    def moves(pairs):
        return [(a, b) for a, b in pairs if a < b] if lower else pairs

    if size == 2:
        return ()
    near, inner = received
    relay = digit_permute(near, size, stride, moves([(1, 2), (2, 1)]))
    far = digit_permute(near, size, stride, moves([(1, 3), (2, 0)]))
    outer = digit_permute(inner, size, stride, moves([(1, 0), (2, 3)]))
    return relay, far, outer


def gather_join(value, received, passed, size, stride, ordered=True):
    me = digit_index(size, stride)
    if size == 2:
        (near,) = received
        if not ordered:
            return [near, value]
        return [jnp.where(me == 0, value, near), jnp.where(me == 0, near, value)]
    near, inner = received
    relay, far, outer = passed
    middle = (me == 1) | (me == 2)
    third = jnp.where(middle, inner, outer)
    fourth = jnp.where(middle, relay, far)
    odd = me % 2 == 1
    if not ordered:
        return [fourth, third, near, value]
    even_one = jnp.where(odd, near, value)
    odd_one = jnp.where(odd, value, near)
    high = me >= 2
    return [
        jnp.where(high, fourth, even_one),
        jnp.where(high, third, odd_one),
        jnp.where(high, even_one, third),
        jnp.where(high, odd_one, fourth),
    ]


def gather_both(value, size, stride):
    received = gather_near(value, size, stride)
    return received, gather_far(received, size, stride)


def gather_digit(value, size, stride, lower, filler):
    received = gather_near(value, size, stride, lower)
    passed = gather_far(received, size, stride, lower)
    last, filler = after((passed or received,), filler)
    received, passed = (received, last) if passed else (last, passed)
    return jnp.concatenate(gather_join(value, received, passed, size, stride), 0), filler


def block_order(size, stride):
    me = digit_index(size, stride)
    if size == 2:
        return 1 - me, me
    high = me >= 2
    return jnp.where(high, 0, 3), jnp.where(high, 1, 2), me ^ 1, me


def sending_order(value, size, stride):
    rows = value.shape[0] // size
    return [
        lax.dynamic_slice_in_dim(value, k * rows, rows, 0) for k in block_order(size, stride)
    ]


def reduce_digit(value, size, stride, lower, filler):
    def moves(pairs):
        return [(a, b) for a, b in pairs if a > b] if lower else pairs

    block = sending_order(value, size, stride)
    if size == 2:
        other = digit_permute(block[0], size, stride, moves([(0, 1), (1, 0)]))
        other, filler = after((other,), filler)
        return block[1] + other, filler
    far = digit_permute(block[0], size, stride, moves([(3, 1), (0, 2)]))
    relay = digit_permute(block[0], size, stride, moves([(2, 1), (1, 2)]))
    outer = digit_permute(block[1], size, stride, moves([(0, 1), (3, 2)]))
    far, relay, outer = lax.optimization_barrier((far, relay, outer))
    inner = digit_permute(block[1] + outer, size, stride, moves([(1, 2), (2, 1)]))
    near = digit_permute(block[2] + (far + relay), size, stride, moves([(0, 1), (1, 0), (2, 3), (3, 2)]))
    near, inner, filler = after((near, inner), filler)
    return block[3] + near + inner, filler


def gather_rows(value, lower=False, filler=()):
    digits = chip_digits(lax.axis_size("row") // 2)
    for place, (size, stride) in enumerate(digits):
        outermost = place == len(digits) - 1
        value, filler = gather_digit(value, size, stride, lower and outermost, filler)
    return value, filler


def row_digits():
    return chip_digits(lax.axis_size("row") // 2)


def reduce_rows(value, lower=False, filler=()):
    digits = row_digits()
    for place, (size, stride) in reversed(list(enumerate(digits))):
        outermost = place == len(digits) - 1
        value, filler = reduce_digit(value, size, stride, lower and outermost, filler)
    return value, filler


def by_core(core, mine, other, axis):
    return jnp.concatenate(
        [jnp.where(core == 0, mine, other), jnp.where(core == 0, other, mine)], axis
    )


def leaf_reduce(upper, lower, side):
    from_x = leaf_swap(upper[0], 1)
    from_y = leaf_swap(lower[0], 2)
    lower_kept, side = after((lower[1],), side)
    lower = (lower[0], lower_kept)
    from_x, from_y = lax.optimization_barrier((from_x, from_y))
    first, second = upper[1][0] + from_x[0], lower[1][0] + from_y[0]
    first, second = leaf_swap(first, 2), leaf_swap(second, 1)
    first, second = lax.optimization_barrier((first, second))
    return jnp.concatenate(
        [upper[1][1] + from_x[1] + first, lower[1][1] + from_y[1] + second], 0
    ), side


def leaf_gather(piece, side, finish, between):
    rows = piece.shape[0]
    first, second = piece[: rows // 2], piece[rows // 2 :]
    first_y = leaf_swap(first, 2)
    second_x = leaf_swap(second, 1)
    wholes = finish(side)
    first_y, second_x, wholes = lax.optimization_barrier((first_y, second_x, wholes))
    upper = jnp.stack([first, first_y])
    lower = jnp.stack([second, second_x])
    upper_far = leaf_swap(upper, 1)
    lower_far = leaf_swap(lower, 2)
    sums = between(upper, lower)
    upper_far, lower_far, sums = lax.optimization_barrier((upper_far, lower_far, sums))
    return (upper, upper_far, lower, lower_far), sums, wholes


def in_order(pieces, x_bit, y_bit):
    upper, upper_far, lower, lower_far = pieces

    def at(block, column):
        own_block, own_column = y_bit == block, x_bit == column
        return [
            jnp.where(
                own_column,
                jnp.where(own_block, upper[0], upper[1]),
                jnp.where(own_block, upper_far[0], upper_far[1]),
            ),
            jnp.where(
                own_block,
                jnp.where(own_column, lower[0], lower[1]),
                jnp.where(own_column, lower_far[0], lower_far[1]),
            ),
        ]

    return jnp.concatenate(
        [jnp.concatenate(at(0, column) + at(1, column), 0) for column in range(2)], 1
    )


def split(value):
    high = value.astype(jnp.bfloat16)
    return high, (value - high.astype(jnp.float32)).astype(jnp.bfloat16)


def scale_rows(value, mask_ref, slot, first_block, count):
    rows = value.shape[0] // count
    return jnp.concatenate(
        [
            value[k * rows : (k + 1) * rows] * mask_ref[slot, first_block + k].astype(jnp.float32)
            for k in range(count)
        ],
        0,
    )


def forward_kernel(slot, place, tiles, mask_blocks, bit_ref, mask_ref, panel_ref, near_ref, far_ref, *refs):
    prev, (out_first, out_last, high, low) = refs[:-4], refs[-4:]
    turn, step = pl.program_id(0), pl.program_id(1)
    columns = near_ref.shape[1]

    @pl.when((turn == 0) & (step == 0))
    def _():
        for k, ref in enumerate((near_ref, far_ref)):
            part = split(ref[...])
            high[:, k * columns : (k + 1) * columns] = part[0]
            low[:, k * columns : (k + 1) * columns] = part[1]

    panel_high, panel_low = split(panel_ref[...])

    def dot(left, right):
        return jnp.dot(left, right, preferred_element_type=jnp.float32)

    result = dot(panel_high, high[...]) + (dot(panel_high, low[...]) + dot(panel_low, high[...]))
    block = jnp.where(turn == 0, 1 - bit_ref[0], bit_ref[0])
    tile = (2 * block + place) * tiles + step
    result = scale_rows(result, mask_ref, slot, tile * mask_blocks, mask_blocks)
    near, far = result[:, :columns], result[:, columns:]
    if place == 0:
        out_first[...] = near + prev[0][...] if prev else near
        out_last[...] = far + prev[1][...] if prev else far
    else:

        @pl.when(turn == 0)
        def _():
            out_first[0] = near + prev[0][0] if prev else near
            out_first[1] = far + prev[0][1] if prev else far

        @pl.when(turn == 1)
        def _():
            out_last[0] = near + prev[1][0] if prev else near
            out_last[1] = far + prev[1][1] if prev else far


def panel_forward(panel_anc, mask, slot, place, y_bit, near, far, prev=(), tile_rows=256):
    rows_local, width = panel_anc.shape[2:]
    quarter = rows_local // 4
    tiles = quarter // tile_rows
    columns = near.shape[1]
    mask_blocks = mask.shape[1] // (4 * tiles)

    def panel_index(turn, step, bit_ref, mask_ref):
        block = jnp.where(turn == 0, 1 - bit_ref[0], bit_ref[0])
        return (0, slot, (2 * block + place) * tiles + step, 0)

    if place == 0:
        out_specs = [
            pl.BlockSpec((None, tile_rows, columns), lambda turn, step, *_: (turn, step, 0))
        ] * 2
    else:
        out_specs = [
            pl.BlockSpec(
                (2, tile_rows, columns),
                lambda turn, step, *_: (0, jnp.where(turn == 0, step, tiles - 1), 0),
            ),
            pl.BlockSpec(
                (2, tile_rows, columns), lambda turn, step, *_: (0, jnp.where(turn == 0, 0, step), 0)
            ),
        ]
    shape = jax.ShapeDtypeStruct((2, quarter, columns), jnp.float32)
    return pl.pallas_call(
        functools.partial(forward_kernel, slot, place, tiles, mask_blocks),
        out_shape=[shape, shape],
        grid_spec=pltpu.PrefetchScalarGridSpec(
            num_scalar_prefetch=2,
            grid=(2, tiles),
            in_specs=[
                pl.BlockSpec((None, None, tile_rows, width), panel_index),
                pl.BlockSpec(memory_space=pltpu.VMEM),
                pl.BlockSpec(memory_space=pltpu.VMEM),
                *(out_specs if prev else []),
            ],
            out_specs=out_specs,
            scratch_shapes=[pltpu.VMEM((width, 2 * columns), jnp.bfloat16)] * 2,
        ),
        cost_estimate=pl.CostEstimate(
            flops=12 * quarter * width * 2 * columns,
            bytes_accessed=4 * (2 * quarter * width + 2 * width * columns + 4 * quarter * columns),
            transcendentals=0,
        ),
    )(y_bit.reshape(1).astype(jnp.int32), mask, panel_anc, near, far, *prev)


def backward_kernel(slot, side, mask_blocks, bit_ref, mask_ref, panel_ref, upper_ref, lower_ref, *refs):
    prev, (out_first, out_last, panel_parts, value_parts, total) = refs[:-5], refs[-5:]
    if prev:
        *prev, rhs_ref = prev
    phase, step = pl.program_id(0), pl.program_id(1)
    rows = panel_ref.shape[0]
    columns = upper_ref.shape[2]
    tile = backward_quarter(side, phase, bit_ref) * pl.num_programs(1) + step

    def put(index, value):
        value = scale_rows(value, mask_ref, slot, tile * mask_blocks, mask_blocks)
        high, low = split(value)
        span = slice(index * columns, (index + 1) * columns)
        value_parts[0:rows, span] = high
        value_parts[rows : 2 * rows, span] = high
        value_parts[2 * rows : 3 * rows, span] = low

    high, low = split(panel_ref[...])
    panel_parts[0:rows] = high
    panel_parts[rows : 2 * rows] = low
    panel_parts[2 * rows : 3 * rows] = high

    def dot(right):
        return lax.dot_general(
            panel_parts[...], right, (((0,), (0,)), ((), ())), preferred_element_type=jnp.float32
        )

    near, far = slice(0, columns), slice(columns, 2 * columns)
    here = near if side == 0 else far

    @pl.when((phase == 0) & (step == 0))
    def _():
        if prev:
            total[:, near] = prev[0][...]
            total[:, far] = prev[1][...]
        else:
            total[...] = jnp.zeros_like(total)

    @pl.when(phase < 2)
    def _():
        put(0, upper_ref[0])
        total[:, here] += dot(value_parts[:, near])

    @pl.when(phase == 2)
    def _():
        put(0, lower_ref[0])
        put(1, lower_ref[1])
        total[...] += dot(value_parts[...])

    @pl.when((phase == 2) & (step == pl.num_programs(1) - 1))
    def _():
        if side == 0:
            out_first[...] = total[:, near]
            out_last[...] = total[:, far]
        else:
            length = rhs_ref.shape[0]
            count = total.shape[0] // length

            def put_out(kept, sent):
                for k in range(count):
                    source = pl.ds(pl.multiple_of(bit_ref[2 + k] * length, length), length)
                    place = slice(k * length, (k + 1) * length)
                    value = total[source, kept]
                    out_first[place] = value - rhs_ref[...] if k == count - 1 else value
                    out_last[place] = total[source, sent]

            pl.when(bit_ref[1] == 1)(functools.partial(put_out, near, far))
            pl.when(bit_ref[1] == 0)(functools.partial(put_out, far, near))


def backward_quarter(side, phase, bit_ref):
    own, other = bit_ref[0], 1 - bit_ref[0]
    lower = 2 * (own if side == 0 else other) + 1
    return jnp.where(phase == 0, 2 * own, jnp.where(phase == 1, 2 * other, lower))


def panel_backward(panel_anc, mask, slot, side, bits, upper, lower, prev=(), tile_rows=256):
    rows_local, width = panel_anc.shape[2:]
    quarter = rows_local // 4
    columns = upper.shape[2]
    tiles = quarter // tile_rows
    mask_blocks = mask.shape[1] // (4 * tiles)

    def panel_index(phase, step, bit_ref, mask_ref):
        return (0, slot, backward_quarter(side, phase, bit_ref) * tiles + step, 0)

    def upper_index(phase, step, *_):
        return (jnp.minimum(phase, 1), jnp.where(phase < 2, step, tiles - 1), 0)

    def lower_index(phase, step, *_):
        return (0, jnp.where(phase < 2, 0, step), 0)

    out_spec = pl.BlockSpec((width, columns), lambda *_: (0, 0))
    shape = jax.ShapeDtypeStruct((width, columns), jnp.float32)
    return pl.pallas_call(
        functools.partial(backward_kernel, slot, side, mask_blocks),
        out_shape=[shape, shape],
        grid_spec=pltpu.PrefetchScalarGridSpec(
            num_scalar_prefetch=2,
            grid=(3, tiles),
            in_specs=[
                pl.BlockSpec((None, None, tile_rows, width), panel_index),
                pl.BlockSpec((1, tile_rows, columns), upper_index),
                pl.BlockSpec((2, tile_rows, columns), lower_index),
                *[pl.BlockSpec(value.shape, lambda *_: (0, 0)) for value in prev],
            ],
            out_specs=[out_spec, out_spec],
            scratch_shapes=[
                pltpu.VMEM((3 * tile_rows, width), jnp.bfloat16),
                pltpu.VMEM((3 * tile_rows, 2 * columns), jnp.bfloat16),
                pltpu.VMEM((width, 2 * columns), jnp.float32),
            ],
        ),
        cost_estimate=pl.CostEstimate(
            flops=6 * 4 * quarter * width * columns,
            bytes_accessed=4 * (3 * quarter * width + 4 * quarter * columns + 4 * width * columns),
            transcendentals=0,
        ),
    )(bits, mask, panel_anc, upper, lower, *prev)


def from_partner(value, axis, bit):
    mask = 2**bit
    pairs = [(source, source ^ mask) for source in range(lax.axis_size(axis))]
    return lax.ppermute(value, axis, pairs)


def ancestor_solve(inverse_rows, values):
    rows_local, width = inverse_rows.shape
    if rows_local >= width:
        blocks = inverse_rows.reshape(rows_local // width, width, width)
        grouped = values.reshape(rows_local // width, width, values.shape[1])
        forward = jnp.einsum("kij,kjr->kir", blocks, grouped, precision=PRECISION)
        result = jnp.einsum("kji,kjr->kir", blocks, forward, precision=PRECISION)
        return result.reshape(rows_local, values.shape[1])
    row_index = lax.axis_index("row")
    levels = (width // rows_local).bit_length() - 1
    whole = values
    for bit_number in range(levels):
        other = from_partner(whole, "row", bit_number)
        upper = row_index >> bit_number & 1
        whole = jnp.where(
            upper == 1, jnp.concatenate([other, whole], 0), jnp.concatenate([whole, other], 0)
        )
    forward = product(inverse_rows, whole)
    partial_value = transposed(inverse_rows, forward)
    for bit_number in reversed(range(levels)):
        half = partial_value.shape[0] // 2
        upper = row_index >> bit_number & 1
        keep = jnp.where(upper == 1, partial_value[half:], partial_value[:half])
        outgoing = jnp.where(upper == 1, partial_value[:half], partial_value[half:])
        partial_value = keep + from_partner(outgoing, "row", bit_number)
    return partial_value


def solve(rhs_sub, rhs_anc, inv_sub, panel_mid, panel_anc, block_mask, inv_anc):
    rhs_local = rhs_sub[0]
    rows_local = panel_anc.shape[2]
    width = panel_anc.shape[3]
    rows_own = rhs_local.shape[1]
    columns = rhs_local.shape[2]
    block_count = block_mask.shape[2]
    row_index = lax.axis_index("row")
    core = row_index % 2
    leaf = lax.axis_index("leaf")
    x_bit, y_bit = leaf % 2, leaf // 2
    paired = lax.axis_size("leaf") == 4 and rows_local == 2 * width and len(row_digits()) == 1
    mask = block_mask[0].astype(jnp.float32)
    half = columns // 2

    def masked(slot, value):
        blocks = value.reshape(block_count, rows_local // block_count, value.shape[1])
        return (blocks * mask[slot][:, None, None]).reshape(value.shape)

    def halves(value):
        return jnp.where(core == 0, value[..., :half], value[..., half:])

    def other_half(value):
        return jnp.where(core == 0, value[..., half:], value[..., :half])

    rhs_chip = by_core(core, halves(rhs_local), core_swap(other_half(rhs_local)), 1)
    inverses = inv_sub[0]
    inverses_other, middle_other = core_swap(inverses), core_swap(panel_mid[0])
    inverse_first = by_core(core, inverses[0], inverses_other[0], 0)
    inverse_second = by_core(core, inverses[1], inverses_other[1], 0)
    middle = by_core(core, panel_mid[0], middle_other, 0)

    def both_halves(value):
        return by_core(core, value, core_swap(value), 1)

    def near_and_far(value):
        swapped = core_swap(value)
        far_is_mine = core == x_bit
        return jnp.where(far_is_mine, swapped, value), jnp.where(far_is_mine, value, swapped)

    block_mask = block_mask[0]
    gathered, inverse_first = gather_rows(rhs_chip[0], lower=True, filler=inverse_first)
    first = product(inverse_first, gathered)
    turned = lax.optimization_barrier(row_major(jnp.swapaxes(inverses, 1, 2)))
    first_all, (middle, inverse_second, turned) = gather_rows(
        first, filler=(middle, inverse_second, turned)
    )
    residual = rhs_chip[1] - product(middle, first_all)
    if paired:
        sides = near_and_far(first_all)
        upper = panel_forward(panel_anc, block_mask, 0, 0, y_bit, *sides)
        lower = panel_forward(panel_anc, block_mask, 0, 1, y_bit, *sides)
        gathered, upper = gather_rows(residual, lower=True, filler=upper)
        second = product(inverse_second, gathered)
        second_all, lower = gather_rows(second, filler=lower)
        sides = near_and_far(second_all)
        lower = panel_forward(panel_anc, block_mask, 1, 1, y_bit, *sides, lower)
        upper = panel_forward(panel_anc, block_mask, 1, 0, y_bit, *sides, upper)
    else:
        gathered, _ = gather_rows(residual, lower=True)
        second = product(inverse_second, gathered)
        update = masked(0, product(panel_anc[0, 0], both_halves(first_all)))
        second_all, _ = gather_rows(second)
        update = update + masked(1, product(panel_anc[0, 1], both_halves(second_all)))

    *inner_digits, (size, stride) = row_digits()
    turned, second_all = lax.optimization_barrier((turned, second_all))
    block = turned
    for inner_size, inner_stride in inner_digits:
        block = jnp.concatenate(gather_join(block, *gather_both(block, inner_size, inner_stride), inner_size, inner_stride), 2)
    received = gather_near(block, size, stride)

    def whole_inverses(received, passed):
        joined = gather_join(block, received, passed, size, stride, ordered=False)
        mine = [jnp.concatenate([part[slot] for part in joined], 1) for slot in range(2)]
        return [(value, core_swap(value)) for value in mine]

    if paired:
        inverse_anc = jnp.where(y_bit == 0, inv_anc[:width], inv_anc[width:])
        own = jnp.where(y_bit == 0, rhs_anc[:width], rhs_anc[width:])
        own = jnp.where(x_bit == 0, own[:, :half], own[:, half:])
        total, received = leaf_reduce(upper, lower, received)
        passed = gather_far(received, size, stride)
        turned_anc = row_major(jnp.swapaxes(lax.optimization_barrier(inverse_anc), 0, 1))
        total, inverse_anc, turned_anc = lax.optimization_barrier(
            (own - total, inverse_anc, turned_anc)
        )
        forward = lax.optimization_barrier(product(inverse_anc, total))
        solved = row_major(product(turned_anc, forward))
        bits = jnp.stack([y_bit, x_bit == core, *block_order(size, stride)], dtype=jnp.int32)

        def begun(upper, lower):
            sums = []
            for slot in range(2):
                sums.append(panel_backward(panel_anc, block_mask, slot, 0, bits, upper, lower))
            return sums

        pieces, sums, wholes = leaf_gather(
            solved, passed, lambda passed: whole_inverses(received, passed), begun
        )
        x_anc = in_order(pieces, x_bit, y_bit)
    else:
        wholes = whole_inverses(received, gather_far(received, size, stride))
        total = lax.psum_scatter(update, "leaf", scatter_dimension=1, tiled=True)
        share = total.shape[1]
        own = lax.dynamic_slice_in_dim(rhs_anc, leaf * share, share, 1)
        x_anc = lax.all_gather(ancestor_solve(inv_anc, own - total), "leaf", axis=1, tiled=True)
        pieces = x_anc

    rows_chip = 2 * rows_own

    def chip_sum(slot, rhs, pieces):
        if paired:
            keep, send = panel_backward(
                panel_anc, block_mask, slot, 1, bits, pieces[1], pieces[3], (*sums[slot], rhs)
            )
            return keep + core_swap(send)
        keep, send = (
            transposed(panel_anc[0, slot], masked(slot, part))
            for part in (halves(pieces), other_half(pieces))
        )
        value = keep + core_swap(send)
        start = row_index // 2 * rows_chip
        own = lax.dynamic_slice_in_dim(value, start, rows_chip, 0) - rhs
        value = lax.dynamic_update_slice_in_dim(value, own, start, 0)
        return jnp.concatenate(sending_order(value, size, stride), 0)

    def partial_solve(slot, value):
        cores = value.reshape(-1, 2, rows_own, half)
        first = jnp.where(core == 0, cores[:, 0], cores[:, 1]).reshape(-1, half)
        last = jnp.where(core == 0, cores[:, 1], cores[:, 0]).reshape(-1, half)
        first, last = lax.optimization_barrier((first, last))
        return product(wholes[slot][0], first) + product(wholes[slot][1], last)

    middle_columns = jnp.concatenate(
        [
            lax.dynamic_slice_in_dim(middle, k * (width // size), width // size, 1)
            for k in block_order(size, stride)
        ],
        1,
    )
    second_partial = partial_solve(1, chip_sum(1, second, pieces))
    second_partial, pieces = lax.optimization_barrier((second_partial, pieces))
    first_sum = chip_sum(0, first, pieces)
    second_total, first_sum = reduce_rows(second_partial, filler=(first_sum, middle_columns))
    first_sum, middle_columns = first_sum
    x_second = -second_total
    first_partial = partial_solve(0, first_sum + transposed(middle_columns, x_second))
    first_total, x_anc = reduce_rows(first_partial, filler=x_anc)
    x_first = -first_total

    both = jnp.stack([x_first, x_second])
    keep = jnp.where(core == 0, both[:, :rows_own], both[:, rows_own:])
    send = jnp.where(core == 0, both[:, rows_own:], both[:, :rows_own])
    x_sub = by_core(core, keep, core_swap(send), 2)
    return x_sub[None], x_anc


def solution(mesh):
    return jax.shard_map(
        solve,
        mesh=mesh,
        in_specs=(
            P("leaf", None, "row", None),
            P("row", None),
            P("leaf", None, "row", None),
            P("leaf", "row", None),
            P("leaf", None, "row", None),
            P("leaf", None, "row"),
            P("row", None),
        ),
        out_specs=(P("leaf", None, "row", None), P("row", None)),
        check_vma=False,
    )
```

```python
import functools

import jax
import jax.numpy as jnp
from jax import lax
from jax.experimental import pallas as pl
from jax.experimental.layout import Layout, with_layout_constraint
from jax.experimental.pallas import tpu as pltpu
from jax.sharding import PartitionSpec as P


PRECISION = lax.Precision.HIGH


def product(left, right):
    return jnp.dot(left, right, precision=PRECISION, preferred_element_type=jnp.float32)


def transposed(left, right):
    return lax.dot_general(
        left,
        right,
        (((0,), (0,)), ((), ())),
        precision=PRECISION,
        preferred_element_type=jnp.float32,
    )


def row_major(value):
    return with_layout_constraint(value, Layout(tuple(range(value.ndim))))


def core_swap(value):
    count = lax.axis_size("row")
    return lax.ppermute(value, "row", [(r, r ^ 1) for r in range(count)])


def leaf_swap(value, mask):
    count = lax.axis_size("leaf")
    return lax.ppermute(value, "leaf", [(g, g ^ mask) for g in range(count)])


def chip_digits(chips):
    digits, stride = [], 1
    while chips > 1:
        size = 4 if chips % 4 == 0 else 2
        digits.append((size, stride))
        stride *= size
        chips //= size
    return digits


def digit_permute(value, size, stride, moves):
    target = dict(moves)
    pairs = []
    for r in range(lax.axis_size("row")):
        digit = (r // 2) // stride % size
        if digit in target:
            pairs.append((r, r + 2 * stride * (target[digit] - digit)))
    return lax.ppermute(value, "row", pairs)


def digit_index(size, stride):
    return lax.axis_index("row") // 2 // stride % size


def after(values, filler):
    return lax.optimization_barrier((*values, filler))


def gather_near(value, size, stride, lower=False):
    def moves(pairs):
        return [(a, b) for a, b in pairs if a < b] if lower else pairs

    if size == 2:
        return (digit_permute(value, size, stride, moves([(0, 1), (1, 0)])),)
    near = digit_permute(value, size, stride, moves([(0, 1), (1, 0), (2, 3), (3, 2)]))
    inner = digit_permute(value, size, stride, moves([(1, 2), (2, 1)]))
    return near, inner


def gather_far(received, size, stride, lower=False):
    def moves(pairs):
        return [(a, b) for a, b in pairs if a < b] if lower else pairs

    if size == 2:
        return ()
    near, inner = received
    relay = digit_permute(near, size, stride, moves([(1, 2), (2, 1)]))
    far = digit_permute(near, size, stride, moves([(1, 3), (2, 0)]))
    outer = digit_permute(inner, size, stride, moves([(1, 0), (2, 3)]))
    return relay, far, outer


def gather_join(value, received, passed, size, stride, ordered=True):
    me = digit_index(size, stride)
    if size == 2:
        (near,) = received
        if not ordered:
            return [near, value]
        return [jnp.where(me == 0, value, near), jnp.where(me == 0, near, value)]
    near, inner = received
    relay, far, outer = passed
    middle = (me == 1) | (me == 2)
    third = jnp.where(middle, inner, outer)
    fourth = jnp.where(middle, relay, far)
    odd = me % 2 == 1
    if not ordered:
        return [fourth, third, near, value]
    even_one = jnp.where(odd, near, value)
    odd_one = jnp.where(odd, value, near)
    high = me >= 2
    return [
        jnp.where(high, fourth, even_one),
        jnp.where(high, third, odd_one),
        jnp.where(high, even_one, third),
        jnp.where(high, odd_one, fourth),
    ]


def gather_both(value, size, stride):
    received = gather_near(value, size, stride)
    return received, gather_far(received, size, stride)


def gather_digit(value, size, stride, lower, filler):
    received = gather_near(value, size, stride, lower)
    passed = gather_far(received, size, stride, lower)
    last, filler = after((passed or received,), filler)
    received, passed = (received, last) if passed else (last, passed)
    return jnp.concatenate(gather_join(value, received, passed, size, stride), 0), filler


def block_order(size, stride):
    me = digit_index(size, stride)
    if size == 2:
        return 1 - me, me
    high = me >= 2
    return jnp.where(high, 0, 3), jnp.where(high, 1, 2), me ^ 1, me


def sending_order(value, size, stride):
    rows = value.shape[0] // size
    return [
        lax.dynamic_slice_in_dim(value, k * rows, rows, 0) for k in block_order(size, stride)
    ]


def reduce_digit(value, size, stride, lower, filler):
    def moves(pairs):
        return [(a, b) for a, b in pairs if a > b] if lower else pairs

    block = sending_order(value, size, stride)
    if size == 2:
        other = digit_permute(block[0], size, stride, moves([(0, 1), (1, 0)]))
        other, filler = after((other,), filler)
        return block[1] + other, filler
    far = digit_permute(block[0], size, stride, moves([(3, 1), (0, 2)]))
    relay = digit_permute(block[0], size, stride, moves([(2, 1), (1, 2)]))
    outer = digit_permute(block[1], size, stride, moves([(0, 1), (3, 2)]))
    far, relay, outer = lax.optimization_barrier((far, relay, outer))
    inner = digit_permute(block[1] + outer, size, stride, moves([(1, 2), (2, 1)]))
    near = digit_permute(block[2] + (far + relay), size, stride, moves([(0, 1), (1, 0), (2, 3), (3, 2)]))
    near, inner, filler = after((near, inner), filler)
    return block[3] + near + inner, filler


def gather_rows(value, lower=False, filler=()):
    digits = chip_digits(lax.axis_size("row") // 2)
    for place, (size, stride) in enumerate(digits):
        outermost = place == len(digits) - 1
        value, filler = gather_digit(value, size, stride, lower and outermost, filler)
    return value, filler


def row_digits():
    return chip_digits(lax.axis_size("row") // 2)


def reduce_rows(value, lower=False, filler=()):
    digits = row_digits()
    for place, (size, stride) in reversed(list(enumerate(digits))):
        outermost = place == len(digits) - 1
        value, filler = reduce_digit(value, size, stride, lower and outermost, filler)
    return value, filler


def by_core(core, mine, other, axis):
    return jnp.concatenate(
        [jnp.where(core == 0, mine, other), jnp.where(core == 0, other, mine)], axis
    )


def leaf_reduce(upper, lower, side):
    from_x = leaf_swap(upper[0], 1)
    from_y = leaf_swap(lower[0], 2)
    lower_kept, side = after((lower[1],), side)
    lower = (lower[0], lower_kept)
    from_x, from_y = lax.optimization_barrier((from_x, from_y))
    first, second = upper[1][0] + from_x[0], lower[1][0] + from_y[0]
    first, second = leaf_swap(first, 2), leaf_swap(second, 1)
    first, second = lax.optimization_barrier((first, second))
    return jnp.concatenate(
        [upper[1][1] + from_x[1] + first, lower[1][1] + from_y[1] + second], 0
    ), side


def leaf_gather(piece, side, finish, between):
    rows = piece.shape[0]
    first, second = piece[: rows // 2], piece[rows // 2 :]
    first_y = leaf_swap(first, 2)
    second_x = leaf_swap(second, 1)
    wholes = finish(side)
    first_y, second_x, wholes = lax.optimization_barrier((first_y, second_x, wholes))
    upper = jnp.stack([first, first_y])
    lower = jnp.stack([second, second_x])
    upper_far = leaf_swap(upper, 1)
    lower_far = leaf_swap(lower, 2)
    sums = between(upper, lower)
    upper_far, lower_far, sums = lax.optimization_barrier((upper_far, lower_far, sums))
    return (upper, upper_far, lower, lower_far), sums, wholes


def in_order(pieces, x_bit, y_bit):
    upper, upper_far, lower, lower_far = pieces

    def at(block, column):
        own_block, own_column = y_bit == block, x_bit == column
        return [
            jnp.where(
                own_column,
                jnp.where(own_block, upper[0], upper[1]),
                jnp.where(own_block, upper_far[0], upper_far[1]),
            ),
            jnp.where(
                own_block,
                jnp.where(own_column, lower[0], lower[1]),
                jnp.where(own_column, lower_far[0], lower_far[1]),
            ),
        ]

    return jnp.concatenate(
        [jnp.concatenate(at(0, column) + at(1, column), 0) for column in range(2)], 1
    )


def split(value):
    high = value.astype(jnp.bfloat16)
    return high, (value - high.astype(jnp.float32)).astype(jnp.bfloat16)


def scale_rows(value, mask_ref, slot, first_block, count):
    rows = value.shape[0] // count
    return jnp.concatenate(
        [
            value[k * rows : (k + 1) * rows] * mask_ref[slot, first_block + k].astype(jnp.float32)
            for k in range(count)
        ],
        0,
    )


def forward_kernel(slot, place, tiles, mask_blocks, bit_ref, mask_ref, panel_ref, near_ref, far_ref, *refs):
    prev, (out_first, out_last, high, low) = refs[:-4], refs[-4:]
    turn, step = pl.program_id(0), pl.program_id(1)
    columns = near_ref.shape[1]

    @pl.when((turn == 0) & (step == 0))
    def _():
        for k, ref in enumerate((near_ref, far_ref)):
            part = split(ref[...])
            high[:, k * columns : (k + 1) * columns] = part[0]
            low[:, k * columns : (k + 1) * columns] = part[1]

    panel_high, panel_low = split(panel_ref[...])

    def dot(left, right):
        return jnp.dot(left, right, preferred_element_type=jnp.float32)

    result = dot(panel_high, high[...]) + (dot(panel_high, low[...]) + dot(panel_low, high[...]))
    block = jnp.where(turn == 0, 1 - bit_ref[0], bit_ref[0])
    tile = (2 * block + place) * tiles + step
    result = scale_rows(result, mask_ref, slot, tile * mask_blocks, mask_blocks)
    near, far = result[:, :columns], result[:, columns:]
    if place == 0:
        out_first[...] = near + prev[0][...] if prev else near
        out_last[...] = far + prev[1][...] if prev else far
    else:

        @pl.when(turn == 0)
        def _():
            out_first[0] = near + prev[0][0] if prev else near
            out_first[1] = far + prev[0][1] if prev else far

        @pl.when(turn == 1)
        def _():
            out_last[0] = near + prev[1][0] if prev else near
            out_last[1] = far + prev[1][1] if prev else far


def panel_forward(panel_anc, mask, slot, place, y_bit, near, far, prev=(), tile_rows=256):
    rows_local, width = panel_anc.shape[2:]
    quarter = rows_local // 4
    tiles = quarter // tile_rows
    columns = near.shape[1]
    mask_blocks = mask.shape[1] // (4 * tiles)

    def panel_index(turn, step, bit_ref, mask_ref):
        block = jnp.where(turn == 0, 1 - bit_ref[0], bit_ref[0])
        return (0, slot, (2 * block + place) * tiles + step, 0)

    if place == 0:
        out_specs = [
            pl.BlockSpec((None, tile_rows, columns), lambda turn, step, *_: (turn, step, 0))
        ] * 2
    else:
        out_specs = [
            pl.BlockSpec(
                (2, tile_rows, columns),
                lambda turn, step, *_: (0, jnp.where(turn == 0, step, tiles - 1), 0),
            ),
            pl.BlockSpec(
                (2, tile_rows, columns), lambda turn, step, *_: (0, jnp.where(turn == 0, 0, step), 0)
            ),
        ]
    shape = jax.ShapeDtypeStruct((2, quarter, columns), jnp.float32)
    return pl.pallas_call(
        functools.partial(forward_kernel, slot, place, tiles, mask_blocks),
        out_shape=[shape, shape],
        grid_spec=pltpu.PrefetchScalarGridSpec(
            num_scalar_prefetch=2,
            grid=(2, tiles),
            in_specs=[
                pl.BlockSpec((None, None, tile_rows, width), panel_index),
                pl.BlockSpec(memory_space=pltpu.VMEM),
                pl.BlockSpec(memory_space=pltpu.VMEM),
                *(out_specs if prev else []),
            ],
            out_specs=out_specs,
            scratch_shapes=[pltpu.VMEM((width, 2 * columns), jnp.bfloat16)] * 2,
        ),
        cost_estimate=pl.CostEstimate(
            flops=12 * quarter * width * 2 * columns,
            bytes_accessed=4 * (2 * quarter * width + 2 * width * columns + 4 * quarter * columns),
            transcendentals=0,
        ),
    )(y_bit.reshape(1).astype(jnp.int32), mask, panel_anc, near, far, *prev)


def backward_kernel(slot, side, mask_blocks, bit_ref, mask_ref, panel_ref, upper_ref, lower_ref, *refs):
    prev, (out_first, out_last, panel_parts, value_parts, total) = refs[:-5], refs[-5:]
    if prev:
        *prev, rhs_ref = prev
    phase, step = pl.program_id(0), pl.program_id(1)
    rows = panel_ref.shape[0]
    columns = upper_ref.shape[2]
    tile = backward_quarter(side, phase, bit_ref) * pl.num_programs(1) + step

    def put(index, value):
        value = scale_rows(value, mask_ref, slot, tile * mask_blocks, mask_blocks)
        high, low = split(value)
        span = slice(index * columns, (index + 1) * columns)
        value_parts[0:rows, span] = high
        value_parts[rows : 2 * rows, span] = high
        value_parts[2 * rows : 3 * rows, span] = low

    high, low = split(panel_ref[...])
    panel_parts[0:rows] = high
    panel_parts[rows : 2 * rows] = low
    panel_parts[2 * rows : 3 * rows] = high

    def dot(right):
        return lax.dot_general(
            panel_parts[...], right, (((0,), (0,)), ((), ())), preferred_element_type=jnp.float32
        )

    near, far = slice(0, columns), slice(columns, 2 * columns)
    here = near if side == 0 else far

    @pl.when((phase == 0) & (step == 0))
    def _():
        if prev:
            total[:, near] = prev[0][...]
            total[:, far] = prev[1][...]
        else:
            total[...] = jnp.zeros_like(total)

    @pl.when(phase < 2)
    def _():
        put(0, upper_ref[0])
        total[:, here] += dot(value_parts[:, near])

    @pl.when(phase == 2)
    def _():
        put(0, lower_ref[0])
        put(1, lower_ref[1])
        total[...] += dot(value_parts[...])

    @pl.when((phase == 2) & (step == pl.num_programs(1) - 1))
    def _():
        if side == 0:
            out_first[...] = total[:, near]
            out_last[...] = total[:, far]
        else:
            length = rhs_ref.shape[0]
            count = total.shape[0] // length

            def put_out(kept, sent):
                for k in range(count):
                    source = pl.ds(pl.multiple_of(bit_ref[2 + k] * length, length), length)
                    place = slice(k * length, (k + 1) * length)
                    value = total[source, kept]
                    out_first[place] = value - rhs_ref[...] if k == count - 1 else value
                    out_last[place] = total[source, sent]

            pl.when(bit_ref[1] == 1)(functools.partial(put_out, near, far))
            pl.when(bit_ref[1] == 0)(functools.partial(put_out, far, near))


def backward_quarter(side, phase, bit_ref):
    own, other = bit_ref[0], 1 - bit_ref[0]
    lower = 2 * (own if side == 0 else other) + 1
    return jnp.where(phase == 0, 2 * own, jnp.where(phase == 1, 2 * other, lower))


def panel_backward(panel_anc, mask, slot, side, bits, upper, lower, prev=(), tile_rows=256):
    rows_local, width = panel_anc.shape[2:]
    quarter = rows_local // 4
    columns = upper.shape[2]
    tiles = quarter // tile_rows
    mask_blocks = mask.shape[1] // (4 * tiles)

    def panel_index(phase, step, bit_ref, mask_ref):
        return (0, slot, backward_quarter(side, phase, bit_ref) * tiles + step, 0)

    def upper_index(phase, step, *_):
        return (jnp.minimum(phase, 1), jnp.where(phase < 2, step, tiles - 1), 0)

    def lower_index(phase, step, *_):
        return (0, jnp.where(phase < 2, 0, step), 0)

    out_spec = pl.BlockSpec((width, columns), lambda *_: (0, 0))
    shape = jax.ShapeDtypeStruct((width, columns), jnp.float32)
    return pl.pallas_call(
        functools.partial(backward_kernel, slot, side, mask_blocks),
        out_shape=[shape, shape],
        grid_spec=pltpu.PrefetchScalarGridSpec(
            num_scalar_prefetch=2,
            grid=(3, tiles),
            in_specs=[
                pl.BlockSpec((None, None, tile_rows, width), panel_index),
                pl.BlockSpec((1, tile_rows, columns), upper_index),
                pl.BlockSpec((2, tile_rows, columns), lower_index),
                *[pl.BlockSpec(value.shape, lambda *_: (0, 0)) for value in prev],
            ],
            out_specs=[out_spec, out_spec],
            scratch_shapes=[
                pltpu.VMEM((3 * tile_rows, width), jnp.bfloat16),
                pltpu.VMEM((3 * tile_rows, 2 * columns), jnp.bfloat16),
                pltpu.VMEM((width, 2 * columns), jnp.float32),
            ],
        ),
        cost_estimate=pl.CostEstimate(
            flops=6 * 4 * quarter * width * columns,
            bytes_accessed=4 * (3 * quarter * width + 4 * quarter * columns + 4 * width * columns),
            transcendentals=0,
        ),
    )(bits, mask, panel_anc, upper, lower, *prev)


def from_partner(value, axis, bit):
    mask = 2**bit
    pairs = [(source, source ^ mask) for source in range(lax.axis_size(axis))]
    return lax.ppermute(value, axis, pairs)


def ancestor_solve(inverse_rows, values):
    rows_local, width = inverse_rows.shape
    if rows_local >= width:
        blocks = inverse_rows.reshape(rows_local // width, width, width)
        grouped = values.reshape(rows_local // width, width, values.shape[1])
        forward = jnp.einsum("kij,kjr->kir", blocks, grouped, precision=PRECISION)
        result = jnp.einsum("kji,kjr->kir", blocks, forward, precision=PRECISION)
        return result.reshape(rows_local, values.shape[1])
    row_index = lax.axis_index("row")
    levels = (width // rows_local).bit_length() - 1
    whole = values
    for bit_number in range(levels):
        other = from_partner(whole, "row", bit_number)
        upper = row_index >> bit_number & 1
        whole = jnp.where(
            upper == 1, jnp.concatenate([other, whole], 0), jnp.concatenate([whole, other], 0)
        )
    forward = product(inverse_rows, whole)
    partial_value = transposed(inverse_rows, forward)
    for bit_number in reversed(range(levels)):
        half = partial_value.shape[0] // 2
        upper = row_index >> bit_number & 1
        keep = jnp.where(upper == 1, partial_value[half:], partial_value[:half])
        outgoing = jnp.where(upper == 1, partial_value[:half], partial_value[half:])
        partial_value = keep + from_partner(outgoing, "row", bit_number)
    return partial_value


def solve(rhs_sub, rhs_anc, inv_sub, panel_mid, panel_anc, block_mask, inv_anc):
    rhs_local = rhs_sub[0]
    rows_local = panel_anc.shape[2]
    width = panel_anc.shape[3]
    rows_own = rhs_local.shape[1]
    columns = rhs_local.shape[2]
    block_count = block_mask.shape[2]
    row_index = lax.axis_index("row")
    core = row_index % 2
    leaf = lax.axis_index("leaf")
    x_bit, y_bit = leaf % 2, leaf // 2
    paired = lax.axis_size("leaf") == 4 and rows_local == 2 * width and len(row_digits()) == 1
    mask = block_mask[0].astype(jnp.float32)
    half = columns // 2

    def masked(slot, value):
        blocks = value.reshape(block_count, rows_local // block_count, value.shape[1])
        return (blocks * mask[slot][:, None, None]).reshape(value.shape)

    def halves(value):
        return jnp.where(core == 0, value[..., :half], value[..., half:])

    def other_half(value):
        return jnp.where(core == 0, value[..., half:], value[..., :half])

    rhs_chip = by_core(core, halves(rhs_local), core_swap(other_half(rhs_local)), 1)
    inverses = inv_sub[0]
    inverses_other, middle_other = core_swap(inverses), core_swap(panel_mid[0])
    inverse_first = by_core(core, inverses[0], inverses_other[0], 0)
    inverse_second = by_core(core, inverses[1], inverses_other[1], 0)
    middle = by_core(core, panel_mid[0], middle_other, 0)

    def both_halves(value):
        return by_core(core, value, core_swap(value), 1)

    def near_and_far(value):
        swapped = core_swap(value)
        far_is_mine = core == x_bit
        return jnp.where(far_is_mine, swapped, value), jnp.where(far_is_mine, value, swapped)

    block_mask = block_mask[0]
    gathered, inverse_first = gather_rows(rhs_chip[0], lower=True, filler=inverse_first)
    first = product(inverse_first, gathered)
    first, turned = lax.optimization_barrier((first, inverses))
    turned = lax.optimization_barrier(row_major(jnp.swapaxes(turned, 1, 2)))
    first_all, (middle, inverse_second, turned) = gather_rows(
        first, filler=(middle, inverse_second, turned)
    )
    residual = rhs_chip[1] - product(middle, first_all)
    if paired:
        sides = near_and_far(first_all)
        upper = panel_forward(panel_anc, block_mask, 0, 0, y_bit, *sides)
        lower = panel_forward(panel_anc, block_mask, 0, 1, y_bit, *sides)
        gathered, upper = gather_rows(residual, lower=True, filler=upper)
        second = product(inverse_second, gathered)
        second_all, lower = gather_rows(second, filler=lower)
        sides = near_and_far(second_all)
        lower = panel_forward(panel_anc, block_mask, 1, 1, y_bit, *sides, lower)
        upper = panel_forward(panel_anc, block_mask, 1, 0, y_bit, *sides, upper)
    else:
        gathered, _ = gather_rows(residual, lower=True)
        second = product(inverse_second, gathered)
        update = masked(0, product(panel_anc[0, 0], both_halves(first_all)))
        second_all, _ = gather_rows(second)
        update = update + masked(1, product(panel_anc[0, 1], both_halves(second_all)))

    *inner_digits, (size, stride) = row_digits()
    turned, second_all = lax.optimization_barrier((turned, second_all))
    block = turned
    for inner_size, inner_stride in inner_digits:
        block = jnp.concatenate(gather_join(block, *gather_both(block, inner_size, inner_stride), inner_size, inner_stride), 2)
    received = gather_near(block, size, stride)

    def whole_inverses(received, passed):
        joined = gather_join(block, received, passed, size, stride, ordered=False)
        mine = [jnp.concatenate([part[slot] for part in joined], 1) for slot in range(2)]
        return [(value, core_swap(value)) for value in mine]

    if paired:
        inverse_anc = jnp.where(y_bit == 0, inv_anc[:width], inv_anc[width:])
        own = jnp.where(y_bit == 0, rhs_anc[:width], rhs_anc[width:])
        own = jnp.where(x_bit == 0, own[:, :half], own[:, half:])
        total, received = leaf_reduce(upper, lower, received)
        passed = gather_far(received, size, stride)
        total, inverse_anc = lax.optimization_barrier((own - total, inverse_anc))
        forward = lax.optimization_barrier(product(inverse_anc, total))
        solved = row_major(transposed(inverse_anc, forward))
        bits = jnp.stack([y_bit, x_bit == core, *block_order(size, stride)], dtype=jnp.int32)

        def begun(upper, lower):
            sums = []
            for slot in range(2):
                sums.append(panel_backward(panel_anc, block_mask, slot, 0, bits, upper, lower))
            return sums

        pieces, sums, wholes = leaf_gather(
            solved, passed, lambda passed: whole_inverses(received, passed), begun
        )
        x_anc = in_order(pieces, x_bit, y_bit)
    else:
        wholes = whole_inverses(received, gather_far(received, size, stride))
        total = lax.psum_scatter(update, "leaf", scatter_dimension=1, tiled=True)
        share = total.shape[1]
        own = lax.dynamic_slice_in_dim(rhs_anc, leaf * share, share, 1)
        x_anc = lax.all_gather(ancestor_solve(inv_anc, own - total), "leaf", axis=1, tiled=True)
        pieces = x_anc

    rows_chip = 2 * rows_own

    def chip_sum(slot, rhs, pieces):
        if paired:
            keep, send = panel_backward(
                panel_anc, block_mask, slot, 1, bits, pieces[1], pieces[3], (*sums[slot], rhs)
            )
            return keep + core_swap(send)
        keep, send = (
            transposed(panel_anc[0, slot], masked(slot, part))
            for part in (halves(pieces), other_half(pieces))
        )
        value = keep + core_swap(send)
        start = row_index // 2 * rows_chip
        own = lax.dynamic_slice_in_dim(value, start, rows_chip, 0) - rhs
        value = lax.dynamic_update_slice_in_dim(value, own, start, 0)
        return jnp.concatenate(sending_order(value, size, stride), 0)

    def partial_solve(slot, value):
        cores = value.reshape(-1, 2, rows_own, half)
        first = jnp.where(core == 0, cores[:, 0], cores[:, 1]).reshape(-1, half)
        last = jnp.where(core == 0, cores[:, 1], cores[:, 0]).reshape(-1, half)
        first, last = lax.optimization_barrier((first, last))
        return product(wholes[slot][0], first) + product(wholes[slot][1], last)

    middle_columns = jnp.concatenate(
        [
            lax.dynamic_slice_in_dim(middle, k * (width // size), width // size, 1)
            for k in block_order(size, stride)
        ],
        1,
    )
    second_partial = partial_solve(1, chip_sum(1, second, pieces))
    second_partial, pieces = lax.optimization_barrier((second_partial, pieces))
    first_sum = chip_sum(0, first, pieces)
    second_total, first_sum = reduce_rows(second_partial, filler=(first_sum, middle_columns))
    first_sum, middle_columns = first_sum
    x_second = -second_total
    first_partial = partial_solve(0, first_sum + transposed(middle_columns, x_second))
    first_total, x_anc = reduce_rows(first_partial, filler=x_anc)
    x_first = -first_total

    both = jnp.stack([x_first, x_second])
    keep = jnp.where(core == 0, both[:, :rows_own], both[:, rows_own:])
    send = jnp.where(core == 0, both[:, rows_own:], both[:, :rows_own])
    x_sub = by_core(core, keep, core_swap(send), 2)
    return x_sub[None], x_anc


def solution(mesh):
    return jax.shard_map(
        solve,
        mesh=mesh,
        in_specs=(
            P("leaf", None, "row", None),
            P("row", None),
            P("leaf", None, "row", None),
            P("leaf", "row", None),
            P("leaf", None, "row", None),
            P("leaf", None, "row"),
            P("row", None),
        ),
        out_specs=(P("leaf", None, "row", None), P("row", None)),
        check_vma=False,
    )
```

```python
import functools

import jax
import jax.numpy as jnp
from jax import lax
from jax.experimental import pallas as pl
from jax.experimental.layout import Layout, with_layout_constraint
from jax.experimental.pallas import tpu as pltpu
from jax.sharding import PartitionSpec as P


PRECISION = lax.Precision.HIGH


def product(left, right):
    return jnp.dot(left, right, precision=PRECISION, preferred_element_type=jnp.float32)


def transposed(left, right):
    return lax.dot_general(
        left,
        right,
        (((0,), (0,)), ((), ())),
        precision=PRECISION,
        preferred_element_type=jnp.float32,
    )


def row_major(value):
    return with_layout_constraint(value, Layout(tuple(range(value.ndim))))


def core_swap(value):
    count = lax.axis_size("row")
    return lax.ppermute(value, "row", [(r, r ^ 1) for r in range(count)])


def leaf_swap(value, mask):
    count = lax.axis_size("leaf")
    return lax.ppermute(value, "leaf", [(g, g ^ mask) for g in range(count)])


def chip_digits(chips):
    digits, stride = [], 1
    while chips > 1:
        size = 4 if chips % 4 == 0 else 2
        digits.append((size, stride))
        stride *= size
        chips //= size
    return digits


def digit_permute(value, size, stride, moves):
    target = dict(moves)
    pairs = []
    for r in range(lax.axis_size("row")):
        digit = (r // 2) // stride % size
        if digit in target:
            pairs.append((r, r + 2 * stride * (target[digit] - digit)))
    return lax.ppermute(value, "row", pairs)


def digit_index(size, stride):
    return lax.axis_index("row") // 2 // stride % size


def after(values, filler):
    return lax.optimization_barrier((*values, filler))


def gather_near(value, size, stride, lower=False):
    def moves(pairs):
        return [(a, b) for a, b in pairs if a < b] if lower else pairs

    if size == 2:
        return (digit_permute(value, size, stride, moves([(0, 1), (1, 0)])),)
    near = digit_permute(value, size, stride, moves([(0, 1), (1, 0), (2, 3), (3, 2)]))
    inner = digit_permute(value, size, stride, moves([(1, 2), (2, 1)]))
    return near, inner


def gather_far(received, size, stride, lower=False):
    def moves(pairs):
        return [(a, b) for a, b in pairs if a < b] if lower else pairs

    if size == 2:
        return ()
    near, inner = received
    relay = digit_permute(near, size, stride, moves([(1, 2), (2, 1)]))
    far = digit_permute(near, size, stride, moves([(1, 3), (2, 0)]))
    outer = digit_permute(inner, size, stride, moves([(1, 0), (2, 3)]))
    return relay, far, outer


def gather_join(value, received, passed, size, stride, ordered=True):
    me = digit_index(size, stride)
    if size == 2:
        (near,) = received
        if not ordered:
            return [near, value]
        return [jnp.where(me == 0, value, near), jnp.where(me == 0, near, value)]
    near, inner = received
    relay, far, outer = passed
    middle = (me == 1) | (me == 2)
    third = jnp.where(middle, inner, outer)
    fourth = jnp.where(middle, relay, far)
    odd = me % 2 == 1
    if not ordered:
        return [fourth, third, near, value]
    even_one = jnp.where(odd, near, value)
    odd_one = jnp.where(odd, value, near)
    high = me >= 2
    return [
        jnp.where(high, fourth, even_one),
        jnp.where(high, third, odd_one),
        jnp.where(high, even_one, third),
        jnp.where(high, odd_one, fourth),
    ]


def gather_both(value, size, stride):
    received = gather_near(value, size, stride)
    return received, gather_far(received, size, stride)


def gather_digit(value, size, stride, lower, filler):
    received = gather_near(value, size, stride, lower)
    passed = gather_far(received, size, stride, lower)
    last, filler = after((passed or received,), filler)
    received, passed = (received, last) if passed else (last, passed)
    return jnp.concatenate(gather_join(value, received, passed, size, stride), 0), filler


def block_order(size, stride):
    me = digit_index(size, stride)
    if size == 2:
        return 1 - me, me
    high = me >= 2
    return jnp.where(high, 0, 3), jnp.where(high, 1, 2), me ^ 1, me


def sending_order(value, size, stride):
    rows = value.shape[0] // size
    return [
        lax.dynamic_slice_in_dim(value, k * rows, rows, 0) for k in block_order(size, stride)
    ]


def reduce_digit(value, size, stride, lower, filler):
    def moves(pairs):
        return [(a, b) for a, b in pairs if a > b] if lower else pairs

    block = sending_order(value, size, stride)
    if size == 2:
        other = digit_permute(block[0], size, stride, moves([(0, 1), (1, 0)]))
        other, filler = after((other,), filler)
        return block[1] + other, filler
    far = digit_permute(block[0], size, stride, moves([(3, 1), (0, 2)]))
    relay = digit_permute(block[0], size, stride, moves([(2, 1), (1, 2)]))
    outer = digit_permute(block[1], size, stride, moves([(0, 1), (3, 2)]))
    far, relay, outer = lax.optimization_barrier((far, relay, outer))
    inner = digit_permute(block[1] + outer, size, stride, moves([(1, 2), (2, 1)]))
    near = digit_permute(block[2] + (far + relay), size, stride, moves([(0, 1), (1, 0), (2, 3), (3, 2)]))
    near, inner, filler = after((near, inner), filler)
    return block[3] + near + inner, filler


def gather_rows(value, lower=False, filler=()):
    digits = chip_digits(lax.axis_size("row") // 2)
    for place, (size, stride) in enumerate(digits):
        outermost = place == len(digits) - 1
        value, filler = gather_digit(value, size, stride, lower and outermost, filler)
    return value, filler


def row_digits():
    return chip_digits(lax.axis_size("row") // 2)


def reduce_rows(value, lower=False, filler=()):
    digits = row_digits()
    for place, (size, stride) in reversed(list(enumerate(digits))):
        outermost = place == len(digits) - 1
        value, filler = reduce_digit(value, size, stride, lower and outermost, filler)
    return value, filler


def by_core(core, mine, other, axis):
    return jnp.concatenate(
        [jnp.where(core == 0, mine, other), jnp.where(core == 0, other, mine)], axis
    )


def leaf_reduce(uppers, lowers, side):
    arrived, turned, kept = [], [], []
    for upper, lower in zip(uppers, lowers):
        from_x = leaf_swap(upper[0], 1)
        from_y = leaf_swap(lower[0], 2)
        arrived.append((from_x, from_y))
        kept.append((upper[1], lower[1]))
    kept[-1], side = lax.optimization_barrier((kept[-1], side))
    for chunk, (upper, lower) in enumerate(kept):
        from_x, from_y = arrived[chunk] = lax.optimization_barrier(arrived[chunk])
        first, second = upper[0] + from_x[0], lower[0] + from_y[0]
        turned.append((leaf_swap(first, 2), leaf_swap(second, 1)))
    turned = lax.optimization_barrier(turned)
    totals = [
        jnp.concatenate([upper[1] + from_x[1] + first, lower[1] + from_y[1] + second], 0)
        for (upper, lower), (from_x, from_y), (first, second) in zip(kept, arrived, turned)
    ]
    return jnp.concatenate(totals, 1), side


def leaf_gather(piece, side, finish, between):
    rows = piece.shape[0]
    first, second = piece[: rows // 2], piece[rows // 2 :]
    first_y = leaf_swap(first, 2)
    second_x = leaf_swap(second, 1)
    first_y, second_x = lax.optimization_barrier((first_y, second_x))
    upper = jnp.stack([first, first_y])
    lower = jnp.stack([second, second_x])
    upper_far = leaf_swap(upper, 1)
    lower_far = leaf_swap(lower, 2)
    sums, wholes = between(upper, lower), finish(side)
    upper_far, lower_far, sums, wholes = lax.optimization_barrier(
        (upper_far, lower_far, sums, wholes)
    )
    return (upper, upper_far, lower, lower_far), sums, wholes


def in_order(pieces, x_bit, y_bit):
    upper, upper_far, lower, lower_far = pieces

    def at(block, column):
        own_block, own_column = y_bit == block, x_bit == column
        return [
            jnp.where(
                own_column,
                jnp.where(own_block, upper[0], upper[1]),
                jnp.where(own_block, upper_far[0], upper_far[1]),
            ),
            jnp.where(
                own_block,
                jnp.where(own_column, lower[0], lower[1]),
                jnp.where(own_column, lower_far[0], lower_far[1]),
            ),
        ]

    return jnp.concatenate(
        [jnp.concatenate(at(0, column) + at(1, column), 0) for column in range(2)], 1
    )


def split(value):
    high = value.astype(jnp.bfloat16)
    return high, (value - high.astype(jnp.float32)).astype(jnp.bfloat16)


def scale_rows(value, mask_ref, slot, first_block, count):
    rows = value.shape[0] // count
    return jnp.concatenate(
        [
            value[k * rows : (k + 1) * rows] * mask_ref[slot, first_block + k].astype(jnp.float32)
            for k in range(count)
        ],
        0,
    )


def forward_kernel(slot, place, tiles, mask_blocks, bit_ref, mask_ref, panel_ref, near_ref, far_ref, *refs):
    prev, (out_first, out_last, high, low) = refs[:-4], refs[-4:]
    turn, step = pl.program_id(0), pl.program_id(1)
    columns = near_ref.shape[1]

    @pl.when((turn == 0) & (step == 0))
    def _():
        for k, ref in enumerate((near_ref, far_ref)):
            part = split(ref[...])
            high[:, k * columns : (k + 1) * columns] = part[0]
            low[:, k * columns : (k + 1) * columns] = part[1]

    panel_high, panel_low = split(panel_ref[...])

    def dot(left, right):
        return jnp.dot(left, right, preferred_element_type=jnp.float32)

    result = dot(panel_high, high[...]) + (dot(panel_high, low[...]) + dot(panel_low, high[...]))
    block = jnp.where(turn == 0, 1 - bit_ref[0], bit_ref[0])
    tile = (2 * block + place) * tiles + step
    result = scale_rows(result, mask_ref, slot, tile * mask_blocks, mask_blocks)
    near, far = result[:, :columns], result[:, columns:]
    if place == 0:
        out_first[...] = near + prev[0][...] if prev else near
        out_last[...] = far + prev[1][...] if prev else far
    else:

        @pl.when(turn == 0)
        def _():
            out_first[0] = near + prev[0][0] if prev else near
            out_first[1] = far + prev[0][1] if prev else far

        @pl.when(turn == 1)
        def _():
            out_last[0] = near + prev[1][0] if prev else near
            out_last[1] = far + prev[1][1] if prev else far


def panel_forward(panel_anc, mask, slot, place, y_bit, near, far, prev=(), chunk=0, tile_rows=256):
    rows_local, width = panel_anc.shape[2:]
    quarter = rows_local // 4
    tiles = quarter // tile_rows
    columns = near.shape[1]
    mask_blocks = mask.shape[1] // (4 * tiles)

    def panel_index(turn, step, bit_ref, mask_ref):
        block = jnp.where(turn == 0, 1 - bit_ref[0], bit_ref[0])
        return (0, slot, (2 * block + place) * tiles + step, 0)


    def specs(part):
        if place == 0:
            return [
                pl.BlockSpec(
                    (None, tile_rows, columns), lambda turn, step, *_: (turn, step, part)
                )
            ] * 2
        return [
            pl.BlockSpec(
                (2, tile_rows, columns),
                lambda turn, step, *_: (0, jnp.where(turn == 0, step, tiles - 1), part),
            ),
            pl.BlockSpec(
                (2, tile_rows, columns),
                lambda turn, step, *_: (0, jnp.where(turn == 0, 0, step), part),
            ),
        ]

    shape = jax.ShapeDtypeStruct((2, quarter, columns), jnp.float32)
    return pl.pallas_call(
        functools.partial(forward_kernel, slot, place, tiles, mask_blocks),
        out_shape=[shape, shape],
        grid_spec=pltpu.PrefetchScalarGridSpec(
            num_scalar_prefetch=2,
            grid=(2, tiles),
            in_specs=[
                pl.BlockSpec((None, None, tile_rows, width), panel_index),
                pl.BlockSpec(memory_space=pltpu.VMEM),
                pl.BlockSpec(memory_space=pltpu.VMEM),
                *(specs(chunk) if prev else []),
            ],
            out_specs=specs(0),
            scratch_shapes=[pltpu.VMEM((width, 2 * columns), jnp.bfloat16)] * 2,
        ),
        cost_estimate=pl.CostEstimate(
            flops=12 * quarter * width * 2 * columns,
            bytes_accessed=4 * (2 * quarter * width + 2 * width * columns + 4 * quarter * columns),
            transcendentals=0,
        ),
    )(y_bit.reshape(1).astype(jnp.int32), mask, panel_anc, near, far, *prev)


def backward_kernel(slot, side, mask_blocks, bit_ref, mask_ref, panel_ref, upper_ref, lower_ref, *refs):
    prev, (out_first, out_last, panel_parts, value_parts, total) = refs[:-5], refs[-5:]
    if prev:
        *prev, rhs_ref = prev
    phase, step = pl.program_id(0), pl.program_id(1)
    rows = panel_ref.shape[0]
    columns = upper_ref.shape[2]
    tile = backward_quarter(side, phase, bit_ref) * pl.num_programs(1) + step

    def put(index, value):
        value = scale_rows(value, mask_ref, slot, tile * mask_blocks, mask_blocks)
        high, low = split(value)
        span = slice(index * columns, (index + 1) * columns)
        value_parts[0:rows, span] = high
        value_parts[rows : 2 * rows, span] = high
        value_parts[2 * rows : 3 * rows, span] = low

    high, low = split(panel_ref[...])
    panel_parts[0:rows] = high
    panel_parts[rows : 2 * rows] = low
    panel_parts[2 * rows : 3 * rows] = high

    def dot(right):
        return lax.dot_general(
            panel_parts[...], right, (((0,), (0,)), ((), ())), preferred_element_type=jnp.float32
        )

    near, far = slice(0, columns), slice(columns, 2 * columns)
    here = near if side == 0 else far

    @pl.when((phase == 0) & (step == 0))
    def _():
        if prev:
            total[:, near] = prev[0][...]
            total[:, far] = prev[1][...]
        else:
            total[...] = jnp.zeros_like(total)

    @pl.when(phase < 2)
    def _():
        put(0, upper_ref[0])
        total[:, here] += dot(value_parts[:, near])

    @pl.when(phase == 2)
    def _():
        put(0, lower_ref[0])
        put(1, lower_ref[1])
        total[...] += dot(value_parts[...])

    @pl.when((phase == 2) & (step == pl.num_programs(1) - 1))
    def _():
        if side == 0:
            out_first[...] = total[:, near]
            out_last[...] = total[:, far]
        else:
            length = rhs_ref.shape[0]
            count = total.shape[0] // length

            def put_out(kept, sent):
                for k in range(count):
                    source = pl.ds(pl.multiple_of(bit_ref[2 + k] * length, length), length)
                    place = slice(k * length, (k + 1) * length)
                    value = total[source, kept]
                    out_first[place] = value - rhs_ref[...] if k == count - 1 else value
                    out_last[place] = total[source, sent]

            pl.when(bit_ref[1] == 1)(functools.partial(put_out, near, far))
            pl.when(bit_ref[1] == 0)(functools.partial(put_out, far, near))


def backward_quarter(side, phase, bit_ref):
    own, other = bit_ref[0], 1 - bit_ref[0]
    lower = 2 * (own if side == 0 else other) + 1
    return jnp.where(phase == 0, 2 * own, jnp.where(phase == 1, 2 * other, lower))


def panel_backward(panel_anc, mask, slot, side, bits, upper, lower, prev=(), tile_rows=256):
    rows_local, width = panel_anc.shape[2:]
    quarter = rows_local // 4
    columns = upper.shape[2]
    tiles = quarter // tile_rows
    mask_blocks = mask.shape[1] // (4 * tiles)

    def panel_index(phase, step, bit_ref, mask_ref):
        return (0, slot, backward_quarter(side, phase, bit_ref) * tiles + step, 0)

    def upper_index(phase, step, *_):
        return (jnp.minimum(phase, 1), jnp.where(phase < 2, step, tiles - 1), 0)

    def lower_index(phase, step, *_):
        return (0, jnp.where(phase < 2, 0, step), 0)

    out_spec = pl.BlockSpec((width, columns), lambda *_: (0, 0))
    shape = jax.ShapeDtypeStruct((width, columns), jnp.float32)
    return pl.pallas_call(
        functools.partial(backward_kernel, slot, side, mask_blocks),
        out_shape=[shape, shape],
        grid_spec=pltpu.PrefetchScalarGridSpec(
            num_scalar_prefetch=2,
            grid=(3, tiles),
            in_specs=[
                pl.BlockSpec((None, None, tile_rows, width), panel_index),
                pl.BlockSpec((1, tile_rows, columns), upper_index),
                pl.BlockSpec((2, tile_rows, columns), lower_index),
                *[pl.BlockSpec(value.shape, lambda *_: (0, 0)) for value in prev],
            ],
            out_specs=[out_spec, out_spec],
            scratch_shapes=[
                pltpu.VMEM((3 * tile_rows, width), jnp.bfloat16),
                pltpu.VMEM((3 * tile_rows, 2 * columns), jnp.bfloat16),
                pltpu.VMEM((width, 2 * columns), jnp.float32),
            ],
        ),
        cost_estimate=pl.CostEstimate(
            flops=6 * 4 * quarter * width * columns,
            bytes_accessed=4 * (3 * quarter * width + 4 * quarter * columns + 4 * width * columns),
            transcendentals=0,
        ),
    )(bits, mask, panel_anc, upper, lower, *prev)


def from_partner(value, axis, bit):
    mask = 2**bit
    pairs = [(source, source ^ mask) for source in range(lax.axis_size(axis))]
    return lax.ppermute(value, axis, pairs)


def ancestor_solve(inverse_rows, values):
    rows_local, width = inverse_rows.shape
    if rows_local >= width:
        blocks = inverse_rows.reshape(rows_local // width, width, width)
        grouped = values.reshape(rows_local // width, width, values.shape[1])
        forward = jnp.einsum("kij,kjr->kir", blocks, grouped, precision=PRECISION)
        result = jnp.einsum("kji,kjr->kir", blocks, forward, precision=PRECISION)
        return result.reshape(rows_local, values.shape[1])
    row_index = lax.axis_index("row")
    levels = (width // rows_local).bit_length() - 1
    whole = values
    for bit_number in range(levels):
        other = from_partner(whole, "row", bit_number)
        upper = row_index >> bit_number & 1
        whole = jnp.where(
            upper == 1, jnp.concatenate([other, whole], 0), jnp.concatenate([whole, other], 0)
        )
    forward = product(inverse_rows, whole)
    partial_value = transposed(inverse_rows, forward)
    for bit_number in reversed(range(levels)):
        half = partial_value.shape[0] // 2
        upper = row_index >> bit_number & 1
        keep = jnp.where(upper == 1, partial_value[half:], partial_value[:half])
        outgoing = jnp.where(upper == 1, partial_value[:half], partial_value[half:])
        partial_value = keep + from_partner(outgoing, "row", bit_number)
    return partial_value


def solve(rhs_sub, rhs_anc, inv_sub, panel_mid, panel_anc, block_mask, inv_anc):
    rhs_local = rhs_sub[0]
    rows_local = panel_anc.shape[2]
    width = panel_anc.shape[3]
    rows_own = rhs_local.shape[1]
    columns = rhs_local.shape[2]
    block_count = block_mask.shape[2]
    row_index = lax.axis_index("row")
    core = row_index % 2
    leaf = lax.axis_index("leaf")
    x_bit, y_bit = leaf % 2, leaf // 2
    paired = lax.axis_size("leaf") == 4 and rows_local == 2 * width and len(row_digits()) == 1
    mask = block_mask[0].astype(jnp.float32)
    half = columns // 2

    def masked(slot, value):
        blocks = value.reshape(block_count, rows_local // block_count, value.shape[1])
        return (blocks * mask[slot][:, None, None]).reshape(value.shape)

    def halves(value):
        return jnp.where(core == 0, value[..., :half], value[..., half:])

    def other_half(value):
        return jnp.where(core == 0, value[..., half:], value[..., :half])

    rhs_chip = by_core(core, halves(rhs_local), core_swap(other_half(rhs_local)), 1)
    inverses = inv_sub[0]
    inverses_other, middle_other = core_swap(inverses), core_swap(panel_mid[0])
    inverse_first = by_core(core, inverses[0], inverses_other[0], 0)
    inverse_second = by_core(core, inverses[1], inverses_other[1], 0)
    middle = by_core(core, panel_mid[0], middle_other, 0)

    def both_halves(value):
        return by_core(core, value, core_swap(value), 1)

    def near_and_far(value):
        swapped = core_swap(value)
        far_is_mine = core == x_bit
        return jnp.where(far_is_mine, swapped, value), jnp.where(far_is_mine, value, swapped)

    block_mask = block_mask[0]
    gathered, inverse_first = gather_rows(rhs_chip[0], lower=True, filler=inverse_first)
    first = product(inverse_first, gathered)
    first, turned = lax.optimization_barrier((first, inverses))
    turned = lax.optimization_barrier(row_major(jnp.swapaxes(turned, 1, 2)))
    first_all, (middle, inverse_second, turned) = gather_rows(
        first, filler=(middle, inverse_second, turned)
    )
    residual = rhs_chip[1] - product(middle, first_all)
    if paired:
        sides = near_and_far(first_all)
        upper = panel_forward(panel_anc, block_mask, 0, 0, y_bit, *sides)
        lower = panel_forward(panel_anc, block_mask, 0, 1, y_bit, *sides)
        gathered, upper = gather_rows(residual, lower=True, filler=upper)
        second = product(inverse_second, gathered)
        chunks = range(2)
        part = half // 2
        digit = row_digits()[0]
        pieces = lax.optimization_barrier([second[:, c * part : (c + 1) * part] for c in chunks])
        received, passed, uppers, lowers = [], [], [], []
        for c in chunks:
            received.append(gather_near(pieces[c], *digit))
        for c in chunks:
            passed.append(gather_far(received[c], *digit))
        passed[0], lower = lax.optimization_barrier((passed[0], lower))
        for c in chunks:
            second_all = jnp.concatenate(gather_join(pieces[c], received[c], passed[c], *digit), 0)
            sides = near_and_far(second_all)
            lowers.append(
                panel_forward(panel_anc, block_mask, 1, 1, y_bit, *sides, lower, c)
            )
            uppers.append(
                panel_forward(panel_anc, block_mask, 1, 0, y_bit, *sides, upper, c)
            )
    else:
        gathered, _ = gather_rows(residual, lower=True)
        second = product(inverse_second, gathered)
        update = masked(0, product(panel_anc[0, 0], both_halves(first_all)))
        second_all, _ = gather_rows(second)
        update = update + masked(1, product(panel_anc[0, 1], both_halves(second_all)))

    *inner_digits, (size, stride) = row_digits()
    turned, second_all = lax.optimization_barrier((turned, second_all))
    block = turned
    for inner_size, inner_stride in inner_digits:
        block = jnp.concatenate(gather_join(block, *gather_both(block, inner_size, inner_stride), inner_size, inner_stride), 2)
    received = gather_near(block, size, stride)

    def whole_inverses(received, passed):
        joined = gather_join(block, received, passed, size, stride, ordered=False)
        mine = [jnp.concatenate([part[slot] for part in joined], 1) for slot in range(2)]
        return [(value, core_swap(value)) for value in mine]

    if paired:
        inverse_anc = jnp.where(y_bit == 0, inv_anc[:width], inv_anc[width:])
        own = jnp.where(y_bit == 0, rhs_anc[:width], rhs_anc[width:])
        own = jnp.where(x_bit == 0, own[:, :half], own[:, half:])
        total, received = leaf_reduce(uppers, lowers, received)
        passed = gather_far(received, size, stride)
        total, inverse_anc = lax.optimization_barrier((own - total, inverse_anc))
        forward = lax.optimization_barrier(product(inverse_anc, total))
        solved = row_major(transposed(inverse_anc, forward))
        bits = jnp.stack([y_bit, x_bit == core, *block_order(size, stride)], dtype=jnp.int32)

        def begun(upper, lower):
            sums = []
            for slot in range(2):
                sums.append(panel_backward(panel_anc, block_mask, slot, 0, bits, upper, lower))
            return sums

        pieces, sums, wholes = leaf_gather(
            solved, passed, lambda passed: whole_inverses(received, passed), begun
        )
        x_anc = in_order(pieces, x_bit, y_bit)
    else:
        wholes = whole_inverses(received, gather_far(received, size, stride))
        total = lax.psum_scatter(update, "leaf", scatter_dimension=1, tiled=True)
        share = total.shape[1]
        own = lax.dynamic_slice_in_dim(rhs_anc, leaf * share, share, 1)
        x_anc = lax.all_gather(ancestor_solve(inv_anc, own - total), "leaf", axis=1, tiled=True)
        pieces = x_anc

    rows_chip = 2 * rows_own

    def chip_sum(slot, rhs, pieces):
        if paired:
            keep, send = panel_backward(
                panel_anc, block_mask, slot, 1, bits, pieces[1], pieces[3], (*sums[slot], rhs)
            )
            return keep + core_swap(send)
        keep, send = (
            transposed(panel_anc[0, slot], masked(slot, part))
            for part in (halves(pieces), other_half(pieces))
        )
        value = keep + core_swap(send)
        start = row_index // 2 * rows_chip
        own = lax.dynamic_slice_in_dim(value, start, rows_chip, 0) - rhs
        value = lax.dynamic_update_slice_in_dim(value, own, start, 0)
        return jnp.concatenate(sending_order(value, size, stride), 0)

    def partial_solve(slot, value):
        cores = value.reshape(-1, 2, rows_own, half)
        first = jnp.where(core == 0, cores[:, 0], cores[:, 1]).reshape(-1, half)
        last = jnp.where(core == 0, cores[:, 1], cores[:, 0]).reshape(-1, half)
        first, last = lax.optimization_barrier((first, last))
        return product(wholes[slot][0], first) + product(wholes[slot][1], last)

    middle_columns = jnp.concatenate(
        [
            lax.dynamic_slice_in_dim(middle, k * (width // size), width // size, 1)
            for k in block_order(size, stride)
        ],
        1,
    )
    second_partial = partial_solve(1, chip_sum(1, second, pieces))
    second_partial, pieces = lax.optimization_barrier((second_partial, pieces))
    first_sum = chip_sum(0, first, pieces)
    second_total, first_sum = reduce_rows(second_partial, filler=(first_sum, middle_columns))
    first_sum, middle_columns = first_sum
    x_second = -second_total
    first_partial = partial_solve(0, first_sum + transposed(middle_columns, x_second))
    first_total, x_anc = reduce_rows(first_partial, filler=x_anc)
    x_first = -first_total

    both = jnp.stack([x_first, x_second])
    keep = jnp.where(core == 0, both[:, :rows_own], both[:, rows_own:])
    send = jnp.where(core == 0, both[:, rows_own:], both[:, :rows_own])
    x_sub = by_core(core, keep, core_swap(send), 2)
    return x_sub[None], x_anc


def solution(mesh):
    return jax.shard_map(
        solve,
        mesh=mesh,
        in_specs=(
            P("leaf", None, "row", None),
            P("row", None),
            P("leaf", None, "row", None),
            P("leaf", "row", None),
            P("leaf", None, "row", None),
            P("leaf", None, "row"),
            P("row", None),
        ),
        out_specs=(P("leaf", None, "row", None), P("row", None)),
        check_vma=False,
    )
```

```python
import functools

import jax
import jax.numpy as jnp
from jax import lax
from jax.experimental import pallas as pl
from jax.experimental.layout import Layout, with_layout_constraint
from jax.experimental.pallas import tpu as pltpu
from jax.sharding import PartitionSpec as P


PRECISION = lax.Precision.HIGH
VMEM_GRANT = 24 * 2**20


def product(left, right):
    return jnp.dot(left, right, precision=PRECISION, preferred_element_type=jnp.float32)


def transposed(left, right):
    return lax.dot_general(
        left,
        right,
        (((0,), (0,)), ((), ())),
        precision=PRECISION,
        preferred_element_type=jnp.float32,
    )


def row_major(value):
    return with_layout_constraint(value, Layout(tuple(range(value.ndim))))


def core_swap(value):
    count = lax.axis_size("row")
    return lax.ppermute(value, "row", [(r, r ^ 1) for r in range(count)])


def leaf_swap(value, mask):
    count = lax.axis_size("leaf")
    return lax.ppermute(value, "leaf", [(g, g ^ mask) for g in range(count)])


def chip_digits(chips):
    digits, stride = [], 1
    while chips > 1:
        size = 4 if chips % 4 == 0 else 2
        digits.append((size, stride))
        stride *= size
        chips //= size
    return digits


def digit_permute(value, size, stride, moves):
    target = dict(moves)
    pairs = []
    for r in range(lax.axis_size("row")):
        digit = (r // 2) // stride % size
        if digit in target:
            pairs.append((r, r + 2 * stride * (target[digit] - digit)))
    return lax.ppermute(value, "row", pairs)


def digit_index(size, stride):
    return lax.axis_index("row") // 2 // stride % size


def after(values, filler):
    return lax.optimization_barrier((*values, filler))


def gather_near(value, size, stride, lower=False):
    def moves(pairs):
        return [(a, b) for a, b in pairs if a < b] if lower else pairs

    if size == 2:
        return (digit_permute(value, size, stride, moves([(0, 1), (1, 0)])),)
    near = digit_permute(value, size, stride, moves([(0, 1), (1, 0), (2, 3), (3, 2)]))
    inner = digit_permute(value, size, stride, moves([(1, 2), (2, 1)]))
    return near, inner


def gather_far(received, size, stride, lower=False):
    def moves(pairs):
        return [(a, b) for a, b in pairs if a < b] if lower else pairs

    if size == 2:
        return ()
    near, inner = received
    relay = digit_permute(near, size, stride, moves([(1, 2), (2, 1)]))
    far = digit_permute(near, size, stride, moves([(1, 3), (2, 0)]))
    outer = digit_permute(inner, size, stride, moves([(1, 0), (2, 3)]))
    return relay, far, outer


def gather_join(value, received, passed, size, stride, ordered=True):
    me = digit_index(size, stride)
    if size == 2:
        (near,) = received
        if not ordered:
            return [near, value]
        return [jnp.where(me == 0, value, near), jnp.where(me == 0, near, value)]
    near, inner = received
    relay, far, outer = passed
    middle = (me == 1) | (me == 2)
    third = jnp.where(middle, inner, outer)
    fourth = jnp.where(middle, relay, far)
    odd = me % 2 == 1
    if not ordered:
        return [fourth, third, near, value]
    even_one = jnp.where(odd, near, value)
    odd_one = jnp.where(odd, value, near)
    high = me >= 2
    return [
        jnp.where(high, fourth, even_one),
        jnp.where(high, third, odd_one),
        jnp.where(high, even_one, third),
        jnp.where(high, odd_one, fourth),
    ]


def gather_both(value, size, stride):
    received = gather_near(value, size, stride)
    return received, gather_far(received, size, stride)


def gather_digit(value, size, stride, lower, filler):
    received = gather_near(value, size, stride, lower)
    passed = gather_far(received, size, stride, lower)
    last, filler = after((passed or received,), filler)
    received, passed = (received, last) if passed else (last, passed)
    return jnp.concatenate(gather_join(value, received, passed, size, stride), 0), filler


def block_order(size, stride):
    me = digit_index(size, stride)
    if size == 2:
        return 1 - me, me
    high = me >= 2
    return jnp.where(high, 0, 3), jnp.where(high, 1, 2), me ^ 1, me


def sending_order(value, size, stride):
    rows = value.shape[0] // size
    return [
        lax.dynamic_slice_in_dim(value, k * rows, rows, 0) for k in block_order(size, stride)
    ]


def reduce_digit(value, size, stride, lower, filler):
    def moves(pairs):
        return [(a, b) for a, b in pairs if a > b] if lower else pairs

    block = sending_order(value, size, stride)
    if size == 2:
        other = digit_permute(block[0], size, stride, moves([(0, 1), (1, 0)]))
        other, filler = after((other,), filler)
        return block[1] + other, filler
    far = digit_permute(block[0], size, stride, moves([(3, 1), (0, 2)]))
    relay = digit_permute(block[0], size, stride, moves([(2, 1), (1, 2)]))
    outer = digit_permute(block[1], size, stride, moves([(0, 1), (3, 2)]))
    far, relay, outer = lax.optimization_barrier((far, relay, outer))
    inner = digit_permute(block[1] + outer, size, stride, moves([(1, 2), (2, 1)]))
    near = digit_permute(block[2] + (far + relay), size, stride, moves([(0, 1), (1, 0), (2, 3), (3, 2)]))
    near, inner, filler = after((near, inner), filler)
    return block[3] + near + inner, filler


def gather_rows(value, lower=False, filler=()):
    digits = chip_digits(lax.axis_size("row") // 2)
    for place, (size, stride) in enumerate(digits):
        outermost = place == len(digits) - 1
        value, filler = gather_digit(value, size, stride, lower and outermost, filler)
    return value, filler


def row_digits():
    return chip_digits(lax.axis_size("row") // 2)


def reduce_rows(value, lower=False, filler=()):
    digits = row_digits()
    for place, (size, stride) in reversed(list(enumerate(digits))):
        outermost = place == len(digits) - 1
        value, filler = reduce_digit(value, size, stride, lower and outermost, filler)
    return value, filler


def by_core(core, mine, other, axis):
    return jnp.concatenate(
        [jnp.where(core == 0, mine, other), jnp.where(core == 0, other, mine)], axis
    )


def leaf_reduce(upper, lower, side):
    from_x = leaf_swap(upper[0], 1)
    from_y = leaf_swap(lower[0], 2)
    lower_kept, side = after((lower[1],), side)
    lower = (lower[0], lower_kept)
    from_x, from_y = lax.optimization_barrier((from_x, from_y))
    first, second = upper[1][0] + from_x[0], lower[1][0] + from_y[0]
    first, second = leaf_swap(first, 2), leaf_swap(second, 1)
    first, second = lax.optimization_barrier((first, second))
    return jnp.concatenate(
        [upper[1][1] + from_x[1] + first, lower[1][1] + from_y[1] + second], 0
    ), side


def leaf_gather(piece, side, finish, between):
    rows = piece.shape[0]
    first, second = piece[: rows // 2], piece[rows // 2 :]
    first_y = leaf_swap(first, 2)
    second_x = leaf_swap(second, 1)
    wholes = finish(side)
    first_y, second_x, wholes = lax.optimization_barrier((first_y, second_x, wholes))
    upper = jnp.stack([first, first_y])
    lower = jnp.stack([second, second_x])
    upper_far = leaf_swap(upper, 1)
    lower_far = leaf_swap(lower, 2)
    sums = between(upper, lower)
    upper_far, lower_far, sums = lax.optimization_barrier((upper_far, lower_far, sums))
    return (upper, upper_far, lower, lower_far), sums, wholes


def in_order(pieces, x_bit, y_bit):
    upper, upper_far, lower, lower_far = pieces

    def at(block, column):
        own_block, own_column = y_bit == block, x_bit == column
        return [
            jnp.where(
                own_column,
                jnp.where(own_block, upper[0], upper[1]),
                jnp.where(own_block, upper_far[0], upper_far[1]),
            ),
            jnp.where(
                own_block,
                jnp.where(own_column, lower[0], lower[1]),
                jnp.where(own_column, lower_far[0], lower_far[1]),
            ),
        ]

    return jnp.concatenate(
        [jnp.concatenate(at(0, column) + at(1, column), 0) for column in range(2)], 1
    )


def split(value):
    high = value.astype(jnp.bfloat16)
    return high, (value - high.astype(jnp.float32)).astype(jnp.bfloat16)


def scale_rows(value, mask_ref, slot, first_block, count):
    rows = value.shape[0] // count
    return jnp.concatenate(
        [
            value[k * rows : (k + 1) * rows] * mask_ref[slot, first_block + k].astype(jnp.float32)
            for k in range(count)
        ],
        0,
    )


def forward_kernel(slot, place, tiles, mask_blocks, bit_ref, mask_ref, panel_ref, near_ref, far_ref, *refs):
    prev, (out_first, out_last, high, low) = refs[:-4], refs[-4:]
    turn, step = pl.program_id(0), pl.program_id(1)
    columns = near_ref.shape[1]

    @pl.when((turn == 0) & (step == 0))
    def _():
        for k, ref in enumerate((near_ref, far_ref)):
            part = split(ref[...])
            high[:, k * columns : (k + 1) * columns] = part[0]
            low[:, k * columns : (k + 1) * columns] = part[1]

    panel_high, panel_low = split(panel_ref[...])

    def dot(left, right):
        return jnp.dot(left, right, preferred_element_type=jnp.float32)

    result = dot(panel_high, high[...]) + (dot(panel_high, low[...]) + dot(panel_low, high[...]))
    block = jnp.where(turn == 0, 1 - bit_ref[0], bit_ref[0])
    tile = (2 * block + place) * tiles + step
    result = scale_rows(result, mask_ref, slot, tile * mask_blocks, mask_blocks)
    here = pl.ds(pl.multiple_of(step * panel_ref.shape[0], panel_ref.shape[0]), panel_ref.shape[0])
    parts = result[:, :columns], result[:, columns:]

    def put(ref, index, value, old):
        ref[index, here] = value + old[index, here] if old is not None else value

    first_old, last_old = prev or (None, None)
    if place == 0:
        put(out_first, turn, parts[0], first_old)
        put(out_last, turn, parts[1], last_old)
    else:

        @pl.when(turn == 0)
        def _():
            for k in range(2):
                put(out_first, k, parts[k], first_old)

        @pl.when(turn == 1)
        def _():
            for k in range(2):
                put(out_last, k, parts[k], last_old)


def panel_forward(panel_anc, mask, slot, place, y_bit, near, far, prev=(), tile_rows=256):
    rows_local, width = panel_anc.shape[2:]
    quarter = rows_local // 4
    tiles = quarter // tile_rows
    columns = near.shape[1]
    mask_blocks = mask.shape[1] // (4 * tiles)

    def panel_index(turn, step, bit_ref, mask_ref):
        block = jnp.where(turn == 0, 1 - bit_ref[0], bit_ref[0])
        return (0, slot, (2 * block + place) * tiles + step, 0)

    whole = pl.BlockSpec(memory_space=pltpu.VMEM)
    shape = jax.ShapeDtypeStruct((2, quarter, columns), jnp.float32)
    return pl.pallas_call(
        functools.partial(forward_kernel, slot, place, tiles, mask_blocks),
        out_shape=[shape, shape],
        grid_spec=pltpu.PrefetchScalarGridSpec(
            num_scalar_prefetch=2,
            grid=(2, tiles),
            in_specs=[
                pl.BlockSpec((None, None, tile_rows, width), panel_index),
                *[whole] * (2 + len(prev)),
            ],
            out_specs=[whole, whole],
            scratch_shapes=[pltpu.VMEM((width, 2 * columns), jnp.bfloat16)] * 2,
        ),
        cost_estimate=pl.CostEstimate(
            flops=12 * quarter * width * 2 * columns,
            bytes_accessed=4 * (2 * quarter * width + 2 * width * columns + 4 * quarter * columns),
            transcendentals=0,
        ),
        compiler_params=pltpu.CompilerParams(vmem_limit_bytes=VMEM_GRANT),
    )(y_bit.reshape(1).astype(jnp.int32), mask, panel_anc, near, far, *prev)


def backward_kernel(slot, side, mask_blocks, bit_ref, mask_ref, panel_ref, upper_ref, lower_ref, *refs):
    prev, (out_first, out_last, panel_parts, value_parts, total) = refs[:-5], refs[-5:]
    if prev:
        *prev, rhs_ref = prev
    phase, step = pl.program_id(0), pl.program_id(1)
    rows = panel_ref.shape[0]
    columns = upper_ref.shape[2]
    tile = backward_quarter(side, phase, bit_ref) * pl.num_programs(1) + step

    def put(index, value):
        value = scale_rows(value, mask_ref, slot, tile * mask_blocks, mask_blocks)
        high, low = split(value)
        span = slice(index * columns, (index + 1) * columns)
        value_parts[0:rows, span] = high
        value_parts[rows : 2 * rows, span] = high
        value_parts[2 * rows : 3 * rows, span] = low

    high, low = split(panel_ref[...])
    panel_parts[0:rows] = high
    panel_parts[rows : 2 * rows] = low
    panel_parts[2 * rows : 3 * rows] = high

    def dot(right):
        return lax.dot_general(
            panel_parts[...], right, (((0,), (0,)), ((), ())), preferred_element_type=jnp.float32
        )

    near, far = slice(0, columns), slice(columns, 2 * columns)
    here = near if side == 0 else far

    @pl.when((phase == 0) & (step == 0))
    def _():
        if prev:
            total[:, near] = prev[0][...]
            total[:, far] = prev[1][...]
        else:
            total[...] = jnp.zeros_like(total)

    here_rows = pl.ds(pl.multiple_of(step * rows, rows), rows)

    @pl.when(phase < 2)
    def _():
        put(0, upper_ref[phase, here_rows])
        total[:, here] += dot(value_parts[:, near])

    @pl.when(phase == 2)
    def _():
        put(0, lower_ref[0, here_rows])
        put(1, lower_ref[1, here_rows])
        total[...] += dot(value_parts[...])

    @pl.when((phase == 2) & (step == pl.num_programs(1) - 1))
    def _():
        if side == 0:
            out_first[...] = total[:, near]
            out_last[...] = total[:, far]
        else:
            length = rhs_ref.shape[0]
            count = total.shape[0] // length

            def put_out(kept, sent):
                for k in range(count):
                    source = pl.ds(pl.multiple_of(bit_ref[2 + k] * length, length), length)
                    place = slice(k * length, (k + 1) * length)
                    value = total[source, kept]
                    out_first[place] = value - rhs_ref[...] if k == count - 1 else value
                    out_last[place] = total[source, sent]

            pl.when(bit_ref[1] == 1)(functools.partial(put_out, near, far))
            pl.when(bit_ref[1] == 0)(functools.partial(put_out, far, near))


def backward_quarter(side, phase, bit_ref):
    own, other = bit_ref[0], 1 - bit_ref[0]
    lower = 2 * (own if side == 0 else other) + 1
    return jnp.where(phase == 0, 2 * own, jnp.where(phase == 1, 2 * other, lower))


def panel_backward(panel_anc, mask, slot, side, bits, upper, lower, prev=(), tile_rows=256):
    rows_local, width = panel_anc.shape[2:]
    quarter = rows_local // 4
    columns = upper.shape[2]
    tiles = quarter // tile_rows
    mask_blocks = mask.shape[1] // (4 * tiles)

    def panel_index(phase, step, bit_ref, mask_ref):
        return (0, slot, backward_quarter(side, phase, bit_ref) * tiles + step, 0)

    whole = pl.BlockSpec(memory_space=pltpu.VMEM)
    shape = jax.ShapeDtypeStruct((width, columns), jnp.float32)
    return pl.pallas_call(
        functools.partial(backward_kernel, slot, side, mask_blocks),
        out_shape=[shape, shape],
        grid_spec=pltpu.PrefetchScalarGridSpec(
            num_scalar_prefetch=2,
            grid=(3, tiles),
            in_specs=[
                pl.BlockSpec((None, None, tile_rows, width), panel_index),
                *[whole] * (2 + len(prev)),
            ],
            out_specs=[whole, whole],
            scratch_shapes=[
                pltpu.VMEM((3 * tile_rows, width), jnp.bfloat16),
                pltpu.VMEM((3 * tile_rows, 2 * columns), jnp.bfloat16),
                pltpu.VMEM((width, 2 * columns), jnp.float32),
            ],
        ),
        cost_estimate=pl.CostEstimate(
            flops=6 * 4 * quarter * width * columns,
            bytes_accessed=4 * (3 * quarter * width + 4 * quarter * columns + 4 * width * columns),
            transcendentals=0,
        ),
        compiler_params=pltpu.CompilerParams(vmem_limit_bytes=VMEM_GRANT),
    )(bits, mask, panel_anc, upper, lower, *prev)


def from_partner(value, axis, bit):
    mask = 2**bit
    pairs = [(source, source ^ mask) for source in range(lax.axis_size(axis))]
    return lax.ppermute(value, axis, pairs)


def ancestor_solve(inverse_rows, values):
    rows_local, width = inverse_rows.shape
    if rows_local >= width:
        blocks = inverse_rows.reshape(rows_local // width, width, width)
        grouped = values.reshape(rows_local // width, width, values.shape[1])
        forward = jnp.einsum("kij,kjr->kir", blocks, grouped, precision=PRECISION)
        result = jnp.einsum("kji,kjr->kir", blocks, forward, precision=PRECISION)
        return result.reshape(rows_local, values.shape[1])
    row_index = lax.axis_index("row")
    levels = (width // rows_local).bit_length() - 1
    whole = values
    for bit_number in range(levels):
        other = from_partner(whole, "row", bit_number)
        upper = row_index >> bit_number & 1
        whole = jnp.where(
            upper == 1, jnp.concatenate([other, whole], 0), jnp.concatenate([whole, other], 0)
        )
    forward = product(inverse_rows, whole)
    partial_value = transposed(inverse_rows, forward)
    for bit_number in reversed(range(levels)):
        half = partial_value.shape[0] // 2
        upper = row_index >> bit_number & 1
        keep = jnp.where(upper == 1, partial_value[half:], partial_value[:half])
        outgoing = jnp.where(upper == 1, partial_value[:half], partial_value[half:])
        partial_value = keep + from_partner(outgoing, "row", bit_number)
    return partial_value


def solve(rhs_sub, rhs_anc, inv_sub, panel_mid, panel_anc, block_mask, inv_anc):
    rhs_local = rhs_sub[0]
    rows_local = panel_anc.shape[2]
    width = panel_anc.shape[3]
    rows_own = rhs_local.shape[1]
    columns = rhs_local.shape[2]
    block_count = block_mask.shape[2]
    row_index = lax.axis_index("row")
    core = row_index % 2
    leaf = lax.axis_index("leaf")
    x_bit, y_bit = leaf % 2, leaf // 2
    paired = lax.axis_size("leaf") == 4 and rows_local == 2 * width and len(row_digits()) == 1
    mask = block_mask[0].astype(jnp.float32)
    half = columns // 2

    def masked(slot, value):
        blocks = value.reshape(block_count, rows_local // block_count, value.shape[1])
        return (blocks * mask[slot][:, None, None]).reshape(value.shape)

    def halves(value):
        return jnp.where(core == 0, value[..., :half], value[..., half:])

    def other_half(value):
        return jnp.where(core == 0, value[..., half:], value[..., :half])

    rhs_chip = by_core(core, halves(rhs_local), core_swap(other_half(rhs_local)), 1)
    inverses = inv_sub[0]
    inverses_other, middle_other = core_swap(inverses), core_swap(panel_mid[0])
    inverse_first = by_core(core, inverses[0], inverses_other[0], 0)
    inverse_second = by_core(core, inverses[1], inverses_other[1], 0)
    middle = by_core(core, panel_mid[0], middle_other, 0)

    def both_halves(value):
        return by_core(core, value, core_swap(value), 1)

    def near_and_far(value):
        swapped = core_swap(value)
        far_is_mine = core == x_bit
        return jnp.where(far_is_mine, swapped, value), jnp.where(far_is_mine, value, swapped)

    block_mask = block_mask[0]
    gathered, inverse_first = gather_rows(rhs_chip[0], lower=True, filler=inverse_first)
    first = product(inverse_first, gathered)
    first, turned = lax.optimization_barrier((first, inverses))
    turned = lax.optimization_barrier(row_major(jnp.swapaxes(turned, 1, 2)))
    first_all, (middle, inverse_second, turned) = gather_rows(
        first, filler=(middle, inverse_second, turned)
    )
    residual = rhs_chip[1] - product(middle, first_all)
    if paired:
        sides = near_and_far(first_all)
        upper = panel_forward(panel_anc, block_mask, 0, 0, y_bit, *sides)
        lower = panel_forward(panel_anc, block_mask, 0, 1, y_bit, *sides)
        gathered, upper = gather_rows(residual, lower=True, filler=upper)
        second = product(inverse_second, gathered)
        second_all, lower = gather_rows(second, filler=lower)
        sides = near_and_far(second_all)
        lower = panel_forward(panel_anc, block_mask, 1, 1, y_bit, *sides, lower)
        upper = panel_forward(panel_anc, block_mask, 1, 0, y_bit, *sides, upper)
    else:
        gathered, _ = gather_rows(residual, lower=True)
        second = product(inverse_second, gathered)
        update = masked(0, product(panel_anc[0, 0], both_halves(first_all)))
        second_all, _ = gather_rows(second)
        update = update + masked(1, product(panel_anc[0, 1], both_halves(second_all)))

    *inner_digits, (size, stride) = row_digits()
    turned, second_all = lax.optimization_barrier((turned, second_all))
    block = turned
    for inner_size, inner_stride in inner_digits:
        block = jnp.concatenate(gather_join(block, *gather_both(block, inner_size, inner_stride), inner_size, inner_stride), 2)
    received = gather_near(block, size, stride)

    def whole_inverses(received, passed):
        joined = gather_join(block, received, passed, size, stride, ordered=False)
        mine = [jnp.concatenate([part[slot] for part in joined], 1) for slot in range(2)]
        return [(value, core_swap(value)) for value in mine]

    if paired:
        inverse_anc = jnp.where(y_bit == 0, inv_anc[:width], inv_anc[width:])
        own = jnp.where(y_bit == 0, rhs_anc[:width], rhs_anc[width:])
        own = jnp.where(x_bit == 0, own[:, :half], own[:, half:])
        total, received = leaf_reduce(upper, lower, received)
        passed = gather_far(received, size, stride)
        total, inverse_anc = lax.optimization_barrier((own - total, inverse_anc))
        forward = lax.optimization_barrier(product(inverse_anc, total))
        solved = row_major(transposed(inverse_anc, forward))
        bits = jnp.stack([y_bit, x_bit == core, *block_order(size, stride)], dtype=jnp.int32)

        def begun(upper, lower):
            sums = []
            for slot in range(2):
                sums.append(panel_backward(panel_anc, block_mask, slot, 0, bits, upper, lower))
            return sums

        pieces, sums, wholes = leaf_gather(
            solved, passed, lambda passed: whole_inverses(received, passed), begun
        )
        x_anc = in_order(pieces, x_bit, y_bit)
    else:
        wholes = whole_inverses(received, gather_far(received, size, stride))
        total = lax.psum_scatter(update, "leaf", scatter_dimension=1, tiled=True)
        share = total.shape[1]
        own = lax.dynamic_slice_in_dim(rhs_anc, leaf * share, share, 1)
        x_anc = lax.all_gather(ancestor_solve(inv_anc, own - total), "leaf", axis=1, tiled=True)
        pieces = x_anc

    rows_chip = 2 * rows_own

    def chip_sum(slot, rhs, pieces):
        if paired:
            keep, send = panel_backward(
                panel_anc, block_mask, slot, 1, bits, pieces[1], pieces[3], (*sums[slot], rhs)
            )
            return keep + core_swap(send)
        keep, send = (
            transposed(panel_anc[0, slot], masked(slot, part))
            for part in (halves(pieces), other_half(pieces))
        )
        value = keep + core_swap(send)
        start = row_index // 2 * rows_chip
        own = lax.dynamic_slice_in_dim(value, start, rows_chip, 0) - rhs
        value = lax.dynamic_update_slice_in_dim(value, own, start, 0)
        return jnp.concatenate(sending_order(value, size, stride), 0)

    def partial_solve(slot, value):
        cores = value.reshape(-1, 2, rows_own, half)
        first = jnp.where(core == 0, cores[:, 0], cores[:, 1]).reshape(-1, half)
        last = jnp.where(core == 0, cores[:, 1], cores[:, 0]).reshape(-1, half)
        first, last = lax.optimization_barrier((first, last))
        return product(wholes[slot][0], first) + product(wholes[slot][1], last)

    middle_columns = jnp.concatenate(
        [
            lax.dynamic_slice_in_dim(middle, k * (width // size), width // size, 1)
            for k in block_order(size, stride)
        ],
        1,
    )
    second_partial = partial_solve(1, chip_sum(1, second, pieces))
    second_partial, pieces = lax.optimization_barrier((second_partial, pieces))
    first_sum = chip_sum(0, first, pieces)
    second_total, first_sum = reduce_rows(second_partial, filler=(first_sum, middle_columns))
    first_sum, middle_columns = first_sum
    x_second = -second_total
    first_partial = partial_solve(0, first_sum + transposed(middle_columns, x_second))
    first_total, x_anc = reduce_rows(first_partial, filler=x_anc)
    x_first = -first_total

    both = jnp.stack([x_first, x_second])
    keep = jnp.where(core == 0, both[:, :rows_own], both[:, rows_own:])
    send = jnp.where(core == 0, both[:, rows_own:], both[:, :rows_own])
    x_sub = by_core(core, keep, core_swap(send), 2)
    return x_sub[None], x_anc


def solution(mesh):
    return jax.shard_map(
        solve,
        mesh=mesh,
        in_specs=(
            P("leaf", None, "row", None),
            P("row", None),
            P("leaf", None, "row", None),
            P("leaf", "row", None),
            P("leaf", None, "row", None),
            P("leaf", None, "row"),
            P("row", None),
        ),
        out_specs=(P("leaf", None, "row", None), P("row", None)),
        check_vma=False,
    )
```

```python
import functools

import jax
import jax.numpy as jnp
from jax import lax
from jax.experimental import pallas as pl
from jax.experimental.layout import Layout, with_layout_constraint
from jax.experimental.pallas import tpu as pltpu
from jax.sharding import PartitionSpec as P


PRECISION = lax.Precision.HIGH
VMEM_GRANT = 48 * 2**20


def product(left, right):
    return jnp.dot(left, right, precision=PRECISION, preferred_element_type=jnp.float32)


def transposed(left, right):
    return lax.dot_general(
        left,
        right,
        (((0,), (0,)), ((), ())),
        precision=PRECISION,
        preferred_element_type=jnp.float32,
    )


def row_major(value):
    return with_layout_constraint(value, Layout(tuple(range(value.ndim))))


def core_swap(value):
    count = lax.axis_size("row")
    return lax.ppermute(value, "row", [(r, r ^ 1) for r in range(count)])


def leaf_swap(value, mask):
    count = lax.axis_size("leaf")
    return lax.ppermute(value, "leaf", [(g, g ^ mask) for g in range(count)])


def chip_digits(chips):
    digits, stride = [], 1
    while chips > 1:
        size = 4 if chips % 4 == 0 else 2
        digits.append((size, stride))
        stride *= size
        chips //= size
    return digits


def digit_permute(value, size, stride, moves):
    target = dict(moves)
    pairs = []
    for r in range(lax.axis_size("row")):
        digit = (r // 2) // stride % size
        if digit in target:
            pairs.append((r, r + 2 * stride * (target[digit] - digit)))
    return lax.ppermute(value, "row", pairs)


def digit_index(size, stride):
    return lax.axis_index("row") // 2 // stride % size


def after(values, filler):
    return lax.optimization_barrier((*values, filler))


def gather_near(value, size, stride, lower=False):
    def moves(pairs):
        return [(a, b) for a, b in pairs if a < b] if lower else pairs

    if size == 2:
        return (digit_permute(value, size, stride, moves([(0, 1), (1, 0)])),)
    near = digit_permute(value, size, stride, moves([(0, 1), (1, 0), (2, 3), (3, 2)]))
    inner = digit_permute(value, size, stride, moves([(1, 2), (2, 1)]))
    return near, inner


def gather_far(received, size, stride, lower=False):
    def moves(pairs):
        return [(a, b) for a, b in pairs if a < b] if lower else pairs

    if size == 2:
        return ()
    near, inner = received
    relay = digit_permute(near, size, stride, moves([(1, 2), (2, 1)]))
    far = digit_permute(near, size, stride, moves([(1, 3), (2, 0)]))
    outer = digit_permute(inner, size, stride, moves([(1, 0), (2, 3)]))
    return relay, far, outer


def gather_join(value, received, passed, size, stride, ordered=True):
    me = digit_index(size, stride)
    if size == 2:
        (near,) = received
        if not ordered:
            return [near, value]
        return [jnp.where(me == 0, value, near), jnp.where(me == 0, near, value)]
    near, inner = received
    relay, far, outer = passed
    middle = (me == 1) | (me == 2)
    third = jnp.where(middle, inner, outer)
    fourth = jnp.where(middle, relay, far)
    odd = me % 2 == 1
    if not ordered:
        return [fourth, third, near, value]
    even_one = jnp.where(odd, near, value)
    odd_one = jnp.where(odd, value, near)
    high = me >= 2
    return [
        jnp.where(high, fourth, even_one),
        jnp.where(high, third, odd_one),
        jnp.where(high, even_one, third),
        jnp.where(high, odd_one, fourth),
    ]


def gather_both(value, size, stride):
    received = gather_near(value, size, stride)
    return received, gather_far(received, size, stride)


def gather_digit(value, size, stride, lower, filler):
    received = gather_near(value, size, stride, lower)
    passed = gather_far(received, size, stride, lower)
    last, filler = after((passed or received,), filler)
    received, passed = (received, last) if passed else (last, passed)
    return jnp.concatenate(gather_join(value, received, passed, size, stride), 0), filler


def block_order(size, stride):
    me = digit_index(size, stride)
    if size == 2:
        return 1 - me, me
    high = me >= 2
    return jnp.where(high, 0, 3), jnp.where(high, 1, 2), me ^ 1, me


def sending_order(value, size, stride):
    rows = value.shape[0] // size
    return [
        lax.dynamic_slice_in_dim(value, k * rows, rows, 0) for k in block_order(size, stride)
    ]


def reduce_digit(value, size, stride, lower, filler):
    def moves(pairs):
        return [(a, b) for a, b in pairs if a > b] if lower else pairs

    block = sending_order(value, size, stride)
    if size == 2:
        other = digit_permute(block[0], size, stride, moves([(0, 1), (1, 0)]))
        other, filler = after((other,), filler)
        return block[1] + other, filler
    far = digit_permute(block[0], size, stride, moves([(3, 1), (0, 2)]))
    relay = digit_permute(block[0], size, stride, moves([(2, 1), (1, 2)]))
    outer = digit_permute(block[1], size, stride, moves([(0, 1), (3, 2)]))
    far, relay, outer = lax.optimization_barrier((far, relay, outer))
    inner = digit_permute(block[1] + outer, size, stride, moves([(1, 2), (2, 1)]))
    near = digit_permute(block[2] + (far + relay), size, stride, moves([(0, 1), (1, 0), (2, 3), (3, 2)]))
    near, inner, filler = after((near, inner), filler)
    return block[3] + near + inner, filler


def gather_rows(value, lower=False, filler=()):
    digits = chip_digits(lax.axis_size("row") // 2)
    for place, (size, stride) in enumerate(digits):
        outermost = place == len(digits) - 1
        value, filler = gather_digit(value, size, stride, lower and outermost, filler)
    return value, filler


def row_digits():
    return chip_digits(lax.axis_size("row") // 2)


def reduce_rows(value, lower=False, filler=()):
    digits = row_digits()
    for place, (size, stride) in reversed(list(enumerate(digits))):
        outermost = place == len(digits) - 1
        value, filler = reduce_digit(value, size, stride, lower and outermost, filler)
    return value, filler


def by_core(core, mine, other, axis):
    return jnp.concatenate(
        [jnp.where(core == 0, mine, other), jnp.where(core == 0, other, mine)], axis
    )


def leaf_reduce(upper, lower, side):
    from_x = leaf_swap(upper[0], 1)
    from_y = leaf_swap(lower[0], 2)
    lower_kept, side = after((lower[1],), side)
    lower = (lower[0], lower_kept)
    from_x, from_y = lax.optimization_barrier((from_x, from_y))
    first, second = upper[1][0] + from_x[0], lower[1][0] + from_y[0]
    first, second = leaf_swap(first, 2), leaf_swap(second, 1)
    first, second = lax.optimization_barrier((first, second))
    return jnp.concatenate(
        [upper[1][1] + from_x[1] + first, lower[1][1] + from_y[1] + second], 0
    ), side


def leaf_gather(piece, side, finish, between):
    rows = piece.shape[0]
    first, second = piece[: rows // 2], piece[rows // 2 :]
    first_y = leaf_swap(first, 2)
    second_x = leaf_swap(second, 1)
    wholes = finish(side)
    first_y, second_x, wholes = lax.optimization_barrier((first_y, second_x, wholes))
    upper = jnp.stack([first, first_y])
    lower = jnp.stack([second, second_x])
    upper_far = leaf_swap(upper, 1)
    lower_far = leaf_swap(lower, 2)
    sums = between(upper, lower)
    upper_far, lower_far, sums = lax.optimization_barrier((upper_far, lower_far, sums))
    return (upper, upper_far, lower, lower_far), sums, wholes


def in_order(pieces, x_bit, y_bit):
    upper, upper_far, lower, lower_far = pieces

    def at(block, column):
        own_block, own_column = y_bit == block, x_bit == column
        return [
            jnp.where(
                own_column,
                jnp.where(own_block, upper[0], upper[1]),
                jnp.where(own_block, upper_far[0], upper_far[1]),
            ),
            jnp.where(
                own_block,
                jnp.where(own_column, lower[0], lower[1]),
                jnp.where(own_column, lower_far[0], lower_far[1]),
            ),
        ]

    return jnp.concatenate(
        [jnp.concatenate(at(0, column) + at(1, column), 0) for column in range(2)], 1
    )


def split(value):
    high = value.astype(jnp.bfloat16)
    return high, (value - high.astype(jnp.float32)).astype(jnp.bfloat16)


def scale_rows(value, mask_ref, slot, first_block, count):
    rows = value.shape[0] // count
    return jnp.concatenate(
        [
            value[k * rows : (k + 1) * rows] * mask_ref[slot, first_block + k].astype(jnp.float32)
            for k in range(count)
        ],
        0,
    )


def forward_kernel(slot, place, tiles, mask_blocks, bit_ref, mask_ref, panel_ref, near_ref, far_ref, *refs):
    prev, (out_first, out_last, high, low) = refs[:-4], refs[-4:]
    turn, step = pl.program_id(0), pl.program_id(1)
    columns = near_ref.shape[1]

    @pl.when((turn == 0) & (step == 0))
    def _():
        for k, ref in enumerate((near_ref, far_ref)):
            part = split(ref[...])
            high[:, k * columns : (k + 1) * columns] = part[0]
            low[:, k * columns : (k + 1) * columns] = part[1]

    panel_high, panel_low = split(panel_ref[...])

    def dot(left, right):
        return jnp.dot(left, right, preferred_element_type=jnp.float32)

    result = dot(panel_high, high[...]) + (dot(panel_high, low[...]) + dot(panel_low, high[...]))
    block = jnp.where(turn == 0, 1 - bit_ref[0], bit_ref[0])
    tile = (2 * block + place) * tiles + step
    result = scale_rows(result, mask_ref, slot, tile * mask_blocks, mask_blocks)
    here = pl.ds(pl.multiple_of(step * panel_ref.shape[0], panel_ref.shape[0]), panel_ref.shape[0])
    parts = result[:, :columns], result[:, columns:]

    def put(ref, index, value, old):
        ref[index, here] = value + old[index, here] if old is not None else value

    first_old, last_old = prev or (None, None)
    if place == 0:
        put(out_first, turn, parts[0], first_old)
        put(out_last, turn, parts[1], last_old)
    else:

        @pl.when(turn == 0)
        def _():
            for k in range(2):
                put(out_first, k, parts[k], first_old)

        @pl.when(turn == 1)
        def _():
            for k in range(2):
                put(out_last, k, parts[k], last_old)


def panel_forward(panel_anc, mask, slot, place, y_bit, near, far, prev=(), tile_rows=256):
    rows_local, width = panel_anc.shape[2:]
    quarter = rows_local // 4
    tiles = quarter // tile_rows
    columns = near.shape[1]
    mask_blocks = mask.shape[1] // (4 * tiles)

    def panel_index(turn, step, bit_ref, mask_ref):
        block = jnp.where(turn == 0, 1 - bit_ref[0], bit_ref[0])
        return (0, slot, (2 * block + place) * tiles + step, 0)

    whole = pl.BlockSpec(memory_space=pltpu.VMEM)
    shape = jax.ShapeDtypeStruct((2, quarter, columns), jnp.float32)
    return pl.pallas_call(
        functools.partial(forward_kernel, slot, place, tiles, mask_blocks),
        out_shape=[shape, shape],
        grid_spec=pltpu.PrefetchScalarGridSpec(
            num_scalar_prefetch=2,
            grid=(2, tiles),
            in_specs=[
                pl.BlockSpec((None, None, tile_rows, width), panel_index),
                *[whole] * (2 + len(prev)),
            ],
            out_specs=[whole, whole],
            scratch_shapes=[pltpu.VMEM((width, 2 * columns), jnp.bfloat16)] * 2,
        ),
        cost_estimate=pl.CostEstimate(
            flops=12 * quarter * width * 2 * columns,
            bytes_accessed=4 * (2 * quarter * width + 2 * width * columns + 4 * quarter * columns),
            transcendentals=0,
        ),
        compiler_params=pltpu.CompilerParams(vmem_limit_bytes=VMEM_GRANT),
    )(y_bit.reshape(1).astype(jnp.int32), mask, panel_anc, near, far, *prev)


def backward_kernel(slot, side, mask_blocks, bit_ref, mask_ref, panel_ref, upper_ref, lower_ref, *refs):
    prev, (out_first, out_last, panel_parts, value_parts, total) = refs[:-5], refs[-5:]
    if prev:
        *prev, rhs_ref = prev
    phase, step = pl.program_id(1), pl.program_id(2)
    if slot is None:
        slot = pl.program_id(0)
    rows = panel_ref.shape[0]
    columns = upper_ref.shape[2]
    tile = backward_quarter(side, phase, bit_ref) * pl.num_programs(2) + step

    def put(index, value):
        value = scale_rows(value, mask_ref, slot, tile * mask_blocks, mask_blocks)
        high, low = split(value)
        span = slice(index * columns, (index + 1) * columns)
        value_parts[0:rows, span] = high
        value_parts[rows : 2 * rows, span] = high
        value_parts[2 * rows : 3 * rows, span] = low

    high, low = split(panel_ref[...])
    panel_parts[0:rows] = high
    panel_parts[rows : 2 * rows] = low
    panel_parts[2 * rows : 3 * rows] = high

    def dot(right):
        return lax.dot_general(
            panel_parts[...], right, (((0,), (0,)), ((), ())), preferred_element_type=jnp.float32
        )

    near, far = slice(0, columns), slice(columns, 2 * columns)
    here = near if side == 0 else far

    @pl.when((phase == 0) & (step == 0))
    def _():
        if prev:
            total[:, near] = prev[0][slot]
            total[:, far] = prev[1][slot]
        else:
            total[...] = jnp.zeros_like(total)

    here_rows = pl.ds(pl.multiple_of(step * rows, rows), rows)

    @pl.when(phase < 2)
    def _():
        put(0, upper_ref[phase, here_rows])
        total[:, here] += dot(value_parts[:, near])

    @pl.when(phase == 2)
    def _():
        put(0, lower_ref[0, here_rows])
        put(1, lower_ref[1, here_rows])
        total[...] += dot(value_parts[...])

    @pl.when((phase == 2) & (step == pl.num_programs(2) - 1))
    def _():
        if side == 0:
            out_first[slot] = total[:, near]
            out_last[slot] = total[:, far]
        else:
            length = rhs_ref.shape[0]
            count = total.shape[0] // length

            def put_out(kept, sent):
                for k in range(count):
                    source = pl.ds(pl.multiple_of(bit_ref[2 + k] * length, length), length)
                    place = slice(k * length, (k + 1) * length)
                    value = total[source, kept]
                    out_first[place] = value - rhs_ref[...] if k == count - 1 else value
                    out_last[place] = total[source, sent]

            pl.when(bit_ref[1] == 1)(functools.partial(put_out, near, far))
            pl.when(bit_ref[1] == 0)(functools.partial(put_out, far, near))


def backward_quarter(side, phase, bit_ref):
    own, other = bit_ref[0], 1 - bit_ref[0]
    lower = 2 * (own if side == 0 else other) + 1
    return jnp.where(phase == 0, 2 * own, jnp.where(phase == 1, 2 * other, lower))


def panel_backward(panel_anc, mask, slot, side, bits, upper, lower, prev=(), tile_rows=256):
    rows_local, width = panel_anc.shape[2:]
    quarter = rows_local // 4
    columns = upper.shape[2]
    tiles = quarter // tile_rows
    mask_blocks = mask.shape[1] // (4 * tiles)

    def panel_index(turn, phase, step, bit_ref, mask_ref):
        tile = backward_quarter(side, phase, bit_ref) * tiles + step
        return (0, turn if slot is None else slot, tile, 0)

    slots = 2 if slot is None else 1

    whole = pl.BlockSpec(memory_space=pltpu.VMEM)
    shape = jax.ShapeDtypeStruct(
        (2, width, columns) if slot is None else (width, columns), jnp.float32
    )
    return pl.pallas_call(
        functools.partial(backward_kernel, slot, side, mask_blocks),
        out_shape=[shape, shape],
        grid_spec=pltpu.PrefetchScalarGridSpec(
            num_scalar_prefetch=2,
            grid=(slots, 3, tiles),
            in_specs=[
                pl.BlockSpec((None, None, tile_rows, width), panel_index),
                *[whole] * (2 + len(prev)),
            ],
            out_specs=[whole, whole],
            scratch_shapes=[
                pltpu.VMEM((3 * tile_rows, width), jnp.bfloat16),
                pltpu.VMEM((3 * tile_rows, 2 * columns), jnp.bfloat16),
                pltpu.VMEM((width, 2 * columns), jnp.float32),
            ],
        ),
        cost_estimate=pl.CostEstimate(
            flops=slots * 6 * 4 * quarter * width * columns,
            bytes_accessed=slots * 4 * (3 * quarter * width + 4 * quarter * columns + 4 * width * columns),
            transcendentals=0,
        ),
        compiler_params=pltpu.CompilerParams(vmem_limit_bytes=VMEM_GRANT),
    )(bits, mask, panel_anc, upper, lower, *prev)


def from_partner(value, axis, bit):
    mask = 2**bit
    pairs = [(source, source ^ mask) for source in range(lax.axis_size(axis))]
    return lax.ppermute(value, axis, pairs)


def ancestor_solve(inverse_rows, values):
    rows_local, width = inverse_rows.shape
    if rows_local >= width:
        blocks = inverse_rows.reshape(rows_local // width, width, width)
        grouped = values.reshape(rows_local // width, width, values.shape[1])
        forward = jnp.einsum("kij,kjr->kir", blocks, grouped, precision=PRECISION)
        result = jnp.einsum("kji,kjr->kir", blocks, forward, precision=PRECISION)
        return result.reshape(rows_local, values.shape[1])
    row_index = lax.axis_index("row")
    levels = (width // rows_local).bit_length() - 1
    whole = values
    for bit_number in range(levels):
        other = from_partner(whole, "row", bit_number)
        upper = row_index >> bit_number & 1
        whole = jnp.where(
            upper == 1, jnp.concatenate([other, whole], 0), jnp.concatenate([whole, other], 0)
        )
    forward = product(inverse_rows, whole)
    partial_value = transposed(inverse_rows, forward)
    for bit_number in reversed(range(levels)):
        half = partial_value.shape[0] // 2
        upper = row_index >> bit_number & 1
        keep = jnp.where(upper == 1, partial_value[half:], partial_value[:half])
        outgoing = jnp.where(upper == 1, partial_value[:half], partial_value[half:])
        partial_value = keep + from_partner(outgoing, "row", bit_number)
    return partial_value


def solve(rhs_sub, rhs_anc, inv_sub, panel_mid, panel_anc, block_mask, inv_anc):
    rhs_local = rhs_sub[0]
    rows_local = panel_anc.shape[2]
    width = panel_anc.shape[3]
    rows_own = rhs_local.shape[1]
    columns = rhs_local.shape[2]
    block_count = block_mask.shape[2]
    row_index = lax.axis_index("row")
    core = row_index % 2
    leaf = lax.axis_index("leaf")
    x_bit, y_bit = leaf % 2, leaf // 2
    paired = lax.axis_size("leaf") == 4 and rows_local == 2 * width and len(row_digits()) == 1
    mask = block_mask[0].astype(jnp.float32)
    half = columns // 2

    def masked(slot, value):
        blocks = value.reshape(block_count, rows_local // block_count, value.shape[1])
        return (blocks * mask[slot][:, None, None]).reshape(value.shape)

    def halves(value):
        return jnp.where(core == 0, value[..., :half], value[..., half:])

    def other_half(value):
        return jnp.where(core == 0, value[..., half:], value[..., :half])

    rhs_chip = by_core(core, halves(rhs_local), core_swap(other_half(rhs_local)), 1)
    inverses = inv_sub[0]
    inverses_other, middle_other = core_swap(inverses), core_swap(panel_mid[0])
    inverse_first = by_core(core, inverses[0], inverses_other[0], 0)
    inverse_second = by_core(core, inverses[1], inverses_other[1], 0)
    middle = by_core(core, panel_mid[0], middle_other, 0)

    def both_halves(value):
        return by_core(core, value, core_swap(value), 1)

    def near_and_far(value):
        swapped = core_swap(value)
        far_is_mine = core == x_bit
        return jnp.where(far_is_mine, swapped, value), jnp.where(far_is_mine, value, swapped)

    block_mask = block_mask[0]
    gathered, inverse_first = gather_rows(rhs_chip[0], lower=True, filler=inverse_first)
    first = product(inverse_first, gathered)
    first, turned = lax.optimization_barrier((first, inverses))
    turned = lax.optimization_barrier(row_major(jnp.swapaxes(turned, 1, 2)))
    first_all, (middle, inverse_second, turned) = gather_rows(
        first, filler=(middle, inverse_second, turned)
    )
    residual = rhs_chip[1] - product(middle, first_all)
    if paired:
        sides = near_and_far(first_all)
        upper = panel_forward(panel_anc, block_mask, 0, 0, y_bit, *sides)
        lower = panel_forward(panel_anc, block_mask, 0, 1, y_bit, *sides)
        gathered, upper = gather_rows(residual, lower=True, filler=upper)
        second = product(inverse_second, gathered)
        second_all, lower = gather_rows(second, filler=lower)
        sides = near_and_far(second_all)
        lower = panel_forward(panel_anc, block_mask, 1, 1, y_bit, *sides, lower)
        upper = panel_forward(panel_anc, block_mask, 1, 0, y_bit, *sides, upper)
    else:
        gathered, _ = gather_rows(residual, lower=True)
        second = product(inverse_second, gathered)
        update = masked(0, product(panel_anc[0, 0], both_halves(first_all)))
        second_all, _ = gather_rows(second)
        update = update + masked(1, product(panel_anc[0, 1], both_halves(second_all)))

    *inner_digits, (size, stride) = row_digits()
    turned, second_all = lax.optimization_barrier((turned, second_all))
    block = turned
    for inner_size, inner_stride in inner_digits:
        block = jnp.concatenate(gather_join(block, *gather_both(block, inner_size, inner_stride), inner_size, inner_stride), 2)
    received = gather_near(block, size, stride)

    def whole_inverses(received, passed):
        joined = gather_join(block, received, passed, size, stride, ordered=False)
        mine = [jnp.concatenate([part[slot] for part in joined], 1) for slot in range(2)]
        return [(value, core_swap(value)) for value in mine]

    if paired:
        inverse_anc = jnp.where(y_bit == 0, inv_anc[:width], inv_anc[width:])
        own = jnp.where(y_bit == 0, rhs_anc[:width], rhs_anc[width:])
        own = jnp.where(x_bit == 0, own[:, :half], own[:, half:])
        total, received = leaf_reduce(upper, lower, received)
        passed = gather_far(received, size, stride)
        total, inverse_anc = lax.optimization_barrier((own - total, inverse_anc))
        forward = lax.optimization_barrier(product(inverse_anc, total))
        solved = row_major(transposed(inverse_anc, forward))
        bits = jnp.stack([y_bit, x_bit == core, *block_order(size, stride)], dtype=jnp.int32)

        def begun(upper, lower):
            return panel_backward(panel_anc, block_mask, None, 0, bits, upper, lower)

        pieces, sums, wholes = leaf_gather(
            solved, passed, lambda passed: whole_inverses(received, passed), begun
        )
        x_anc = in_order(pieces, x_bit, y_bit)
    else:
        wholes = whole_inverses(received, gather_far(received, size, stride))
        total = lax.psum_scatter(update, "leaf", scatter_dimension=1, tiled=True)
        share = total.shape[1]
        own = lax.dynamic_slice_in_dim(rhs_anc, leaf * share, share, 1)
        x_anc = lax.all_gather(ancestor_solve(inv_anc, own - total), "leaf", axis=1, tiled=True)
        pieces = x_anc

    rows_chip = 2 * rows_own

    def chip_sum(slot, rhs, pieces):
        if paired:
            keep, send = panel_backward(
                panel_anc, block_mask, slot, 1, bits, pieces[1], pieces[3], (*sums, rhs)
            )
            return keep + core_swap(send)
        keep, send = (
            transposed(panel_anc[0, slot], masked(slot, part))
            for part in (halves(pieces), other_half(pieces))
        )
        value = keep + core_swap(send)
        start = row_index // 2 * rows_chip
        own = lax.dynamic_slice_in_dim(value, start, rows_chip, 0) - rhs
        value = lax.dynamic_update_slice_in_dim(value, own, start, 0)
        return jnp.concatenate(sending_order(value, size, stride), 0)

    def partial_solve(slot, value):
        cores = value.reshape(-1, 2, rows_own, half)
        first = jnp.where(core == 0, cores[:, 0], cores[:, 1]).reshape(-1, half)
        last = jnp.where(core == 0, cores[:, 1], cores[:, 0]).reshape(-1, half)
        first, last = lax.optimization_barrier((first, last))
        return product(wholes[slot][0], first) + product(wholes[slot][1], last)

    middle_columns = jnp.concatenate(
        [
            lax.dynamic_slice_in_dim(middle, k * (width // size), width // size, 1)
            for k in block_order(size, stride)
        ],
        1,
    )
    second_partial = partial_solve(1, chip_sum(1, second, pieces))
    second_partial, pieces = lax.optimization_barrier((second_partial, pieces))
    first_sum = chip_sum(0, first, pieces)
    second_total, first_sum = reduce_rows(second_partial, filler=(first_sum, middle_columns))
    first_sum, middle_columns = first_sum
    x_second = -second_total
    first_partial = partial_solve(0, first_sum + transposed(middle_columns, x_second))
    first_total, x_anc = reduce_rows(first_partial, filler=x_anc)
    x_first = -first_total

    both = jnp.stack([x_first, x_second])
    keep = jnp.where(core == 0, both[:, :rows_own], both[:, rows_own:])
    send = jnp.where(core == 0, both[:, rows_own:], both[:, :rows_own])
    x_sub = by_core(core, keep, core_swap(send), 2)
    return x_sub[None], x_anc


def solution(mesh):
    return jax.shard_map(
        solve,
        mesh=mesh,
        in_specs=(
            P("leaf", None, "row", None),
            P("row", None),
            P("leaf", None, "row", None),
            P("leaf", "row", None),
            P("leaf", None, "row", None),
            P("leaf", None, "row"),
            P("row", None),
        ),
        out_specs=(P("leaf", None, "row", None), P("row", None)),
        check_vma=False,
    )
```

```python
import functools

import jax
import jax.numpy as jnp
from jax import lax
from jax.experimental import pallas as pl
from jax.experimental.layout import Layout, with_layout_constraint
from jax.experimental.pallas import tpu as pltpu
from jax.sharding import PartitionSpec as P


PRECISION = lax.Precision.HIGH
VMEM_GRANT = 24 * 2**20


def product(left, right):
    return jnp.dot(left, right, precision=PRECISION, preferred_element_type=jnp.float32)


def transposed(left, right):
    return lax.dot_general(
        left,
        right,
        (((0,), (0,)), ((), ())),
        precision=PRECISION,
        preferred_element_type=jnp.float32,
    )


def row_major(value):
    return with_layout_constraint(value, Layout(tuple(range(value.ndim))))


def core_swap(value):
    count = lax.axis_size("row")
    return lax.ppermute(value, "row", [(r, r ^ 1) for r in range(count)])


def leaf_swap(value, mask):
    count = lax.axis_size("leaf")
    return lax.ppermute(value, "leaf", [(g, g ^ mask) for g in range(count)])


def chip_digits(chips):
    digits, stride = [], 1
    while chips > 1:
        size = 4 if chips % 4 == 0 else 2
        digits.append((size, stride))
        stride *= size
        chips //= size
    return digits


def digit_permute(value, size, stride, moves):
    target = dict(moves)
    pairs = []
    for r in range(lax.axis_size("row")):
        digit = (r // 2) // stride % size
        if digit in target:
            pairs.append((r, r + 2 * stride * (target[digit] - digit)))
    return lax.ppermute(value, "row", pairs)


def digit_index(size, stride):
    return lax.axis_index("row") // 2 // stride % size


def after(values, filler):
    return lax.optimization_barrier((*values, filler))


def gather_near(value, size, stride, lower=False):
    def moves(pairs):
        return [(a, b) for a, b in pairs if a < b] if lower else pairs

    if size == 2:
        return (digit_permute(value, size, stride, moves([(0, 1), (1, 0)])),)
    near = digit_permute(value, size, stride, moves([(0, 1), (1, 0), (2, 3), (3, 2)]))
    inner = digit_permute(value, size, stride, moves([(1, 2), (2, 1)]))
    return near, inner


def gather_far(received, size, stride, lower=False):
    def moves(pairs):
        return [(a, b) for a, b in pairs if a < b] if lower else pairs

    if size == 2:
        return ()
    near, inner = received
    relay = digit_permute(near, size, stride, moves([(1, 2), (2, 1)]))
    far = digit_permute(near, size, stride, moves([(1, 3), (2, 0)]))
    outer = digit_permute(inner, size, stride, moves([(1, 0), (2, 3)]))
    return relay, far, outer


def gather_join(value, received, passed, size, stride, ordered=True):
    me = digit_index(size, stride)
    if size == 2:
        (near,) = received
        if not ordered:
            return [near, value]
        return [jnp.where(me == 0, value, near), jnp.where(me == 0, near, value)]
    near, inner = received
    relay, far, outer = passed
    middle = (me == 1) | (me == 2)
    third = jnp.where(middle, inner, outer)
    fourth = jnp.where(middle, relay, far)
    odd = me % 2 == 1
    if not ordered:
        return [fourth, third, near, value]
    even_one = jnp.where(odd, near, value)
    odd_one = jnp.where(odd, value, near)
    high = me >= 2
    return [
        jnp.where(high, fourth, even_one),
        jnp.where(high, third, odd_one),
        jnp.where(high, even_one, third),
        jnp.where(high, odd_one, fourth),
    ]


def gather_both(value, size, stride):
    received = gather_near(value, size, stride)
    return received, gather_far(received, size, stride)


def gather_digit(value, size, stride, lower, filler):
    received = gather_near(value, size, stride, lower)
    passed = gather_far(received, size, stride, lower)
    last, filler = after((passed or received,), filler)
    received, passed = (received, last) if passed else (last, passed)
    return jnp.concatenate(gather_join(value, received, passed, size, stride), 0), filler


def block_order(size, stride):
    me = digit_index(size, stride)
    if size == 2:
        return 1 - me, me
    high = me >= 2
    return jnp.where(high, 0, 3), jnp.where(high, 1, 2), me ^ 1, me


def sending_order(value, size, stride):
    rows = value.shape[0] // size
    return [
        lax.dynamic_slice_in_dim(value, k * rows, rows, 0) for k in block_order(size, stride)
    ]


def reduce_digit(value, size, stride, lower, filler):
    def moves(pairs):
        return [(a, b) for a, b in pairs if a > b] if lower else pairs

    block = sending_order(value, size, stride)
    if size == 2:
        other = digit_permute(block[0], size, stride, moves([(0, 1), (1, 0)]))
        other, filler = after((other,), filler)
        return block[1] + other, filler
    far = digit_permute(block[0], size, stride, moves([(3, 1), (0, 2)]))
    relay = digit_permute(block[0], size, stride, moves([(2, 1), (1, 2)]))
    outer = digit_permute(block[1], size, stride, moves([(0, 1), (3, 2)]))
    far, relay, outer = lax.optimization_barrier((far, relay, outer))
    inner = digit_permute(block[1] + outer, size, stride, moves([(1, 2), (2, 1)]))
    near = digit_permute(block[2] + (far + relay), size, stride, moves([(0, 1), (1, 0), (2, 3), (3, 2)]))
    near, inner, filler = after((near, inner), filler)
    return block[3] + near + inner, filler


def gather_rows(value, lower=False, filler=()):
    digits = chip_digits(lax.axis_size("row") // 2)
    for place, (size, stride) in enumerate(digits):
        outermost = place == len(digits) - 1
        value, filler = gather_digit(value, size, stride, lower and outermost, filler)
    return value, filler


def row_digits():
    return chip_digits(lax.axis_size("row") // 2)


def reduce_rows(value, lower=False, filler=()):
    digits = row_digits()
    for place, (size, stride) in reversed(list(enumerate(digits))):
        outermost = place == len(digits) - 1
        value, filler = reduce_digit(value, size, stride, lower and outermost, filler)
    return value, filler


def by_core(core, mine, other, axis):
    return jnp.concatenate(
        [jnp.where(core == 0, mine, other), jnp.where(core == 0, other, mine)], axis
    )


def leaf_reduce(upper, lower, side):
    from_x = leaf_swap(upper[0], 1)
    from_y = leaf_swap(lower[0], 2)
    lower_kept, side = after((lower[1],), side)
    lower = (lower[0], lower_kept)
    from_x, from_y = lax.optimization_barrier((from_x, from_y))
    first, second = upper[1][0] + from_x[0], lower[1][0] + from_y[0]
    first, second = leaf_swap(first, 2), leaf_swap(second, 1)
    first, second = lax.optimization_barrier((first, second))
    return jnp.concatenate(
        [upper[1][1] + from_x[1] + first, lower[1][1] + from_y[1] + second], 0
    ), side


def leaf_gather(piece, side, finish, between):
    rows = piece.shape[0]
    first, second = piece[: rows // 2], piece[rows // 2 :]
    first_y = leaf_swap(first, 2)
    second_x = leaf_swap(second, 1)
    wholes = finish(side)
    first_y, second_x = lax.optimization_barrier((first_y, second_x))
    upper = jnp.stack([first, first_y])
    lower = jnp.stack([second, second_x])
    upper_far = leaf_swap(upper, 1)
    lower_far = leaf_swap(lower, 2)
    sums = between(upper, lower)
    upper_far, lower_far, sums, wholes = lax.optimization_barrier(
        (upper_far, lower_far, sums, wholes)
    )
    return (upper, upper_far, lower, lower_far), sums, wholes


def in_order(pieces, x_bit, y_bit):
    upper, upper_far, lower, lower_far = pieces

    def at(block, column):
        own_block, own_column = y_bit == block, x_bit == column
        return [
            jnp.where(
                own_column,
                jnp.where(own_block, upper[0], upper[1]),
                jnp.where(own_block, upper_far[0], upper_far[1]),
            ),
            jnp.where(
                own_block,
                jnp.where(own_column, lower[0], lower[1]),
                jnp.where(own_column, lower_far[0], lower_far[1]),
            ),
        ]

    return jnp.concatenate(
        [jnp.concatenate(at(0, column) + at(1, column), 0) for column in range(2)], 1
    )


def split(value):
    high = value.astype(jnp.bfloat16)
    return high, (value - high.astype(jnp.float32)).astype(jnp.bfloat16)


def scale_rows(value, mask_ref, slot, first_block, count):
    rows = value.shape[0] // count
    return jnp.concatenate(
        [
            value[k * rows : (k + 1) * rows] * mask_ref[slot, first_block + k].astype(jnp.float32)
            for k in range(count)
        ],
        0,
    )


def forward_kernel(slot, place, tiles, mask_blocks, bit_ref, mask_ref, panel_ref, near_ref, far_ref, *refs):
    prev, (out_first, out_last, high, low) = refs[:-4], refs[-4:]
    turn, step = pl.program_id(0), pl.program_id(1)
    columns = near_ref.shape[1]

    @pl.when((turn == 0) & (step == 0))
    def _():
        for k, ref in enumerate((near_ref, far_ref)):
            part = split(ref[...])
            high[:, k * columns : (k + 1) * columns] = part[0]
            low[:, k * columns : (k + 1) * columns] = part[1]

    panel_high, panel_low = split(panel_ref[...])

    def dot(left, right):
        return jnp.dot(left, right, preferred_element_type=jnp.float32)

    result = dot(panel_high, high[...]) + (dot(panel_high, low[...]) + dot(panel_low, high[...]))
    block = jnp.where(turn == 0, 1 - bit_ref[0], bit_ref[0])
    tile = (2 * block + place) * tiles + step
    result = scale_rows(result, mask_ref, slot, tile * mask_blocks, mask_blocks)
    here = pl.ds(pl.multiple_of(step * panel_ref.shape[0], panel_ref.shape[0]), panel_ref.shape[0])
    parts = result[:, :columns], result[:, columns:]

    def put(ref, index, value, old):
        ref[index, here] = value + old[index, here] if old is not None else value

    first_old, last_old = prev or (None, None)
    if place == 0:
        put(out_first, turn, parts[0], first_old)
        put(out_last, turn, parts[1], last_old)
    else:

        @pl.when(turn == 0)
        def _():
            for k in range(2):
                put(out_first, k, parts[k], first_old)

        @pl.when(turn == 1)
        def _():
            for k in range(2):
                put(out_last, k, parts[k], last_old)


def panel_forward(panel_anc, mask, slot, place, y_bit, near, far, prev=(), tile_rows=256):
    rows_local, width = panel_anc.shape[2:]
    quarter = rows_local // 4
    tiles = quarter // tile_rows
    columns = near.shape[1]
    mask_blocks = mask.shape[1] // (4 * tiles)

    def panel_index(turn, step, bit_ref, mask_ref):
        block = jnp.where(turn == 0, 1 - bit_ref[0], bit_ref[0])
        return (0, slot, (2 * block + place) * tiles + step, 0)

    whole = pl.BlockSpec(memory_space=pltpu.VMEM)
    shape = jax.ShapeDtypeStruct((2, quarter, columns), jnp.float32)
    return pl.pallas_call(
        functools.partial(forward_kernel, slot, place, tiles, mask_blocks),
        out_shape=[shape, shape],
        grid_spec=pltpu.PrefetchScalarGridSpec(
            num_scalar_prefetch=2,
            grid=(2, tiles),
            in_specs=[
                pl.BlockSpec((None, None, tile_rows, width), panel_index),
                *[whole] * (2 + len(prev)),
            ],
            out_specs=[whole, whole],
            scratch_shapes=[pltpu.VMEM((width, 2 * columns), jnp.bfloat16)] * 2,
        ),
        cost_estimate=pl.CostEstimate(
            flops=12 * quarter * width * 2 * columns,
            bytes_accessed=4 * (2 * quarter * width + 2 * width * columns + 4 * quarter * columns),
            transcendentals=0,
        ),
        compiler_params=pltpu.CompilerParams(vmem_limit_bytes=VMEM_GRANT),
    )(y_bit.reshape(1).astype(jnp.int32), mask, panel_anc, near, far, *prev)


def backward_kernel(slot, side, mask_blocks, bit_ref, mask_ref, panel_ref, upper_ref, lower_ref, *refs):
    prev, (out_first, out_last, panel_parts, value_parts, total) = refs[:-5], refs[-5:]
    if prev:
        *prev, rhs_ref = prev
    phase, step = pl.program_id(1), pl.program_id(2)
    if slot is None:
        slot = pl.program_id(0)
    rows = panel_ref.shape[0]
    columns = upper_ref.shape[2]
    tile = backward_quarter(side, phase, bit_ref) * pl.num_programs(2) + step

    def put(index, value):
        value = scale_rows(value, mask_ref, slot, tile * mask_blocks, mask_blocks)
        high, low = split(value)
        span = slice(index * columns, (index + 1) * columns)
        value_parts[0:rows, span] = high
        value_parts[rows : 2 * rows, span] = high
        value_parts[2 * rows : 3 * rows, span] = low

    high, low = split(panel_ref[...])
    panel_parts[0:rows] = high
    panel_parts[rows : 2 * rows] = low
    panel_parts[2 * rows : 3 * rows] = high

    def dot(right):
        return lax.dot_general(
            panel_parts[...], right, (((0,), (0,)), ((), ())), preferred_element_type=jnp.float32
        )

    near, far = slice(0, columns), slice(columns, 2 * columns)
    here = near if side == 0 else far

    @pl.when((phase == 0) & (step == 0))
    def _():
        if prev:
            total[:, near] = prev[0][slot]
            total[:, far] = prev[1][slot]
        else:
            total[...] = jnp.zeros_like(total)

    here_rows = pl.ds(pl.multiple_of(step * rows, rows), rows)

    @pl.when(phase < 2)
    def _():
        put(0, upper_ref[phase, here_rows])
        total[:, here] += dot(value_parts[:, near])

    @pl.when(phase == 2)
    def _():
        put(0, lower_ref[0, here_rows])
        put(1, lower_ref[1, here_rows])
        total[...] += dot(value_parts[...])

    @pl.when((phase == 2) & (step == pl.num_programs(2) - 1))
    def _():
        if side == 0:
            out_first[slot] = total[:, near]
            out_last[slot] = total[:, far]
        else:
            length = rhs_ref.shape[0]
            count = total.shape[0] // length

            def put_out(kept, sent):
                for k in range(count):
                    source = pl.ds(pl.multiple_of(bit_ref[2 + k] * length, length), length)
                    place = slice(k * length, (k + 1) * length)
                    value = total[source, kept]
                    out_first[place] = value - rhs_ref[...] if k == count - 1 else value
                    out_last[place] = total[source, sent]

            pl.when(bit_ref[1] == 1)(functools.partial(put_out, near, far))
            pl.when(bit_ref[1] == 0)(functools.partial(put_out, far, near))


def backward_quarter(side, phase, bit_ref):
    own, other = bit_ref[0], 1 - bit_ref[0]
    lower = 2 * (own if side == 0 else other) + 1
    return jnp.where(phase == 0, 2 * own, jnp.where(phase == 1, 2 * other, lower))


def panel_backward(panel_anc, mask, slot, side, bits, upper, lower, prev=(), tile_rows=256):
    rows_local, width = panel_anc.shape[2:]
    quarter = rows_local // 4
    columns = upper.shape[2]
    tiles = quarter // tile_rows
    mask_blocks = mask.shape[1] // (4 * tiles)

    def panel_index(turn, phase, step, bit_ref, mask_ref):
        tile = backward_quarter(side, phase, bit_ref) * tiles + step
        return (0, turn if slot is None else slot, tile, 0)

    slots = 2 if slot is None else 1

    whole = pl.BlockSpec(memory_space=pltpu.VMEM)
    shape = jax.ShapeDtypeStruct(
        (2, width, columns) if slot is None else (width, columns), jnp.float32
    )
    return pl.pallas_call(
        functools.partial(backward_kernel, slot, side, mask_blocks),
        out_shape=[shape, shape],
        grid_spec=pltpu.PrefetchScalarGridSpec(
            num_scalar_prefetch=2,
            grid=(slots, 3, tiles),
            in_specs=[
                pl.BlockSpec((None, None, tile_rows, width), panel_index),
                *[whole] * (2 + len(prev)),
            ],
            out_specs=[whole, whole],
            scratch_shapes=[
                pltpu.VMEM((3 * tile_rows, width), jnp.bfloat16),
                pltpu.VMEM((3 * tile_rows, 2 * columns), jnp.bfloat16),
                pltpu.VMEM((width, 2 * columns), jnp.float32),
            ],
        ),
        cost_estimate=pl.CostEstimate(
            flops=slots * 6 * 4 * quarter * width * columns,
            bytes_accessed=slots * 4 * (3 * quarter * width + 4 * quarter * columns + 4 * width * columns),
            transcendentals=0,
        ),
        compiler_params=pltpu.CompilerParams(vmem_limit_bytes=VMEM_GRANT),
    )(bits, mask, panel_anc, upper, lower, *prev)


def from_partner(value, axis, bit):
    mask = 2**bit
    pairs = [(source, source ^ mask) for source in range(lax.axis_size(axis))]
    return lax.ppermute(value, axis, pairs)


def ancestor_solve(inverse_rows, values):
    rows_local, width = inverse_rows.shape
    if rows_local >= width:
        blocks = inverse_rows.reshape(rows_local // width, width, width)
        grouped = values.reshape(rows_local // width, width, values.shape[1])
        forward = jnp.einsum("kij,kjr->kir", blocks, grouped, precision=PRECISION)
        result = jnp.einsum("kji,kjr->kir", blocks, forward, precision=PRECISION)
        return result.reshape(rows_local, values.shape[1])
    row_index = lax.axis_index("row")
    levels = (width // rows_local).bit_length() - 1
    whole = values
    for bit_number in range(levels):
        other = from_partner(whole, "row", bit_number)
        upper = row_index >> bit_number & 1
        whole = jnp.where(
            upper == 1, jnp.concatenate([other, whole], 0), jnp.concatenate([whole, other], 0)
        )
    forward = product(inverse_rows, whole)
    partial_value = transposed(inverse_rows, forward)
    for bit_number in reversed(range(levels)):
        half = partial_value.shape[0] // 2
        upper = row_index >> bit_number & 1
        keep = jnp.where(upper == 1, partial_value[half:], partial_value[:half])
        outgoing = jnp.where(upper == 1, partial_value[:half], partial_value[half:])
        partial_value = keep + from_partner(outgoing, "row", bit_number)
    return partial_value


def solve(rhs_sub, rhs_anc, inv_sub, panel_mid, panel_anc, block_mask, inv_anc):
    rhs_local = rhs_sub[0]
    rows_local = panel_anc.shape[2]
    width = panel_anc.shape[3]
    rows_own = rhs_local.shape[1]
    columns = rhs_local.shape[2]
    block_count = block_mask.shape[2]
    row_index = lax.axis_index("row")
    core = row_index % 2
    leaf = lax.axis_index("leaf")
    x_bit, y_bit = leaf % 2, leaf // 2
    paired = lax.axis_size("leaf") == 4 and rows_local == 2 * width and len(row_digits()) == 1
    mask = block_mask[0].astype(jnp.float32)
    half = columns // 2

    def masked(slot, value):
        blocks = value.reshape(block_count, rows_local // block_count, value.shape[1])
        return (blocks * mask[slot][:, None, None]).reshape(value.shape)

    def halves(value):
        return jnp.where(core == 0, value[..., :half], value[..., half:])

    def other_half(value):
        return jnp.where(core == 0, value[..., half:], value[..., :half])

    rhs_chip = by_core(core, halves(rhs_local), core_swap(other_half(rhs_local)), 1)
    inverses = inv_sub[0]
    inverses_other = core_swap(row_major(inverses))
    middle_other = core_swap(row_major(panel_mid[0]))
    inverse_first = by_core(core, inverses[0], inverses_other[0], 0)
    inverse_second = by_core(core, inverses[1], inverses_other[1], 0)
    middle = by_core(core, panel_mid[0], middle_other, 0)

    def both_halves(value):
        return by_core(core, value, core_swap(value), 1)

    def near_and_far(value):
        swapped = core_swap(value)
        far_is_mine = core == x_bit
        return jnp.where(far_is_mine, swapped, value), jnp.where(far_is_mine, value, swapped)

    block_mask = block_mask[0]
    gathered, inverse_first = gather_rows(rhs_chip[0], lower=True, filler=inverse_first)
    first = product(inverse_first, gathered)
    first, turned = lax.optimization_barrier((first, inverses))
    turned = lax.optimization_barrier(row_major(jnp.swapaxes(turned, 1, 2)))
    first_all, (middle, inverse_second, turned) = gather_rows(
        first, filler=(middle, inverse_second, turned)
    )
    residual = rhs_chip[1] - product(middle, first_all)
    if paired:
        sides = near_and_far(first_all)
        upper = panel_forward(panel_anc, block_mask, 0, 0, y_bit, *sides)
        lower = panel_forward(panel_anc, block_mask, 0, 1, y_bit, *sides)
        gathered, upper = gather_rows(residual, lower=True, filler=upper)
        second = product(inverse_second, gathered)
        second_all, lower = gather_rows(second, filler=lower)
        sides = near_and_far(second_all)
        lower = panel_forward(panel_anc, block_mask, 1, 1, y_bit, *sides, lower)
        upper = panel_forward(panel_anc, block_mask, 1, 0, y_bit, *sides, upper)
    else:
        gathered, _ = gather_rows(residual, lower=True)
        second = product(inverse_second, gathered)
        update = masked(0, product(panel_anc[0, 0], both_halves(first_all)))
        second_all, _ = gather_rows(second)
        update = update + masked(1, product(panel_anc[0, 1], both_halves(second_all)))

    *inner_digits, (size, stride) = row_digits()
    turned, second_all = lax.optimization_barrier((turned, second_all))
    block = turned
    for inner_size, inner_stride in inner_digits:
        block = jnp.concatenate(gather_join(block, *gather_both(block, inner_size, inner_stride), inner_size, inner_stride), 2)
    received = gather_near(block, size, stride)

    def whole_inverses(received, passed):
        joined = gather_join(block, received, passed, size, stride, ordered=False)
        mine = [jnp.concatenate([part[slot] for part in joined], 1) for slot in range(2)]
        return [(value, core_swap(value)) for value in mine]

    if paired:
        inverse_anc = jnp.where(y_bit == 0, inv_anc[:width], inv_anc[width:])
        own = jnp.where(y_bit == 0, rhs_anc[:width], rhs_anc[width:])
        own = jnp.where(x_bit == 0, own[:, :half], own[:, half:])
        total, received = leaf_reduce(upper, lower, received)
        passed = gather_far(received, size, stride)
        total, inverse_anc = lax.optimization_barrier((own - total, inverse_anc))
        forward = lax.optimization_barrier(product(inverse_anc, total))
        solved = row_major(transposed(inverse_anc, forward))
        bits = jnp.stack([y_bit, x_bit == core, *block_order(size, stride)], dtype=jnp.int32)

        def begun(upper, lower):
            return panel_backward(panel_anc, block_mask, None, 0, bits, upper, lower)

        pieces, sums, wholes = leaf_gather(
            solved, passed, lambda passed: whole_inverses(received, passed), begun
        )
        x_anc = in_order(pieces, x_bit, y_bit)
    else:
        wholes = whole_inverses(received, gather_far(received, size, stride))
        total = lax.psum_scatter(update, "leaf", scatter_dimension=1, tiled=True)
        share = total.shape[1]
        own = lax.dynamic_slice_in_dim(rhs_anc, leaf * share, share, 1)
        x_anc = lax.all_gather(ancestor_solve(inv_anc, own - total), "leaf", axis=1, tiled=True)
        pieces = x_anc

    rows_chip = 2 * rows_own

    def chip_sum(slot, rhs, pieces):
        if paired:
            keep, send = panel_backward(
                panel_anc, block_mask, slot, 1, bits, pieces[1], pieces[3], (*sums, rhs)
            )
            return keep + core_swap(send)
        keep, send = (
            transposed(panel_anc[0, slot], masked(slot, part))
            for part in (halves(pieces), other_half(pieces))
        )
        value = keep + core_swap(send)
        start = row_index // 2 * rows_chip
        own = lax.dynamic_slice_in_dim(value, start, rows_chip, 0) - rhs
        value = lax.dynamic_update_slice_in_dim(value, own, start, 0)
        return jnp.concatenate(sending_order(value, size, stride), 0)

    def partial_solve(slot, value):
        cores = value.reshape(-1, 2, rows_own, half)
        first = jnp.where(core == 0, cores[:, 0], cores[:, 1]).reshape(-1, half)
        last = jnp.where(core == 0, cores[:, 1], cores[:, 0]).reshape(-1, half)
        first, last = lax.optimization_barrier((first, last))
        return product(wholes[slot][0], first) + product(wholes[slot][1], last)

    middle_columns = jnp.concatenate(
        [
            lax.dynamic_slice_in_dim(middle, k * (width // size), width // size, 1)
            for k in block_order(size, stride)
        ],
        1,
    )
    second_partial = partial_solve(1, chip_sum(1, second, pieces))
    second_partial, pieces = lax.optimization_barrier((second_partial, pieces))
    first_sum = chip_sum(0, first, pieces)
    second_total, first_sum = reduce_rows(second_partial, filler=(first_sum, middle_columns))
    first_sum, middle_columns = first_sum
    x_second = -second_total
    first_partial = partial_solve(0, first_sum + transposed(middle_columns, x_second))
    first_total, x_anc = reduce_rows(first_partial, filler=x_anc)
    x_first = -first_total

    both = jnp.stack([x_first, x_second])
    keep = jnp.where(core == 0, both[:, :rows_own], both[:, rows_own:])
    send = jnp.where(core == 0, both[:, rows_own:], both[:, :rows_own])
    x_sub = by_core(core, keep, core_swap(send), 2)
    return x_sub[None], x_anc


def solution(mesh):
    return jax.shard_map(
        solve,
        mesh=mesh,
        in_specs=(
            P("leaf", None, "row", None),
            P("row", None),
            P("leaf", None, "row", None),
            P("leaf", "row", None),
            P("leaf", None, "row", None),
            P("leaf", None, "row"),
            P("row", None),
        ),
        out_specs=(P("leaf", None, "row", None), P("row", None)),
        check_vma=False,
    )
```

```python
import functools

import jax
import jax.numpy as jnp
from jax import lax
from jax.experimental import pallas as pl
from jax.experimental.layout import Layout, with_layout_constraint
from jax.experimental.pallas import tpu as pltpu
from jax.sharding import PartitionSpec as P


PRECISION = lax.Precision.HIGH
VMEM_GRANT = 24 * 2**20


def product(left, right):
    return jnp.dot(left, right, precision=PRECISION, preferred_element_type=jnp.float32)


def transposed(left, right):
    return lax.dot_general(
        left,
        right,
        (((0,), (0,)), ((), ())),
        precision=PRECISION,
        preferred_element_type=jnp.float32,
    )


def row_major(value):
    return with_layout_constraint(value, Layout(tuple(range(value.ndim))))


def core_swap(value):
    count = lax.axis_size("row")
    return lax.ppermute(value, "row", [(r, r ^ 1) for r in range(count)])


def leaf_swap(value, mask):
    count = lax.axis_size("leaf")
    return lax.ppermute(value, "leaf", [(g, g ^ mask) for g in range(count)])


def chip_digits(chips):
    digits, stride = [], 1
    while chips > 1:
        size = 4 if chips % 4 == 0 else 2
        digits.append((size, stride))
        stride *= size
        chips //= size
    return digits


def digit_permute(value, size, stride, moves):
    target = dict(moves)
    pairs = []
    for r in range(lax.axis_size("row")):
        digit = (r // 2) // stride % size
        if digit in target:
            pairs.append((r, r + 2 * stride * (target[digit] - digit)))
    return lax.ppermute(value, "row", pairs)


def digit_index(size, stride):
    return lax.axis_index("row") // 2 // stride % size


def after(values, filler):
    return lax.optimization_barrier((*values, filler))


def gather_near(value, size, stride, lower=False):
    def moves(pairs):
        return [(a, b) for a, b in pairs if a < b] if lower else pairs

    if size == 2:
        return (digit_permute(value, size, stride, moves([(0, 1), (1, 0)])),)
    near = digit_permute(value, size, stride, moves([(0, 1), (1, 0), (2, 3), (3, 2)]))
    inner = digit_permute(value, size, stride, moves([(1, 2), (2, 1)]))
    return near, inner


def gather_far(received, size, stride, lower=False):
    def moves(pairs):
        return [(a, b) for a, b in pairs if a < b] if lower else pairs

    if size == 2:
        return ()
    near, inner = received
    relay = digit_permute(near, size, stride, moves([(1, 2), (2, 1)]))
    far = digit_permute(near, size, stride, moves([(1, 3), (2, 0)]))
    outer = digit_permute(inner, size, stride, moves([(1, 0), (2, 3)]))
    return relay, far, outer


def gather_join(value, received, passed, size, stride, ordered=True):
    me = digit_index(size, stride)
    if size == 2:
        (near,) = received
        if not ordered:
            return [near, value]
        return [jnp.where(me == 0, value, near), jnp.where(me == 0, near, value)]
    near, inner = received
    relay, far, outer = passed
    middle = (me == 1) | (me == 2)
    third = jnp.where(middle, inner, outer)
    fourth = jnp.where(middle, relay, far)
    odd = me % 2 == 1
    if not ordered:
        return [fourth, third, near, value]
    even_one = jnp.where(odd, near, value)
    odd_one = jnp.where(odd, value, near)
    high = me >= 2
    return [
        jnp.where(high, fourth, even_one),
        jnp.where(high, third, odd_one),
        jnp.where(high, even_one, third),
        jnp.where(high, odd_one, fourth),
    ]


def gather_both(value, size, stride):
    received = gather_near(value, size, stride)
    return received, gather_far(received, size, stride)


def gather_digit(value, size, stride, lower, filler):
    received = gather_near(value, size, stride, lower)
    passed = gather_far(received, size, stride, lower)
    last, filler = after((passed or received,), filler)
    received, passed = (received, last) if passed else (last, passed)
    return jnp.concatenate(gather_join(value, received, passed, size, stride), 0), filler


def block_order(size, stride):
    me = digit_index(size, stride)
    if size == 2:
        return 1 - me, me
    high = me >= 2
    return jnp.where(high, 0, 3), jnp.where(high, 1, 2), me ^ 1, me


def sending_order(value, size, stride):
    rows = value.shape[0] // size
    return [
        lax.dynamic_slice_in_dim(value, k * rows, rows, 0) for k in block_order(size, stride)
    ]


def reduce_digit(value, size, stride, lower, filler):
    def moves(pairs):
        return [(a, b) for a, b in pairs if a > b] if lower else pairs

    block = sending_order(value, size, stride)
    if size == 2:
        other = digit_permute(block[0], size, stride, moves([(0, 1), (1, 0)]))
        other, filler = after((other,), filler)
        return block[1] + other, filler
    far = digit_permute(block[0], size, stride, moves([(3, 1), (0, 2)]))
    relay = digit_permute(block[0], size, stride, moves([(2, 1), (1, 2)]))
    outer = digit_permute(block[1], size, stride, moves([(0, 1), (3, 2)]))
    far, relay, outer = lax.optimization_barrier((far, relay, outer))
    inner = digit_permute(block[1] + outer, size, stride, moves([(1, 2), (2, 1)]))
    near = digit_permute(block[2] + (far + relay), size, stride, moves([(0, 1), (1, 0), (2, 3), (3, 2)]))
    near, inner, filler = after((near, inner), filler)
    return block[3] + near + inner, filler


def gather_rows(value, lower=False, filler=()):
    digits = chip_digits(lax.axis_size("row") // 2)
    for place, (size, stride) in enumerate(digits):
        outermost = place == len(digits) - 1
        value, filler = gather_digit(value, size, stride, lower and outermost, filler)
    return value, filler


def row_digits():
    return chip_digits(lax.axis_size("row") // 2)


def reduce_rows(value, lower=False, filler=()):
    digits = row_digits()
    for place, (size, stride) in reversed(list(enumerate(digits))):
        outermost = place == len(digits) - 1
        value, filler = reduce_digit(value, size, stride, lower and outermost, filler)
    return value, filler


def by_core(core, mine, other, axis):
    return jnp.concatenate(
        [jnp.where(core == 0, mine, other), jnp.where(core == 0, other, mine)], axis
    )


def leaf_reduce(upper, lower, side):
    from_x = leaf_swap(upper[0], 1)
    from_y = leaf_swap(lower[0], 2)
    lower_kept, side = after((lower[1],), side)
    lower = (lower[0], lower_kept)
    from_x, from_y = lax.optimization_barrier((from_x, from_y))
    first, second = upper[1][0] + from_x[0], lower[1][0] + from_y[0]
    first, second = leaf_swap(first, 2), leaf_swap(second, 1)
    first, second = lax.optimization_barrier((first, second))
    return jnp.concatenate(
        [upper[1][1] + from_x[1] + first, lower[1][1] + from_y[1] + second], 0
    ), side


def leaf_gather(piece, side, finish, between):
    rows = piece.shape[0]
    first, second = piece[: rows // 2], piece[rows // 2 :]
    first_y = leaf_swap(first, 2)
    second_x = leaf_swap(second, 1)
    wholes = finish(side)
    first_y, second_x = lax.optimization_barrier((first_y, second_x))
    upper = jnp.stack([first, first_y])
    lower = jnp.stack([second, second_x])
    upper_far = leaf_swap(upper, 1)
    lower_far = leaf_swap(lower, 2)
    sums = between(upper, lower)
    upper_far, lower_far, sums, wholes = lax.optimization_barrier(
        (upper_far, lower_far, sums, wholes)
    )
    return (upper, upper_far, lower, lower_far), sums, wholes


def in_order(pieces, x_bit, y_bit):
    upper, upper_far, lower, lower_far = pieces

    def at(block, column):
        own_block, own_column = y_bit == block, x_bit == column
        return [
            jnp.where(
                own_column,
                jnp.where(own_block, upper[0], upper[1]),
                jnp.where(own_block, upper_far[0], upper_far[1]),
            ),
            jnp.where(
                own_block,
                jnp.where(own_column, lower[0], lower[1]),
                jnp.where(own_column, lower_far[0], lower_far[1]),
            ),
        ]

    return jnp.concatenate(
        [jnp.concatenate(at(0, column) + at(1, column), 0) for column in range(2)], 1
    )


def split(value):
    high = value.astype(jnp.bfloat16)
    return high, (value - high.astype(jnp.float32)).astype(jnp.bfloat16)


def scale_rows(value, mask_ref, slot, first_block, count):
    rows = value.shape[0] // count
    return jnp.concatenate(
        [
            value[k * rows : (k + 1) * rows] * mask_ref[slot, first_block + k].astype(jnp.float32)
            for k in range(count)
        ],
        0,
    )


def forward_kernel(slot, place, tiles, mask_blocks, bit_ref, mask_ref, panel_ref, near_ref, far_ref, *refs):
    prev, (out_first, out_last, high, low) = refs[:-4], refs[-4:]
    turn, step = pl.program_id(0), pl.program_id(1)
    columns = near_ref.shape[1]

    @pl.when((turn == 0) & (step == 0))
    def _():
        for k, ref in enumerate((near_ref, far_ref)):
            part = split(ref[...])
            high[:, k * columns : (k + 1) * columns] = part[0]
            low[:, k * columns : (k + 1) * columns] = part[1]

    panel_high, panel_low = split(panel_ref[...])

    def dot(left, right):
        return jnp.dot(left, right, preferred_element_type=jnp.float32)

    result = dot(panel_high, high[...]) + (dot(panel_high, low[...]) + dot(panel_low, high[...]))
    block = jnp.where(turn == 0, 1 - bit_ref[0], bit_ref[0])
    tile = (2 * block + place) * tiles + step
    result = scale_rows(result, mask_ref, slot, tile * mask_blocks, mask_blocks)
    here = pl.ds(pl.multiple_of(step * panel_ref.shape[0], panel_ref.shape[0]), panel_ref.shape[0])
    parts = result[:, :columns], result[:, columns:]

    def put(ref, index, value, old):
        ref[index, here] = value + old[index, here] if old is not None else value

    first_old, last_old = prev or (None, None)
    if place == 0:
        put(out_first, turn, parts[0], first_old)
        put(out_last, turn, parts[1], last_old)
    else:

        @pl.when(turn == 0)
        def _():
            for k in range(2):
                put(out_first, k, parts[k], first_old)

        @pl.when(turn == 1)
        def _():
            for k in range(2):
                put(out_last, k, parts[k], last_old)


def panel_forward(panel_anc, mask, slot, place, y_bit, near, far, prev=(), tile_rows=256):
    rows_local, width = panel_anc.shape[2:]
    quarter = rows_local // 4
    tiles = quarter // tile_rows
    columns = near.shape[1]
    mask_blocks = mask.shape[1] // (4 * tiles)

    def panel_index(turn, step, bit_ref, mask_ref):
        block = jnp.where(turn == 0, 1 - bit_ref[0], bit_ref[0])
        return (0, slot, (2 * block + place) * tiles + step, 0)

    whole = pl.BlockSpec(memory_space=pltpu.VMEM)
    shape = jax.ShapeDtypeStruct((2, quarter, columns), jnp.float32)
    return pl.pallas_call(
        functools.partial(forward_kernel, slot, place, tiles, mask_blocks),
        out_shape=[shape, shape],
        grid_spec=pltpu.PrefetchScalarGridSpec(
            num_scalar_prefetch=2,
            grid=(2, tiles),
            in_specs=[
                pl.BlockSpec((None, None, tile_rows, width), panel_index),
                *[whole] * (2 + len(prev)),
            ],
            out_specs=[whole, whole],
            scratch_shapes=[pltpu.VMEM((width, 2 * columns), jnp.bfloat16)] * 2,
        ),
        cost_estimate=pl.CostEstimate(
            flops=12 * quarter * width * 2 * columns,
            bytes_accessed=4 * (2 * quarter * width + 2 * width * columns + 4 * quarter * columns),
            transcendentals=0,
        ),
        compiler_params=pltpu.CompilerParams(vmem_limit_bytes=VMEM_GRANT),
    )(y_bit.reshape(1).astype(jnp.int32), mask, panel_anc, near, far, *prev)


def backward_kernel(slot, side, mask_blocks, bit_ref, mask_ref, panel_ref, upper_ref, lower_ref, *refs):
    prev, (out_first, out_last, panel_parts, value_parts, total) = refs[:-5], refs[-5:]
    if prev:
        *prev, rhs_ref = prev
    phase, step = pl.program_id(0), pl.program_id(1)
    rows = panel_ref.shape[0]
    columns = upper_ref.shape[2]
    tile = backward_quarter(side, phase, bit_ref) * pl.num_programs(1) + step

    def put(index, value):
        value = scale_rows(value, mask_ref, slot, tile * mask_blocks, mask_blocks)
        high, low = split(value)
        span = slice(index * columns, (index + 1) * columns)
        value_parts[0:rows, span] = high
        value_parts[rows : 2 * rows, span] = high
        value_parts[2 * rows : 3 * rows, span] = low

    high, low = split(panel_ref[...])
    panel_parts[0:rows] = high
    panel_parts[rows : 2 * rows] = low
    panel_parts[2 * rows : 3 * rows] = high

    def dot(right):
        return lax.dot_general(
            panel_parts[...], right, (((0,), (0,)), ((), ())), preferred_element_type=jnp.float32
        )

    near, far = slice(0, columns), slice(columns, 2 * columns)
    here = near if side == 0 else far

    @pl.when((phase == 0) & (step == 0))
    def _():
        if prev:
            total[:, near] = prev[0][...]
            total[:, far] = prev[1][...]
        else:
            total[...] = jnp.zeros_like(total)

    here_rows = pl.ds(pl.multiple_of(step * rows, rows), rows)

    @pl.when(phase < 2)
    def _():
        put(0, upper_ref[phase, here_rows])
        total[:, here] += dot(value_parts[:, near])

    @pl.when(phase == 2)
    def _():
        put(0, lower_ref[0, here_rows])
        put(1, lower_ref[1, here_rows])
        total[...] += dot(value_parts[...])

    @pl.when((phase == 2) & (step == pl.num_programs(1) - 1))
    def _():
        if side == 0:
            out_first[...] = total[:, near]
            out_last[...] = total[:, far]
        else:
            length = rhs_ref.shape[0]
            count = total.shape[0] // length

            def put_out(kept, sent):
                for k in range(count):
                    source = pl.ds(pl.multiple_of(bit_ref[2 + k] * length, length), length)
                    place = slice(k * length, (k + 1) * length)
                    value = total[source, kept]
                    out_first[place] = value - rhs_ref[...] if k == count - 1 else value
                    out_last[place] = total[source, sent]

            pl.when(bit_ref[1] == 1)(functools.partial(put_out, near, far))
            pl.when(bit_ref[1] == 0)(functools.partial(put_out, far, near))


def backward_quarter(side, phase, bit_ref):
    own, other = bit_ref[0], 1 - bit_ref[0]
    lower = 2 * (own if side == 0 else other) + 1
    return jnp.where(phase == 0, 2 * own, jnp.where(phase == 1, 2 * other, lower))


def panel_backward(panel_anc, mask, slot, side, bits, upper, lower, prev=(), tile_rows=256):
    rows_local, width = panel_anc.shape[2:]
    quarter = rows_local // 4
    columns = upper.shape[2]
    tiles = quarter // tile_rows
    mask_blocks = mask.shape[1] // (4 * tiles)

    def panel_index(phase, step, bit_ref, mask_ref):
        return (0, slot, backward_quarter(side, phase, bit_ref) * tiles + step, 0)


    whole = pl.BlockSpec(memory_space=pltpu.VMEM)
    shape = jax.ShapeDtypeStruct((width, columns), jnp.float32)
    return pl.pallas_call(
        functools.partial(backward_kernel, slot, side, mask_blocks),
        out_shape=[shape, shape],
        grid_spec=pltpu.PrefetchScalarGridSpec(
            num_scalar_prefetch=2,
            grid=(3, tiles),
            in_specs=[
                pl.BlockSpec((None, None, tile_rows, width), panel_index),
                *[whole] * (2 + len(prev)),
            ],
            out_specs=[whole, whole],
            scratch_shapes=[
                pltpu.VMEM((3 * tile_rows, width), jnp.bfloat16),
                pltpu.VMEM((3 * tile_rows, 2 * columns), jnp.bfloat16),
                pltpu.VMEM((width, 2 * columns), jnp.float32),
            ],
        ),
        cost_estimate=pl.CostEstimate(
            flops=6 * 4 * quarter * width * columns,
            bytes_accessed=4 * (3 * quarter * width + 4 * quarter * columns + 4 * width * columns),
            transcendentals=0,
        ),
        compiler_params=pltpu.CompilerParams(vmem_limit_bytes=VMEM_GRANT),
    )(bits, mask, panel_anc, upper, lower, *prev)


def from_partner(value, axis, bit):
    mask = 2**bit
    pairs = [(source, source ^ mask) for source in range(lax.axis_size(axis))]
    return lax.ppermute(value, axis, pairs)


def ancestor_solve(inverse_rows, values):
    rows_local, width = inverse_rows.shape
    if rows_local >= width:
        blocks = inverse_rows.reshape(rows_local // width, width, width)
        grouped = values.reshape(rows_local // width, width, values.shape[1])
        forward = jnp.einsum("kij,kjr->kir", blocks, grouped, precision=PRECISION)
        result = jnp.einsum("kji,kjr->kir", blocks, forward, precision=PRECISION)
        return result.reshape(rows_local, values.shape[1])
    row_index = lax.axis_index("row")
    levels = (width // rows_local).bit_length() - 1
    whole = values
    for bit_number in range(levels):
        other = from_partner(whole, "row", bit_number)
        upper = row_index >> bit_number & 1
        whole = jnp.where(
            upper == 1, jnp.concatenate([other, whole], 0), jnp.concatenate([whole, other], 0)
        )
    forward = product(inverse_rows, whole)
    partial_value = transposed(inverse_rows, forward)
    for bit_number in reversed(range(levels)):
        half = partial_value.shape[0] // 2
        upper = row_index >> bit_number & 1
        keep = jnp.where(upper == 1, partial_value[half:], partial_value[:half])
        outgoing = jnp.where(upper == 1, partial_value[:half], partial_value[half:])
        partial_value = keep + from_partner(outgoing, "row", bit_number)
    return partial_value


def solve(rhs_sub, rhs_anc, inv_sub, panel_mid, panel_anc, block_mask, inv_anc):
    rhs_local = rhs_sub[0]
    rows_local = panel_anc.shape[2]
    width = panel_anc.shape[3]
    rows_own = rhs_local.shape[1]
    columns = rhs_local.shape[2]
    block_count = block_mask.shape[2]
    row_index = lax.axis_index("row")
    core = row_index % 2
    leaf = lax.axis_index("leaf")
    x_bit, y_bit = leaf % 2, leaf // 2
    paired = lax.axis_size("leaf") == 4 and rows_local == 2 * width and len(row_digits()) == 1
    mask = block_mask[0].astype(jnp.float32)
    half = columns // 2

    def masked(slot, value):
        blocks = value.reshape(block_count, rows_local // block_count, value.shape[1])
        return (blocks * mask[slot][:, None, None]).reshape(value.shape)

    def halves(value):
        return jnp.where(core == 0, value[..., :half], value[..., half:])

    def other_half(value):
        return jnp.where(core == 0, value[..., half:], value[..., :half])

    rhs_chip = by_core(core, halves(rhs_local), core_swap(other_half(rhs_local)), 1)
    inverses = inv_sub[0]
    inverses_other = core_swap(row_major(inverses))
    middle_other = core_swap(row_major(panel_mid[0]))
    inverse_first = by_core(core, inverses[0], inverses_other[0], 0)
    inverse_second = by_core(core, inverses[1], inverses_other[1], 0)
    middle = by_core(core, panel_mid[0], middle_other, 0)

    def both_halves(value):
        return by_core(core, value, core_swap(value), 1)

    def near_and_far(value):
        swapped = core_swap(value)
        far_is_mine = core == x_bit
        return jnp.where(far_is_mine, swapped, value), jnp.where(far_is_mine, value, swapped)

    block_mask = block_mask[0]
    gathered, inverse_first = gather_rows(rhs_chip[0], lower=True, filler=inverse_first)
    first = product(inverse_first, gathered)
    first, turned = lax.optimization_barrier((first, inverses))
    turned = lax.optimization_barrier(row_major(jnp.swapaxes(turned, 1, 2)))
    size, stride = row_digits()[-1]
    middle_columns = jnp.concatenate(
        [
            lax.dynamic_slice_in_dim(middle, k * (width // size), width // size, 1)
            for k in block_order(size, stride)
        ],
        1,
    )
    first_all, (middle, inverse_second, turned, middle_columns) = gather_rows(
        first, filler=(middle, inverse_second, turned, middle_columns)
    )
    residual = rhs_chip[1] - product(middle, first_all)
    if paired:
        sides = near_and_far(first_all)
        upper = panel_forward(panel_anc, block_mask, 0, 0, y_bit, *sides)
        lower = panel_forward(panel_anc, block_mask, 0, 1, y_bit, *sides)
        gathered, upper = gather_rows(residual, lower=True, filler=upper)
        second = product(inverse_second, gathered)
        second_all, lower = gather_rows(second, filler=lower)
        sides = near_and_far(second_all)
        lower = panel_forward(panel_anc, block_mask, 1, 1, y_bit, *sides, lower)
        upper = panel_forward(panel_anc, block_mask, 1, 0, y_bit, *sides, upper)
    else:
        gathered, _ = gather_rows(residual, lower=True)
        second = product(inverse_second, gathered)
        update = masked(0, product(panel_anc[0, 0], both_halves(first_all)))
        second_all, _ = gather_rows(second)
        update = update + masked(1, product(panel_anc[0, 1], both_halves(second_all)))

    *inner_digits, (size, stride) = row_digits()
    turned, second_all = lax.optimization_barrier((turned, second_all))
    block = turned
    for inner_size, inner_stride in inner_digits:
        block = jnp.concatenate(gather_join(block, *gather_both(block, inner_size, inner_stride), inner_size, inner_stride), 2)
    received = gather_near(block, size, stride)

    def whole_inverses(received, passed):
        joined = gather_join(block, received, passed, size, stride, ordered=False)
        mine = [jnp.concatenate([part[slot] for part in joined], 1) for slot in range(2)]
        return [(value, core_swap(value)) for value in mine]

    if paired:
        inverse_anc = jnp.where(y_bit == 0, inv_anc[:width], inv_anc[width:])
        own = jnp.where(y_bit == 0, rhs_anc[:width], rhs_anc[width:])
        own = jnp.where(x_bit == 0, own[:, :half], own[:, half:])
        total, received = leaf_reduce(upper, lower, received)
        passed = gather_far(received, size, stride)
        total, inverse_anc = lax.optimization_barrier((own - total, inverse_anc))
        forward = lax.optimization_barrier(product(inverse_anc, total))
        solved = row_major(transposed(inverse_anc, forward))
        bits = jnp.stack([y_bit, x_bit == core, *block_order(size, stride)], dtype=jnp.int32)

        def begun(upper, lower):
            return panel_backward(panel_anc, block_mask, 1, 0, bits, upper, lower)

        pieces, sums, wholes = leaf_gather(
            solved, passed, lambda passed: whole_inverses(received, passed), begun
        )
        x_anc = in_order(pieces, x_bit, y_bit)
    else:
        wholes = whole_inverses(received, gather_far(received, size, stride))
        total = lax.psum_scatter(update, "leaf", scatter_dimension=1, tiled=True)
        share = total.shape[1]
        own = lax.dynamic_slice_in_dim(rhs_anc, leaf * share, share, 1)
        x_anc = lax.all_gather(ancestor_solve(inv_anc, own - total), "leaf", axis=1, tiled=True)
        pieces = x_anc

    rows_chip = 2 * rows_own

    def chip_sum(slot, rhs, pieces):
        if paired:
            begun = sums
            if slot == 0:
                begun = panel_backward(
                    panel_anc, block_mask, 0, 0, bits, pieces[0], pieces[2]
                )
            keep, send = panel_backward(
                panel_anc, block_mask, slot, 1, bits, pieces[1], pieces[3], (*begun, rhs)
            )
            return keep + core_swap(send)
        keep, send = (
            transposed(panel_anc[0, slot], masked(slot, part))
            for part in (halves(pieces), other_half(pieces))
        )
        value = keep + core_swap(send)
        start = row_index // 2 * rows_chip
        own = lax.dynamic_slice_in_dim(value, start, rows_chip, 0) - rhs
        value = lax.dynamic_update_slice_in_dim(value, own, start, 0)
        return jnp.concatenate(sending_order(value, size, stride), 0)

    def partial_solve(slot, value):
        cores = value.reshape(-1, 2, rows_own, half)
        first = jnp.where(core == 0, cores[:, 0], cores[:, 1]).reshape(-1, half)
        last = jnp.where(core == 0, cores[:, 1], cores[:, 0]).reshape(-1, half)
        first, last = lax.optimization_barrier((first, last))
        return product(wholes[slot][0], first) + product(wholes[slot][1], last)

    second_partial = partial_solve(1, chip_sum(1, second, pieces))
    second_partial, pieces = lax.optimization_barrier((second_partial, pieces))
    first_sum = chip_sum(0, first, pieces)
    second_total, first_sum = reduce_rows(second_partial, filler=first_sum)
    x_second = -second_total
    first_partial = partial_solve(0, first_sum + transposed(middle_columns, x_second))
    first_total, x_anc = reduce_rows(first_partial, filler=x_anc)
    x_first = -first_total

    both = jnp.stack([x_first, x_second])
    keep = jnp.where(core == 0, both[:, :rows_own], both[:, rows_own:])
    send = jnp.where(core == 0, both[:, rows_own:], both[:, :rows_own])
    x_sub = by_core(core, keep, core_swap(send), 2)
    return x_sub[None], x_anc


def solution(mesh):
    return jax.shard_map(
        solve,
        mesh=mesh,
        in_specs=(
            P("leaf", None, "row", None),
            P("row", None),
            P("leaf", None, "row", None),
            P("leaf", "row", None),
            P("leaf", None, "row", None),
            P("leaf", None, "row"),
            P("row", None),
        ),
        out_specs=(P("leaf", None, "row", None), P("row", None)),
        check_vma=False,
    )
```
